128 devices in a mesh: strip: 8 (over y, core), depth: 16 (over z, x).
Axes of the slice: x: 4, y: 4, z: 4, core: 2. Of those that a mesh axis runs over, the one named last changes fastest.
Arguments:
- warmth_before: float32 [512, 512, 1024], P('depth', 'strip'), may hold values from -6 to 6
- stratum_category: int32 [512, 512, 1024], P('depth', 'strip'), may hold values from 0 to 7
- conductance_catalogue: float32 [8], replicated, may hold values from 0.3 to 3
- pivot_matrix_reciprocal: float32 [512, 32], P('depth'), may hold values from 0 to 1, as said below
- linkage_factor: float32 [16], P('depth'), may hold values from 0 to 1, as said below
- well_position_inside: int32 [1024], P('strip'), may hold values from 0 to 65535, as said below
- well_holder_sequence: int32 [1024], P('strip'), may hold values from 0 to 127, as said below
- well_reach: int32 [1024], P('strip'), may hold values from 128 to 512
- entering_warmth: float32 [1024], P('strip'), may hold values from -4 to 4
- well_transfer_speed: float32 [1024], P('strip'), may hold values from 0.0005 to 0.03
Outputs:
- new_temperature: float32 [512, 512, 1024], P('depth', 'strip')
- leaving_warmth: float32 [1024], P(('strip', 'depth'))
The draws below stay inside these ranges and needn't reach their ends.
Inputs may be any that keep to these rules, and one draw needn't show every extreme that they name: `well_position_inside`: within each strip's block of 128 entries the positions are distinct; a position counts y * 1024 + x over the strip's 64 x 1024 cells. `well_holder_sequence`: each strip's block of 128 entries is a permutation of 0 to 127. `pivot_matrix_reciprocal`: entries are positive. `linkage_factor`: entries are positive and below 1.
All inputs are finite; a program needn't handle non-finite values.
Results may differ from the reference program's by a relative error of at most 0.0003.
Values sent between devices are 32-bit elements; how exact they have to be, the bound alone decides.
A program may use at most 192 MiB of HBM per device.

```python
import math
import jax
import jax.numpy as jnp
from jax import lax

CZ = 32
CY = 64
SPAN_EAST = 1024
NBS = 128
NL = 8
VERTICAL_SLABS = 512
SPAN_NORTH = 512
WELL_COUNT = 1024


def draw_pivot_matrix_reciprocal(key, part):
    blocks = VERTICAL_SLABS // CZ
    scales = jax.random.uniform(key, (blocks, CZ), jnp.float32, 0.6, 1.6)
    row_index = jnp.arange(CZ, dtype=jnp.int32)[:, None]
    column_index = jnp.arange(CZ, dtype=jnp.int32)[None, :]
    lesser = jnp.minimum(row_index, column_index) + 1
    greater = jnp.maximum(row_index, column_index)
    norm_factor = float(CZ + 1) * 2.0 * float(CZ) * math.sqrt(float(CZ))
    kernel = (lesser * (CZ - greater)).astype(jnp.float32) / norm_factor
    full = scales[:, :, None] * scales[:, None, :] * kernel[None, :, :]
    return full.reshape(VERTICAL_SLABS, CZ)


def draw_linkage_factor(key, part):
    blocks = VERTICAL_SLABS // CZ
    low_gap = math.log(1.0 / (24.0 * CZ))
    high_gap = math.log(1.0 / (6.0 * CZ))
    gap = jnp.exp(jax.random.uniform(key, (blocks,), jnp.float32, low_gap, high_gap))
    return 1.0 - gap


def draw_well_position_inside(key, part):
    strips = WELL_COUNT // NBS

    def one_strip(strip_index):
        shuffled = jax.random.permutation(jax.random.fold_in(key, strip_index), CY * SPAN_EAST - 2)[:NBS - 2] + 1
        return jnp.concatenate([jnp.array([0, CY * SPAN_EAST - 1], jnp.int32), shuffled.astype(jnp.int32)])
    return jax.vmap(one_strip)(jnp.arange(strips, dtype=jnp.int32)).reshape(WELL_COUNT)


def draw_well_holder_sequence(key, part):
    strips = WELL_COUNT // NBS

    def one_strip(strip_index):
        return jax.random.permutation(jax.random.fold_in(key, strip_index + 7919), NBS).astype(jnp.int32)
    return jax.vmap(one_strip)(jnp.arange(strips, dtype=jnp.int32)).reshape(WELL_COUNT)


def draw_well_reach(key, part):
    drawn = jax.random.randint(key, (WELL_COUNT,), VERTICAL_SLABS // 4, VERTICAL_SLABS + 1, jnp.int32)
    drawn = drawn.at[0::NBS].set(VERTICAL_SLABS)
    return drawn.at[1::NBS].set(VERTICAL_SLABS // 4)


def with_ends(values, own_key, least, top_value):
    index_at = [jax.random.randint(jax.random.fold_in(own_key, axis), (), 0, length) for axis, length in enumerate(values.shape)]
    longest = values.shape.index(max(values.shape))
    neighbour = index_at[:longest] + [(index_at[longest] + 1) % values.shape[longest]] + index_at[longest + 1:]
    return values.at[tuple(index_at)].set(least).at[tuple(neighbour)].set(top_value)


def level_of(rng, dims, pieces, least, top_value):
    loudness, own = 1.0, jax.random.fold_in(rng, 6)
    for dim, blocks in pieces:
        draws = jnp.exp(jax.random.uniform(jax.random.fold_in(own, dim), (blocks,), jnp.float32, least / len(pieces), top_value / len(pieces)))
        loudness = loudness * jnp.repeat(draws, dims[dim] // blocks).reshape([-1 if axis == dim else 1 for axis in range(len(dims))])
    return loudness


def noise(own_key, shape, width, reach, cuts=(), kind=jnp.bfloat16):
    values = jax.random.normal(own_key, shape, jnp.float32) * width
    if len(cuts) > 0:
        values = level_of(own_key, shape, cuts, -0.22, 0.18) * values
    return jnp.clip(values, min=-reach, max=reach).astype(kind)


def setup_inputs(seed: int = 0) -> dict:
    keys = jax.random.split(jax.random.key(seed), 11)
    return {
        "warmth_before": noise(keys[0], (VERTICAL_SLABS, SPAN_NORTH, SPAN_EAST), 1.0, 6.0, ((0, 16), (1, 8)), jnp.float32),
        "stratum_category": with_ends(jax.random.randint(keys[1], (VERTICAL_SLABS, SPAN_NORTH, SPAN_EAST), 0, NL), jax.random.fold_in(keys[1], 1), 0, NL - 1).astype(jnp.int32),
        "conductance_catalogue": jnp.clip(jnp.exp(jax.random.uniform(keys[2], (NL,), jnp.float32, math.log(0.3), math.log(3.0))), 0.3, 3.0),
        "pivot_matrix_reciprocal": draw_pivot_matrix_reciprocal(jax.random.fold_in(keys[10], 71), 0),
        "linkage_factor": draw_linkage_factor(jax.random.fold_in(keys[10], 71), 0),
        "well_position_inside": draw_well_position_inside(jax.random.fold_in(keys[10], 71), 0),
        "well_holder_sequence": draw_well_holder_sequence(jax.random.fold_in(keys[10], 71), 0),
        "well_reach": draw_well_reach(jax.random.fold_in(keys[10], 71), 0),
        "entering_warmth": noise(keys[8], (WELL_COUNT,), 1.0, 4.0, ((0, 8),), jnp.float32),
        "well_transfer_speed": jnp.clip(jnp.exp(math.log(0.03) - 4.0943445 * jax.random.uniform(keys[9], (WELL_COUNT,), jnp.float32) ** level_of(keys[9], (WELL_COUNT,), ((0, 8),), -0.2, 0.2)), 0.0005, 0.03),
    }


backward_euler_advance = 0.2
storage_volume = 2.0

def lookup(stratum_category, conductance_catalogue):
    running = jnp.zeros(stratum_category.shape, jnp.float32)
    for level_index in range(conductance_catalogue.shape[0]):
        running = running + jnp.where(stratum_category == level_index, conductance_catalogue[level_index], jnp.zeros((), jnp.float32))
    return running

def overall_thermal_current(framed_warmth, framed_conductance):
    middle_value = framed_warmth[:, 1:-1, 1:-1]
    cond_centre = framed_conductance[:, 1:-1, 1:-1]
    vertical_extent = middle_value.shape[1]
    lateral_count = middle_value.shape[2]
    running = jnp.zeros_like(middle_value)
    for offset_north, offset_east in ((0, 1), (2, 1), (1, 0), (1, 2)):
        adjacent_value = framed_warmth[:, offset_north:offset_north + vertical_extent, offset_east:offset_east + lateral_count]
        cond_neighbour = framed_conductance[:, offset_north:offset_north + vertical_extent, offset_east:offset_east + lateral_count]
        running = running + 0.5 * (cond_centre + cond_neighbour) * (adjacent_value - middle_value)
    return running

def affine_pair(earlier, later):
    return (later[0] * earlier[0], later[0] * earlier[1] + later[1])

def liquid_circuit(stratum_lines, conductance_lines, inlets, rates, lengths):
    overall_slabs = stratum_lines.shape[1]
    levels = jnp.arange(overall_slabs, dtype=jnp.int32)[None, :]
    active = (levels < lengths[:, None]).astype(jnp.float32)
    exchange_rate = rates[:, None] * conductance_lines / (1.0 + conductance_lines) * active
    keeping = 1.0 - exchange_rate
    forcing = exchange_rate * stratum_lines
    down_coef, down_add = lax.associative_scan(affine_pair, (keeping, forcing), axis=1)
    down_after = down_coef * inlets[:, None] + down_add
    bottom = down_after[:, -1]
    down_before = jnp.concatenate([inlets[:, None], down_after[:, :-1]], axis=1)
    rise_coef, rise_add = lax.associative_scan(affine_pair, (keeping, forcing), reverse=True, axis=1)
    rise_at = rise_coef * bottom[:, None] + rise_add
    rise_below = jnp.concatenate([rise_at[:, 1:], bottom[:, None]], axis=1)
    withdrawal = exchange_rate * (2.0 * stratum_lines - down_before - rise_below)
    return (withdrawal, rise_at[:, 0])

def reduced_scalars(corners, block_size):
    corner_first = corners[:, 0]
    corner_upper = corners[:, 1]
    corner_lower = corners[:, 2]
    corner_last = corners[:, 3]
    coupling_ratio = corners[:, 4]
    blocks = corners.shape[0]
    previous_last = jnp.concatenate([jnp.ones((1,), jnp.float32), corner_last[:-1]])
    has_upper = (jnp.arange(blocks) >= 1).astype(jnp.float32)
    couple_now = has_upper * coupling_ratio * (block_size / (block_size + 1.0)) / jnp.sqrt(previous_last * corner_first)
    couple_next = jnp.concatenate([couple_now[1:], jnp.zeros((1,), jnp.float32)])
    down_first = couple_now * corner_first
    down_last = couple_now * corner_lower
    rise_first = couple_next * corner_upper
    rise_last = couple_next * corner_last

    def advance(ratio_prev, entries):
        spike_first, spike_last, next_first, next_last = entries
        pivot_value = 1.0 - spike_first * ratio_prev
        ratio_here = next_last + spike_last * ratio_prev * next_first / pivot_value
        return (ratio_here, (ratio_prev, pivot_value))
    final_ratio, (ratio_before, pivots) = lax.scan(advance, jnp.zeros((), jnp.float32), (down_first, down_last, rise_first, rise_last))
    return (couple_now, couple_next, down_first, down_last, rise_first, ratio_before, pivots)

def sweep_all(scalars, firsts, lasts):
    couple_now, couple_next, down_first, down_last, rise_first, ratio_before, pivots = scalars

    def forward(carry_prefix, entries):
        spike_first, spike_last, ratio_prev, pivot_value, value_first, value_last = entries
        prefix_here = value_last + spike_last * ratio_prev * value_first / pivot_value + spike_last / pivot_value * carry_prefix
        return (prefix_here, carry_prefix)
    final_prefix, prefix_before = lax.scan(forward, jnp.zeros_like(firsts[0]), (down_first, down_last, ratio_before, pivots, firsts, lasts))
    alpha_part = (firsts + down_first[:, None] * prefix_before) / pivots[:, None]
    beta_part = rise_first / pivots

    def backward(carry_first, entries):
        alpha_row, beta_value = entries
        first_here = alpha_row + beta_value * carry_first
        return (first_here, (first_here, carry_first))
    final_first, (first_here, first_next) = lax.scan(backward, jnp.zeros_like(firsts[0]), (alpha_part, beta_part), reverse=True)
    return (prefix_before, first_here, first_next)

def reference(warmth_before, stratum_category, conductance_catalogue, pivot_matrix_reciprocal, linkage_factor, well_position_inside, well_holder_sequence, well_reach, entering_warmth, well_transfer_speed):
    overall_slabs, overall_lines, span_eastward = warmth_before.shape
    overall_tubes = overall_lines * span_eastward
    conduct = lookup(stratum_category, conductance_catalogue)
    framed_warmth = jnp.pad(warmth_before, ((0, 0), (1, 1), (1, 1)))
    framed_conductance = jnp.pad(conduct, ((0, 0), (1, 1), (1, 1)))
    warmed_state = warmth_before + backward_euler_advance * overall_thermal_current(framed_warmth, framed_conductance)
    strip_base = jnp.arange(well_position_inside.shape[0], dtype=jnp.int32) // NBS * NBS
    sorted_values = strip_base + well_holder_sequence
    locations = jnp.take(well_position_inside, sorted_values) + strip_base // NBS * (CY * SPAN_EAST)
    linear_warmth = warmth_before.reshape(overall_slabs, overall_tubes)
    flat_cond = conduct.reshape(overall_slabs, overall_tubes)
    stratum_lines = jnp.take(linear_warmth, locations, axis=1).T
    conductance_lines = jnp.take(flat_cond, locations, axis=1).T
    withdrawal, leaving_warmth = liquid_circuit(stratum_lines, conductance_lines, jnp.take(entering_warmth, sorted_values), jnp.take(well_transfer_speed, sorted_values), jnp.take(well_reach, sorted_values))
    source_vector_linear = warmed_state.reshape(overall_slabs, overall_tubes).at[:, locations].add(-storage_volume * withdrawal.T)
    blocks = linkage_factor.shape[0]
    block_size = pivot_matrix_reciprocal.shape[1]
    inverses = pivot_matrix_reciprocal.reshape(blocks, block_size, block_size)
    local_part = jnp.einsum('jrc,jcn->jrn', inverses, source_vector_linear.reshape(blocks, block_size, overall_tubes), precision=lax.Precision.HIGHEST)
    corners = jnp.stack([inverses[:, 0, 0], inverses[:, 0, -1], inverses[:, -1, 0], inverses[:, -1, -1], linkage_factor], axis=1)
    scalars = reduced_scalars(corners, block_size)
    couple_now, couple_next = (scalars[0], scalars[1])
    ratio_before = scalars[5]
    prefix_before, first_here, first_next = sweep_all(scalars, local_part[:, 0], local_part[:, -1])
    last_before = prefix_before + ratio_before[:, None] * first_here
    solved = local_part + (couple_now[:, None] * inverses[:, :, 0])[:, :, None] * last_before[:, None, :]
    solved = solved + (couple_next[:, None] * inverses[:, :, -1])[:, :, None] * first_next[:, None, :]
    return (solved.reshape(overall_slabs, overall_lines, span_eastward), leaving_warmth)
```

```python
import jax
import jax.numpy as jnp
from jax import lax
from jax.experimental import pallas as pl
from jax.experimental.pallas import tpu as pltpu
from jax.sharding import PartitionSpec as P

F32 = jnp.float32
BF16 = jnp.bfloat16
MESH = pl.DeviceIdType.MESH
HIGHEST = lax.Precision.HIGHEST

CZ, CY, CX = 32, 64, 1024
NB = 128
ND = 16
NS = 8
YT = 8
NT = CY // YT
HX = CX // 2
PAD = 8


def dot(a, b, precision=None):
    return lax.dot_general(
        a, b, (((1,), (0,)), ((), ())), precision=precision, preferred_element_type=F32
    )


def split(v):
    hi = v.astype(BF16)
    lo = (v - hi.astype(F32)).astype(BF16)
    return hi, lo


def iota(shape, dim):
    return lax.broadcasted_iota(jnp.int32, shape, dim)


def lookup(cat, table):
    b0 = (cat & 1) != 0
    b1 = (cat & 2) != 0
    b2 = cat >= 4
    pick = lambda m, hi, lo: jnp.where(m, hi, lo)
    e = [pick(b0, table[2 * i + 1], table[2 * i]) for i in range(4)]
    return pick(b2, pick(b1, e[3], e[2]), pick(b1, e[1], e[0]))


def kernel(
    t_h, cat_h, table_s, g_ref, link_s, pos_ref, perm_s, reach_ref, inlet_ref, speed_ref,
    local_h, pq_h, leave_s,
    t_v, k_v, cat_v, h_v, ohx, oht, khi, klo, acc_r, acc_c, rate_v, rock_v, down_v, up_v, wmat,
    gs, ga, hs, hr, fl, rx, tx, coef,
    in_t, in_c, h_send, h_recv, g_send, g_recv, a_send, a_recv, b_send, b_recv, out_sem, own_sem,
):
    me = lax.axis_index("depth")
    strip = lax.axis_index("strip")
    north = lax.rem(strip + NS - 1, NS)
    south = lax.rem(strip + 1, NS)

    def rows(t):
        return pl.ds(pl.multiple_of(t * YT, YT), YT)

    def prows(t):
        return pl.ds(pl.multiple_of(t * YT + PAD, YT), YT)

    def order(i):
        return jnp.where(i == 0, 0, jnp.where(i == 1, NT - 1, i - 1))

    def load_t(t):
        return pltpu.make_async_copy(t_h.at[:, rows(t), :], t_v.at[:, prows(t), :], in_t.at[t])

    def load_c(t):
        return pltpu.make_async_copy(cat_h.at[:, rows(t), :], cat_v.at[:, rows(t), :], in_c.at[t])

    for i in range(NT):
        t = (0, NT - 1, 1, 2, 3, 4, 5, 6)[i]
        load_c(t).start()
        load_t(t).start()

    barrier = pltpu.get_barrier_semaphore()
    pl.semaphore_signal(barrier, inc=1, device_id={"strip": north}, device_id_type=MESH)
    pl.semaphore_signal(barrier, inc=1, device_id={"strip": south}, device_id_type=MESH)

    def greet(j, c):
        @pl.when(j != me)
        def _():
            pl.semaphore_signal(barrier, inc=1, device_id={"depth": j}, device_id_type=MESH)
        return c

    lax.fori_loop(0, ND, greet, 0)

    table = [table_s[i] for i in range(8)]
    pos = pos_ref[...]
    xpos = pos & (CX - 1)
    ypos = pos >> 10

    ohx[...] = (iota((CX, NB), 0) == xpos).astype(F32).astype(BF16)
    xcol = jnp.transpose(jnp.broadcast_to(xpos, (NB, NB)))
    for q in range(CX // NB):
        oht[:, q * NB : (q + 1) * NB] = (
            (iota((NB, NB), 1) + q * NB == xcol).astype(F32).astype(BF16)
        )
    g = g_ref[...]
    spread = ((iota((256, CZ), 0) >> 3) == iota((256, CZ), 1)).astype(F32)
    spread_t = ((iota((CZ, 256), 1) >> 3) == iota((CZ, 256), 0)).astype(F32)
    wide = dot(dot(spread, g, HIGHEST), spread_t, HIGHEST)
    wide = jnp.where((iota((256, 256), 0) & 7) == (iota((256, 256), 1) & 7), wide, 0.0)
    whi, wlo = split(wide)
    khi[...] = whi
    klo[...] = wlo
    acc_r[...] = jnp.zeros_like(acc_r)
    acc_c[...] = jnp.zeros_like(acc_c)

    pl.semaphore_wait(barrier, ND - 1 + 2)

    def halo_copies():
        up = pltpu.make_async_remote_copy(
            src_ref=hs.at[0], dst_ref=hr.at[1], send_sem=h_send.at[0], recv_sem=h_recv.at[1],
            device_id={"strip": north}, device_id_type=MESH)
        down = pltpu.make_async_remote_copy(
            src_ref=hs.at[1], dst_ref=hr.at[0], send_sem=h_send.at[1], recv_sem=h_recv.at[0],
            device_id={"strip": south}, device_id_type=MESH)
        return up, down

    def first_pass(i, c):
        t = order(i)
        load_c(t).wait()
        load_t(t).wait()

        def planes(z4, c2):
            for u in range(4):
                z = z4 * 4 + u
                k_v[z, prows(t), :] = lookup(cat_v[z, rows(t), :], table)
            return c2

        lax.fori_loop(0, CZ // 4, planes, 0)
        hi, lo = split(t_v[:, prows(t), :].reshape(256, CX))
        cats = cat_v[:, rows(t), :].reshape(256, CX).astype(F32).astype(BF16)
        sel = ohx[...]
        got = dot(hi, sel) + dot(lo, sel)
        kind = dot(cats, sel)
        here = ((iota((YT, NB), 0) + t * YT) == ypos).astype(F32)
        acc_r[...] += got.reshape(CZ, YT, NB) * here
        acc_c[...] += kind.reshape(CZ, YT, NB) * here

        @pl.when(i == 1)
        def _():
            hs[0, 0] = t_v[:, PAD, :]
            hs[0, 1] = k_v[:, PAD, :]
            hs[1, 0] = t_v[:, PAD + CY - 1, :]
            hs[1, 1] = k_v[:, PAD + CY - 1, :]
            for cp in halo_copies():
                cp.start()
        return c

    lax.fori_loop(0, NT, first_pass, 0)

    rock = jnp.sum(acc_r[...], axis=1)
    kind = jnp.sum(acc_c[...], axis=1).astype(jnp.int32)
    cond = lookup(kind, table)
    level = iota((CZ, NB), 0) + me * CZ
    rate = speed_ref[...] * cond / (1.0 + cond)
    rate = jnp.where(level < reach_ref[...], rate, 0.0)
    rate_v[...] = rate
    rock_v[...] = rock
    prod = jnp.ones((1, NB), F32)
    add_d = jnp.zeros((1, NB), F32)
    add_r = jnp.zeros((1, NB), F32)
    for z in range(CZ):
        r = rate_v[z : z + 1, :]
        prod = prod * (1.0 - r)
        add_d = (1.0 - r) * add_d + r * rock_v[z : z + 1, :]
    for z in reversed(range(CZ)):
        r = rate_v[z : z + 1, :]
        add_r = (1.0 - r) * add_r + r * rock_v[z : z + 1, :]
    gs[0:1, :] = prod
    gs[1:2, :] = add_d
    gs[2:3, :] = add_r
    last = CZ - 1
    gs[3:4, :] = jnp.broadcast_to(g_ref[0:1, 0:1], (1, NB))
    gs[4:5, :] = jnp.broadcast_to(g_ref[0:1, last:CZ], (1, NB))
    gs[5:6, :] = jnp.broadcast_to(g_ref[last:CZ, 0:1], (1, NB))
    gs[6:7, :] = jnp.broadcast_to(g_ref[last:CZ, last:CZ], (1, NB))
    gs[7:8, :] = jnp.full((1, NB), link_s[0], F32)
    ga[me] = gs[...]

    def g_copy(j):
        return pltpu.make_async_remote_copy(
            src_ref=gs, dst_ref=ga.at[me], send_sem=g_send.at[j], recv_sem=g_recv.at[me],
            device_id={"depth": j}, device_id_type=MESH)

    def others(fn):
        def step(i, c):
            fn(lax.rem(me + i, ND))
            return c
        lax.fori_loop(1, ND, step, 0)

    others(lambda j: g_copy(j).start())

    up, down = halo_copies()
    up.wait()
    down.wait()
    has_north = (strip > 0).astype(F32)
    has_south = (strip < NS - 1).astype(F32)
    t_v[:, PAD - 1, :] = hr[0, 0] * has_north
    k_v[:, PAD - 1, :] = hr[0, 1] * has_north
    t_v[:, PAD + CY, :] = hr[1, 0] * has_south
    k_v[:, PAD + CY, :] = hr[1, 1] * has_south

    sub = iota((YT, CX), 0)
    lane = iota((YT, CX), 1)
    top, bottom = sub == 0, sub == YT - 1
    west, east = lane == 0, lane == CX - 1

    def tile_of(i):
        return lax.rem((me >> 1) + i, NT)

    def stencil(i, c):
        t = tile_of(i)

        def plane(z, c2):
            tc = t_v[z, prows(t), :]
            kc = k_v[z, prows(t), :]
            y0 = t * YT + PAD
            ta = t_v[z, pl.ds(y0 - 1, 1), :]
            ka = k_v[z, pl.ds(y0 - 1, 1), :]
            tb = t_v[z, pl.ds(y0 + YT, 1), :]
            kb = k_v[z, pl.ds(y0 + YT, 1), :]
            tu = jnp.where(top, ta, pltpu.roll(tc, 1, 0))
            ku = jnp.where(top, ka, pltpu.roll(kc, 1, 0))
            face = (kc + ku) * (tu - tc)
            below = (kc + kb) * (tb - tc)
            flux = face + jnp.where(bottom, below, -pltpu.roll(face, YT - 1, 0))
            te = jnp.where(east, 0.0, pltpu.roll(tc, CX - 1, 1))
            ke = jnp.where(east, 0.0, pltpu.roll(kc, CX - 1, 1))
            fe = (kc + ke) * (te - tc)
            fw = jnp.where(west, kc * tc, pltpu.roll(fe, 1, 1))
            flux = flux + (fe - fw)
            h_v[z, rows(t), :] = tc + 0.1 * flux
            return c2

        lax.fori_loop(0, CZ, plane, 0)
        return c

    lax.fori_loop(0, NT, stencil, 0)

    others(lambda j: pltpu.make_async_remote_copy(
        src_ref=gs, dst_ref=ga.at[j], send_sem=g_send.at[j], recv_sem=g_recv.at[j],
        device_id={"depth": j}, device_id_type=MESH).wait())

    flow = inlet_ref[...]
    mine = jnp.zeros((1, NB), F32)
    for j in range(ND):
        mine = mine + flow * (me == j).astype(F32)
        flow = ga[j, 0:1, :] * flow + ga[j, 1:2, :]
    rising = jnp.zeros((1, NB), F32)
    for j in reversed(range(ND)):
        rising = rising + flow * (me == j).astype(F32)
        flow = ga[j, 0:1, :] * flow + ga[j, 2:3, :]
    who = iota((1, NB), 1)
    for b in range(NB // ND):
        leave_s[b] = jnp.sum(jnp.where(who == perm_s[me * (NB // ND) + b], flow, 0.0))
    for z in range(CZ):
        r = rate_v[z : z + 1, :]
        down_v[z : z + 1, :] = mine
        mine = (1.0 - r) * mine + r * rock_v[z : z + 1, :]
    for z in reversed(range(CZ)):
        r = rate_v[z : z + 1, :]
        up_v[z : z + 1, :] = rising
        rising = (1.0 - r) * rising + r * rock_v[z : z + 1, :]
    ext = rate_v[...] * (2.0 * rock_v[...] - down_v[...] - up_v[...])
    wmat[...] = -2.0 * dot(g_ref[...], ext, HIGHEST)

    one = jnp.ones((1, NB), F32)
    zero = jnp.zeros((1, NB), F32)
    cs = [zero]
    for j in range(1, ND):
        cs.append(ga[j, 7:8, :] * (CZ / (CZ + 1.0)) / jnp.sqrt(ga[j - 1, 6:7, :] * ga[j, 3:4, :]))
    cs.append(zero)
    q = zero
    for j in range(ND):
        vf = cs[j] * ga[j, 3:4, :]
        vl = cs[j] * ga[j, 5:6, :]
        wf = cs[j + 1] * ga[j, 4:5, :]
        wl = cs[j + 1] * ga[j, 6:7, :]
        den = one - vf * q
        inv = one / den
        coef[j, 0:1, :] = vl * q * inv
        coef[j, 1:2, :] = vl * inv
        coef[j, 2:3, :] = inv
        coef[j, 3:4, :] = vf * inv
        coef[j, 4:5, :] = wf * inv
        coef[j, 5:6, :] = cs[j]
        coef[j, 6:7, :] = q
        coef[j, 7:8, :] = cs[j + 1]
        q = wl + vl * q * wf * inv

    def a_copy(o, source):
        return pltpu.make_async_remote_copy(
            src_ref=fl.at[o], dst_ref=rx.at[source], send_sem=a_send.at[o],
            recv_sem=a_recv.at[source], device_id={"depth": o}, device_id_type=MESH)

    def out_copy(t):
        return pltpu.make_async_copy(
            h_v.at[:, rows(t), :], local_h.at[:, rows(t), :], out_sem.at[t])

    def solve(i, c):
        t = tile_of(i)
        here = ((iota((YT, NB), 0) + t * YT) == ypos).astype(F32)
        lhs = (wmat[...][:, None, :] * here[None, :, :]).reshape(256, NB)
        lhi, llo = split(lhs)
        for n in range(4):
            cols = slice(n * 256, (n + 1) * 256)
            hi, lo = split(h_v[:, rows(t), cols].reshape(256, 256))
            out = dot(khi[...], hi) + dot(khi[...], lo) + dot(klo[...], hi)
            out = out + dot(lhi, oht[:, cols]) + dot(llo, oht[:, cols])
            out = out.reshape(CZ, YT, 256)
            h_v[:, rows(t), cols] = out
            part = slice((n % 2) * 256, (n % 2) * 256 + 256)
            fl[2 * t + n // 2, 0, :, part] = out[0]
            fl[2 * t + n // 2, 1, :, part] = out[CZ - 1]
        out_copy(t).start()
        for half in range(2):
            o = 2 * t + half

            @pl.when(o == me)
            def _():
                rx[me] = fl[o]

            @pl.when(o != me)
            def _():
                a_copy(o, me).start()
        return c

    lax.fori_loop(0, NT, solve, 0)

    others(lambda j: a_copy(j, j).wait())

    for xs in range(HX // 128):
        cols = slice(xs * 128, (xs + 1) * 128)
        p = jnp.zeros((YT, 128), F32)
        ps = []
        for j in range(ND):
            ps.append(p)
            p = rx[j, 1, :, cols] + coef[j, 0:1, :] * rx[j, 0, :, cols] + coef[j, 1:2, :] * p
        a = jnp.zeros((YT, 128), F32)
        for j in reversed(range(ND)):
            tx[j, 1, :, cols] = coef[j, 7:8, :] * a
            a = coef[j, 2:3, :] * rx[j, 0, :, cols] + coef[j, 3:4, :] * ps[j] + coef[j, 4:5, :] * a
            tx[j, 0, :, cols] = coef[j, 5:6, :] * (ps[j] + coef[j, 6:7, :] * a)

    def block_of(o):
        return (slice(None), rows(o >> 1), pl.ds(pl.multiple_of((o & 1) * HX, HX), HX))

    def b_copy(j, source):
        return pltpu.make_async_remote_copy(
            src_ref=tx.at[j], dst_ref=pq_h.at[block_of(source)], send_sem=b_send.at[j],
            recv_sem=b_recv.at[source], device_id={"depth": j}, device_id_type=MESH)

    others(lambda j: b_copy(j, me).start())
    own = pltpu.make_async_copy(tx.at[me], pq_h.at[block_of(me)], own_sem)
    own.start()
    for t in range(NT):
        out_copy(t).wait()
    own.wait()
    others(lambda j: b_copy(j, j).wait())


def fused(*args):
    dma = pltpu.SemaphoreType.DMA
    vm = lambda *s: pltpu.VMEM(s, F32)
    vb = lambda *s: pltpu.VMEM(s, BF16)
    any_ = pl.BlockSpec(memory_space=pl.ANY)
    smem = pl.BlockSpec(memory_space=pltpu.SMEM)
    vmem = pl.BlockSpec(memory_space=pltpu.VMEM)
    return pl.pallas_call(
        kernel,
        out_shape=(
            jax.ShapeDtypeStruct((CZ, CY, CX), F32),
            jax.ShapeDtypeStruct((2, CY, CX), F32),
            jax.ShapeDtypeStruct((NB // ND,), F32),
        ),
        in_specs=[any_, any_, smem, vmem, smem, vmem, smem, vmem, vmem, vmem],
        out_specs=(any_, any_, smem),
        scratch_shapes=[
            vm(CZ, CY + 2 * PAD, CX), vm(CZ, CY + 2 * PAD, CX),
            pltpu.VMEM((CZ, CY, CX), jnp.int32), vm(CZ, CY, CX),
            vb(CX, NB), vb(NB, CX), vb(256, 256), vb(256, 256),
            vm(CZ, YT, NB), vm(CZ, YT, NB),
            vm(CZ, NB), vm(CZ, NB), vm(CZ, NB), vm(CZ, NB), vm(CZ, NB),
            vm(8, NB), vm(ND, 8, NB),
            vm(2, 2, CZ, CX), vm(2, 2, CZ, CX),
            vm(ND, 2, YT, HX), vm(ND, 2, YT, HX), vm(ND, 2, YT, HX),
            vm(ND, 8, NB),
            dma((NT,)), dma((NT,)), dma((2,)), dma((2,)),
            dma((ND,)), dma((ND,)), dma((ND,)), dma((ND,)), dma((ND,)), dma((ND,)),
            dma((NT,)), dma,
        ],
        compiler_params=pltpu.CompilerParams(
            collective_id=0, has_side_effects=True, vmem_limit_bytes=60 * 1024 * 1024
        ),
    )(*args)


def body(warmth, category, catalogue, pivot, linkage, position, holder, reach, entering, speed):
    row = lambda v: v.reshape(1, NB)
    local, pq, leaving = fused(
        warmth, category, catalogue, pivot, linkage, row(position), holder, row(reach),
        row(entering), row(speed),
    )
    solved = local + pivot[:, 0][:, None, None] * pq[0][None]
    solved = solved + pivot[:, CZ - 1][:, None, None] * pq[1][None]
    return solved, leaving


def solution(mesh):
    in_specs = (
        P("depth", "strip", None),
        P("depth", "strip", None),
        P(),
        P("depth", None),
        P("depth"),
        P("strip"),
        P("strip"),
        P("strip"),
        P("strip"),
        P("strip"),
    )
    out_specs = (P("depth", "strip", None), P(("strip", "depth")))
    return jax.shard_map(body, mesh=mesh, in_specs=in_specs, out_specs=out_specs, check_vma=False)
```

```python
import jax
import jax.numpy as jnp
from jax import lax
from jax.experimental import pallas as pl
from jax.experimental.pallas import tpu as pltpu
from jax.sharding import PartitionSpec as P

F32 = jnp.float32
BF16 = jnp.bfloat16
MESH = pl.DeviceIdType.MESH
HIGHEST = lax.Precision.HIGHEST

CZ, CY, CX = 32, 64, 1024
NB = 128
ND = 16
NS = 8
YT = 8
NT = CY // YT
HX = CX // 2
PAD = 8
NX = CX // 128
YR = CY + 2 * PAD
ZR = NX * YR
VMEM_LIMIT = 60 * 1024 * 1024


def dot(a, b, precision=None):
    return lax.dot_general(
        a, b, (((1,), (0,)), ((), ())), precision=precision, preferred_element_type=F32
    )


def split(v):
    hi = v.astype(BF16)
    lo = (v - hi.astype(F32)).astype(BF16)
    return hi, lo


def iota(shape, dim):
    return lax.broadcasted_iota(jnp.int32, shape, dim)


def kernel(
    t_h, cat_h, table_s, g_ref, link_s, pos_s, pos_ref, perm_s, reach_ref, inlet_ref, speed_ref,
    h_o, pq_h, leave_s,
    t_v, k_v, cat_v, x3, kcat, oht, rate_v, rock_v, down_v, up_v, west_v,
    gs, ga, ws, wa, hs, hr, fl, rx, tx, coef,
    in_t, in_c, h_send, h_recv, g_send, g_recv, w_send, w_recv, a_send, a_recv, b_send, b_recv,
    own_sem,
):
    me = lax.axis_index("depth")
    strip = lax.axis_index("strip")
    north = lax.rem(strip + NS - 1, NS)
    south = lax.rem(strip + 1, NS)
    first = me >> 1
    t2 = t_v.reshape(CZ * ZR, 128)
    k2 = k_v.reshape(CZ * ZR, 128)

    def rows(t):
        return pl.ds(pl.multiple_of(t * YT, YT), YT)

    def prows(t):
        return pl.ds(pl.multiple_of(t * YT + PAD, YT), YT)

    def edge(t):
        return jnp.logical_or(t == 0, t == NT - 1)

    def load_c(t):
        return pltpu.make_async_copy(cat_h.at[:, rows(t), :], cat_v.at[:, rows(t), :], in_c.at[t])

    def load_t(t, x):
        return pltpu.make_async_copy(
            t_h.at[:, rows(t), x * 128 : (x + 1) * 128], t_v.at[:, x, prows(t), :], in_t.at[t, x])

    def load(t):
        load_c(t).start()
        for x in range(NX):
            load_t(t, x).start()

    def ring(i):
        return lax.rem(first + NT - 1 + i, NT)

    load(0)
    load(NT - 1)

    def load_rest(i, c):
        t = ring(i)

        @pl.when(jnp.logical_not(edge(t)))
        def _():
            load(t)
        return c

    lax.fori_loop(0, NT, load_rest, 0)

    barrier = pltpu.get_barrier_semaphore()
    pl.semaphore_signal(barrier, inc=1, device_id={"strip": north}, device_id_type=MESH)
    pl.semaphore_signal(barrier, inc=1, device_id={"strip": south}, device_id_type=MESH)

    def others(fn):
        def step(i, c):
            fn(lax.rem(me + i, ND))
            return c
        lax.fori_loop(1, ND, step, 0)

    others(lambda j: pl.semaphore_signal(
        barrier, inc=1, device_id={"depth": j}, device_id_type=MESH))

    table = [table_s[i] * 0.1 for i in range(8)]
    level_of = jnp.zeros((8, 128), F32)
    for i in range(8):
        level_of = jnp.where(iota((8, 128), 0) == i, table[i], level_of)

    def pick(cat):
        return jnp.take_along_axis(level_of, cat, axis=0, mode="promise_in_bounds")

    g = g_ref[...]
    spread = ((iota((256, CZ), 0) >> 3) == iota((256, CZ), 1)).astype(F32)
    spread_t = ((iota((CZ, 256), 1) >> 3) == iota((CZ, 256), 0)).astype(F32)
    wide = dot(dot(spread, g, HIGHEST), spread_t, HIGHEST)
    wide = jnp.where((iota((256, 256), 0) & 7) == (iota((256, 256), 1) & 7), wide, 0.0)
    whi, wlo = split(wide)
    kcat[:, 0:256] = whi
    kcat[:, 256:512] = whi
    kcat[:, 512:768] = wlo
    pos = pos_ref[...]
    ypos = pos >> 10
    xcol = jnp.transpose(jnp.broadcast_to(pos & (CX - 1), (NB, NB)))
    for q in range(NX):
        hot = (iota((NB, NB), 1) + q * NB == xcol).astype(F32).astype(BF16)
        oht[0:NB, q * NB : (q + 1) * NB] = hot
        oht[NB : 2 * NB, q * NB : (q + 1) * NB] = hot

    pl.semaphore_wait(barrier, ND - 1 + 2)

    def halo_copies():
        up = pltpu.make_async_remote_copy(
            src_ref=hs.at[0], dst_ref=hr.at[1], send_sem=h_send.at[0], recv_sem=h_recv.at[1],
            device_id={"strip": north}, device_id_type=MESH)
        down = pltpu.make_async_remote_copy(
            src_ref=hs.at[1], dst_ref=hr.at[0], send_sem=h_send.at[1], recv_sem=h_recv.at[0],
            device_id={"strip": south}, device_id_type=MESH)
        return up, down

    def lines(z, x, y):
        return pl.ds(z * ZR + x * YR + y, 8, stride=ZR)

    def arrive(t):
        load_c(t).wait()
        for x in range(NX):
            load_t(t, x).wait()

        def planes(i, c):
            for u in range(4):
                z = i * 4 + u
                for x in range(NX):
                    k_v[z, x, prows(t), :] = pick(cat_v[z, rows(t), x * 128 : (x + 1) * 128])
            return c

        lax.fori_loop(0, CZ // 4, planes, 0)

    arrive(0)
    for x in range(NX):
        for z in range(0, CZ, 8):
            hs[0, 0, x, z : z + 8, :] = t2[lines(z, x, PAD), :]
            hs[0, 1, x, z : z + 8, :] = k2[lines(z, x, PAD), :]
    halo_copies()[0].start()
    arrive(NT - 1)
    for x in range(NX):
        for z in range(0, CZ, 8):
            hs[1, 0, x, z : z + 8, :] = t2[lines(z, x, PAD + CY - 1), :]
            hs[1, 1, x, z : z + 8, :] = k2[lines(z, x, PAD + CY - 1), :]
    halo_copies()[1].start()

    def arrive_inner(t):
        @pl.when(jnp.logical_not(edge(t)))
        def _():
            arrive(t)

    arrive_inner(ring(0))
    arrive_inner(ring(1))

    def g_copy(j, source):
        return pltpu.make_async_remote_copy(
            src_ref=gs, dst_ref=ga.at[source], send_sem=g_send.at[j], recv_sem=g_recv.at[source],
            device_id={"depth": j}, device_id_type=MESH)

    def w_copy(j, source):
        return pltpu.make_async_remote_copy(
            src_ref=ws, dst_ref=wa.at[source], send_sem=w_send.at[j], recv_sem=w_recv.at[source],
            device_id={"depth": j}, device_id_type=MESH)

    def halo_in():
        up, down = halo_copies()
        up.wait()
        down.wait()
        has_north = (strip > 0).astype(F32)
        has_south = (strip < NS - 1).astype(F32)
        for x in range(NX):
            for z in range(0, CZ, 8):
                t2[lines(z, x, PAD - 1), :] = hr[0, 0, x, z : z + 8, :] * has_north
                k2[lines(z, x, PAD - 1), :] = hr[0, 1, x, z : z + 8, :] * has_north
                t2[lines(z, x, PAD + CY), :] = hr[1, 0, x, z : z + 8, :] * has_south
                k2[lines(z, x, PAD + CY), :] = hr[1, 1, x, z : z + 8, :] * has_south

    who8 = iota((8, NB), 1)

    def wells():
        def fetch(i, acc):
            acc = list(acc)
            for u in range(4):
                b = i * 4 + u
                p = pos_s[b]
                base = ((p >> 7) & 7) * YR + (p >> 10) + PAD
                shift = (b - p) & 127
                mine = who8 == b
                for zg in range(4):
                    at = pl.ds(base + zg * 8 * ZR, 8, stride=ZR)
                    acc[zg] = jnp.where(mine, pltpu.roll(t2[at, :], shift, 1), acc[zg])
                    acc[4 + zg] = jnp.where(mine, pltpu.roll(k2[at, :], shift, 1), acc[4 + zg])
            return tuple(acc)

        acc = lax.fori_loop(0, NB // 4, fetch, tuple(jnp.zeros((8, NB), F32) for _ in range(8)))
        for zg in range(4):
            part = slice(zg * 8, zg * 8 + 8)
            cond = 10.0 * acc[4 + zg]
            rate = speed_ref[...] * cond / (1.0 + cond)
            level = iota((8, NB), 0) + (me * CZ + zg * 8)
            rate_v[part, :] = jnp.where(level < reach_ref[...], rate, 0.0)
            rock_v[part, :] = acc[zg]
        prod = jnp.ones((1, NB), F32)
        add_d = jnp.zeros((1, NB), F32)
        add_r = jnp.zeros((1, NB), F32)
        for z in range(CZ):
            r = rate_v[z : z + 1, :]
            prod = prod * (1.0 - r)
            add_d = (1.0 - r) * add_d + r * rock_v[z : z + 1, :]
            y = CZ - 1 - z
            r = rate_v[y : y + 1, :]
            add_r = (1.0 - r) * add_r + r * rock_v[y : y + 1, :]
        gs[0:1, :] = prod
        gs[1:2, :] = add_d
        gs[2:3, :] = add_r
        last = CZ - 1
        gs[3:4, :] = jnp.broadcast_to(g_ref[0:1, 0:1], (1, NB))
        gs[4:5, :] = jnp.broadcast_to(g_ref[0:1, last:CZ], (1, NB))
        gs[5:6, :] = jnp.broadcast_to(g_ref[last:CZ, 0:1], (1, NB))
        gs[6:7, :] = jnp.broadcast_to(g_ref[last:CZ, last:CZ], (1, NB))
        gs[7:8, :] = jnp.full((1, NB), link_s[0], F32)
        ga[me] = gs[...]
        others(lambda j: g_copy(j, me).start())

    def a_copy(o, source):
        return pltpu.make_async_remote_copy(
            src_ref=fl.at[o], dst_ref=rx.at[source], send_sem=a_send.at[o],
            recv_sem=a_recv.at[source], device_id={"depth": o}, device_id_type=MESH)

    west, east = who8 == 0, who8 == 127

    def face_row(z, t, xs):
        base = pl.multiple_of(z * ZR + t * YT + PAD, YT)
        tc = {x: t2[pl.ds(base + x * YR, YT), :] for x in xs}
        kc = {x: k2[pl.ds(base + x * YR, YT), :] for x in xs}
        return base, tc, kc

    def block(t, n):
        xs = [x for x in range(2 * n, 2 * n + 3) if x < NX]
        done = []
        for z in range(CZ):
            base, tc, kc = face_row(z, t, xs)
            rt = {x: pltpu.roll(tc[x], 127, 1) for x in xs}
            rk = {x: pltpu.roll(kc[x], 127, 1) for x in xs}
            prev = west_v[z] if n > 0 else None
            out = []
            for x in (2 * n, 2 * n + 1):
                te = jnp.where(east, rt[x + 1] if x + 1 < NX else 0.0, rt[x])
                ke = jnp.where(east, rk[x + 1] if x + 1 < NX else 0.0, rk[x])
                fe = (kc[x] + ke) * (te - tc[x])
                rf = pltpu.roll(fe, 1, 1)
                fw = jnp.where(west, kc[x] * tc[x] if prev is None else prev, rf)
                prev = rf
                ta = t2[pl.ds(base + x * YR - 1, YT), :]
                ka = k2[pl.ds(base + x * YR - 1, YT), :]
                tb = t2[pl.ds(base + x * YR + 1, YT), :]
                kb = k2[pl.ds(base + x * YR + 1, YT), :]
                flux = (kc[x] + ka) * (ta - tc[x]) + (kc[x] + kb) * (tb - tc[x])
                out.append(tc[x] + (flux + (fe - fw)))
            if n < 3:
                west_v[z] = prev
            done.append(jnp.concatenate(out, axis=1))
            if z % 2 == 1:
                hi, lo = split(jnp.concatenate(done, axis=0))
                done = []
                at = (z - 1) * 8
                x3[n, at : at + 16, :] = hi
                x3[n, 256 + at : 256 + at + 16, :] = lo
                x3[n, 512 + at : 512 + at + 16, :] = hi
        res = dot(kcat[...], x3[n]).reshape(CZ, YT, 256)
        cols = slice(n * 256, n * 256 + 256)
        h_o[:, rows(t), cols] = res
        part = slice((n % 2) * 256, (n % 2) * 256 + 256)
        fl[2 * t + n // 2, 0, :, part] = res[0]
        fl[2 * t + n // 2, 1, :, part] = res[CZ - 1]

    def work(i, c):
        t = ring(i + 1)

        @pl.when(i < 6)
        def _():
            arrive_inner(ring(i + 2))

        @pl.when(i == 5)
        def _():
            wells()

        @pl.when(i == 0)
        def _():
            halo_in()

        for n in range(4):
            block(t, n)
        for half in range(2):
            o = 2 * t + half

            @pl.when(o == me)
            def _():
                rx[me] = fl[o]

            @pl.when(o != me)
            def _():
                a_copy(o, me).start()
        return c

    lax.fori_loop(0, NT, work, 0)

    others(lambda j: g_copy(j, j).wait())

    flow = inlet_ref[...]
    mine = jnp.zeros((1, NB), F32)
    for j in range(ND):
        mine = mine + flow * (me == j).astype(F32)
        flow = ga[j, 0:1, :] * flow + ga[j, 1:2, :]
    rising = jnp.zeros((1, NB), F32)
    for j in reversed(range(ND)):
        rising = rising + flow * (me == j).astype(F32)
        flow = ga[j, 0:1, :] * flow + ga[j, 2:3, :]
    for z in range(CZ):
        r = rate_v[z : z + 1, :]
        down_v[z : z + 1, :] = mine
        mine = (1.0 - r) * mine + r * rock_v[z : z + 1, :]
        y = CZ - 1 - z
        r = rate_v[y : y + 1, :]
        up_v[y : y + 1, :] = rising
        rising = (1.0 - r) * rising + r * rock_v[y : y + 1, :]
    ext = rate_v[...] * (2.0 * rock_v[...] - down_v[...] - up_v[...])
    wmat = -2.0 * dot(g, ext, HIGHEST)
    ws[0:1, :] = wmat[0:1, :]
    ws[1:2, :] = wmat[CZ - 1 : CZ, :]
    wa[me, 0:2, :] = ws[0:2, :]
    others(lambda j: w_copy(j, me).start())

    one = jnp.ones((1, NB), F32)
    zero = jnp.zeros((1, NB), F32)
    cs = [zero]
    for j in range(1, ND):
        cs.append(ga[j, 7:8, :] * (CZ / (CZ + 1.0)) / jnp.sqrt(ga[j - 1, 6:7, :] * ga[j, 3:4, :]))
    cs.append(zero)
    q = zero
    for j in range(ND):
        vf = cs[j] * ga[j, 3:4, :]
        vl = cs[j] * ga[j, 5:6, :]
        wf = cs[j + 1] * ga[j, 4:5, :]
        wl = cs[j + 1] * ga[j, 6:7, :]
        den = one - vf * q
        inv = one / den
        coef[j, 0:1, :] = vl * q * inv
        coef[j, 1:2, :] = vl * inv
        coef[j, 2:3, :] = inv
        coef[j, 3:4, :] = vf * inv
        coef[j, 4:5, :] = wf * inv
        coef[j, 5:6, :] = cs[j]
        coef[j, 6:7, :] = q
        coef[j, 7:8, :] = cs[j + 1]
        q = wl + vl * q * wf * inv

    def hot_rows(w, t):
        here = ((iota((YT, NB), 0) + t * YT) == ypos).astype(F32)
        hi, lo = split((w[:, None, :] * here[None, :, :]).reshape(w.shape[0] * YT, NB))
        return jnp.concatenate([hi, lo], axis=1)

    others(lambda j: w_copy(j, j).wait())
    lhs = hot_rows(wa[:, 0:2, :].reshape(2 * ND, NB), me >> 1)
    half = pl.ds(pl.multiple_of((me & 1) * HX, HX), HX)
    wells_part = dot(lhs, oht[:, half]).reshape(ND, 2, YT, HX)
    others(lambda j: a_copy(j, j).wait())
    rx[...] += wells_part

    for xs in range(HX // 128):
        cols = slice(xs * 128, (xs + 1) * 128)
        p = jnp.zeros((YT, 128), F32)
        ps = []
        for j in range(ND):
            ps.append(p)
            p = rx[j, 1, :, cols] + coef[j, 0:1, :] * rx[j, 0, :, cols] + coef[j, 1:2, :] * p
        a = jnp.zeros((YT, 128), F32)
        for j in reversed(range(ND)):
            tx[j, 1, :, cols] = coef[j, 7:8, :] * a
            a = coef[j, 2:3, :] * rx[j, 0, :, cols] + coef[j, 3:4, :] * ps[j] + coef[j, 4:5, :] * a
            tx[j, 0, :, cols] = coef[j, 5:6, :] * (ps[j] + coef[j, 6:7, :] * a)

    def block_of(o):
        return (slice(None), rows(o >> 1), pl.ds(pl.multiple_of((o & 1) * HX, HX), HX))

    def b_copy(j, source):
        return pltpu.make_async_remote_copy(
            src_ref=tx.at[j], dst_ref=pq_h.at[block_of(source)], send_sem=b_send.at[j],
            recv_sem=b_recv.at[source], device_id={"depth": j}, device_id_type=MESH)

    others(lambda j: b_copy(j, me).start())
    own = pltpu.make_async_copy(tx.at[me], pq_h.at[block_of(me)], own_sem)
    own.start()

    for b in range(NB // ND):
        leave_s[b] = jnp.sum(jnp.where(who8[0:1] == perm_s[me * (NB // ND) + b], flow, 0.0))

    def add_wells(t, c):
        lhs = hot_rows(wmat, t)
        for n in range(4):
            cols = slice(n * 256, n * 256 + 256)
            h_o[:, rows(t), cols] += dot(lhs, oht[:, cols]).reshape(CZ, YT, 256)
        return c

    lax.fori_loop(0, NT, add_wells, 0)
    own.wait()
    others(lambda j: b_copy(j, j).wait())


def fused(*args):
    dma = pltpu.SemaphoreType.DMA
    vm = lambda *s: pltpu.VMEM(s, F32)
    vb = lambda *s: pltpu.VMEM(s, BF16)
    any_ = pl.BlockSpec(memory_space=pl.ANY)
    smem = pl.BlockSpec(memory_space=pltpu.SMEM)
    vmem = pl.BlockSpec(memory_space=pltpu.VMEM)
    return pl.pallas_call(
        kernel,
        out_shape=(
            jax.ShapeDtypeStruct((CZ, CY, CX), F32),
            jax.ShapeDtypeStruct((2, CY, CX), F32),
            jax.ShapeDtypeStruct((NB // ND,), F32),
        ),
        in_specs=[any_, any_, smem, vmem, smem, smem, vmem, smem, vmem, vmem, vmem],
        out_specs=(vmem, any_, smem),
        scratch_shapes=[
            vm(CZ, NX, YR, 128), vm(CZ, NX, YR, 128), pltpu.VMEM((CZ, CY, CX), jnp.int32),
            vb(4, 768, 256), vb(256, 768), vb(2 * NB, CX),
            vm(CZ, NB), vm(CZ, NB), vm(CZ, NB), vm(CZ, NB), vm(CZ, YT, 128),
            vm(8, NB), vm(ND, 8, NB), vm(8, NB), vm(ND, 8, NB),
            vm(2, 2, NX, CZ, 128), vm(2, 2, NX, CZ, 128),
            vm(ND, 2, YT, HX), vm(ND, 2, YT, HX), vm(ND, 2, YT, HX),
            vm(ND, 8, NB),
            dma((NT, NX)), dma((NT,)), dma((2,)), dma((2,)),
            dma((ND,)), dma((ND,)), dma((ND,)), dma((ND,)),
            dma((ND,)), dma((ND,)), dma((ND,)), dma((ND,)), dma,
        ],
        compiler_params=pltpu.CompilerParams(
            collective_id=0, has_side_effects=True, vmem_limit_bytes=VMEM_LIMIT
        ),
    )(*args)


def body(warmth, category, catalogue, pivot, linkage, position, holder, reach, entering, speed):
    row = lambda v: v.reshape(1, NB)
    local, pq, leaving = fused(
        warmth, category, catalogue, pivot, linkage, position, row(position), holder, row(reach),
        row(entering), row(speed),
    )
    solved = local + pivot[:, 0][:, None, None] * pq[0][None]
    solved = solved + pivot[:, CZ - 1][:, None, None] * pq[1][None]
    return solved, leaving


def solution(mesh):
    in_specs = (
        P("depth", "strip", None),
        P("depth", "strip", None),
        P(),
        P("depth", None),
        P("depth"),
        P("strip"),
        P("strip"),
        P("strip"),
        P("strip"),
        P("strip"),
    )
    out_specs = (P("depth", "strip", None), P(("strip", "depth")))
    return jax.shard_map(body, mesh=mesh, in_specs=in_specs, out_specs=out_specs, check_vma=False)
```

```python
import jax
import jax.numpy as jnp
from jax import lax
from jax.experimental import pallas as pl
from jax.experimental.pallas import tpu as pltpu
from jax.sharding import PartitionSpec as P

F32 = jnp.float32
BF16 = jnp.bfloat16
MESH = pl.DeviceIdType.MESH
HIGHEST = lax.Precision.HIGHEST

CZ, CY, CX = 32, 64, 1024
NB = 128
ND = 16
NS = 8
YT = 8
NT = CY // YT
HX = CX // 2
PAD = 8
NX = CX // 128
YR = CY + 2 * PAD
ZR = NX * YR
GZ = 2
PER = 4
VMEM_LIMIT = 52 * 1024 * 1024
FINISH_LIMIT = 16 * 1024 * 1024
OZ = 2
OS = 4


def dot(a, b, precision=None):
    return lax.dot_general(
        a, b, (((1,), (0,)), ((), ())), precision=precision, preferred_element_type=F32
    )


def split(v):
    hi = v.astype(BF16)
    lo = (v - hi.astype(F32)).astype(BF16)
    return hi, lo


def iota(shape, dim):
    return lax.broadcasted_iota(jnp.int32, shape, dim)


def kernel(
    t_h, cat_h, table_s, g_ref, link_s, pos_s, pos_ref, perm_s, reach_ref, inlet_ref, speed_ref,
    h_o, pq_h, leave_s,
    t_v, k_v, f_v, cat_v, x2, fe_s, kcat, oht, rate_v, rock_v, down_v, up_v,
    gs, ga, ws, wa, hs, hr, fl, rx, tx, coef,
    in_t, in_c, h_send, h_recv, g_send, g_recv, w_send, w_recv, a_send, a_recv, b_send, b_recv,
    own_sem,
):
    me = lax.axis_index("depth")
    strip = lax.axis_index("strip")
    north = lax.rem(strip + NS - 1, NS)
    south = lax.rem(strip + 1, NS)
    first = me >> 1
    t2 = t_v.reshape(CZ * ZR, 128)
    k2 = k_v.reshape(CZ * ZR, 128)
    f2 = f_v.reshape(CZ * ZR, 128)

    def rows(t):
        return pl.ds(pl.multiple_of(t * YT, YT), YT)

    def prows(t):
        return pl.ds(pl.multiple_of(t * YT + PAD, YT), YT)

    def load_c(t):
        return pltpu.make_async_copy(cat_h.at[:, rows(t), :], cat_v.at[:, rows(t), :], in_c.at[t])

    def load_t(t, x):
        return pltpu.make_async_copy(
            t_h.at[:, rows(t), x * 128 : (x + 1) * 128], t_v.at[:, x, prows(t), :], in_t.at[t, x])

    def load(t):
        load_c(t).start()
        for x in range(NX):
            load_t(t, x).start()

    def ring(i):
        return lax.rem(first + i, NT)

    load(NT - 1)
    load(0)

    def load_rest(t, c):
        load(t)
        return c

    lax.fori_loop(1, NT - 1, load_rest, 0)

    barrier = pltpu.get_barrier_semaphore()
    pl.semaphore_signal(barrier, inc=1, device_id={"strip": north}, device_id_type=MESH)
    pl.semaphore_signal(barrier, inc=1, device_id={"strip": south}, device_id_type=MESH)

    def others(fn):
        def step(i, c):
            fn(lax.rem(me + i, ND))
            return c
        lax.fori_loop(1, ND, step, 0)

    others(lambda j: pl.semaphore_signal(
        barrier, inc=1, device_id={"depth": j}, device_id_type=MESH))

    table = [table_s[i] * 0.1 for i in range(8)]
    level_of = jnp.zeros((8, 128), F32)
    for i in range(8):
        level_of = jnp.where(iota((8, 128), 0) == i, table[i], level_of)

    def pick(cat):
        return jnp.take_along_axis(level_of, cat, axis=0, mode="promise_in_bounds")

    g = g_ref[...]
    spread = ((iota((256, CZ), 0) >> 3) == iota((256, CZ), 1)).astype(F32)
    spread_t = ((iota((CZ, 256), 1) >> 3) == iota((CZ, 256), 0)).astype(F32)
    wide = dot(dot(spread, g, HIGHEST), spread_t, HIGHEST)
    wide = jnp.where((iota((256, 256), 0) & 7) == (iota((256, 256), 1) & 7), wide, 0.0)
    whi, wlo = split(wide)
    kcat[:, 0:256] = whi
    kcat[:, 256:512] = whi
    kcat[:, 512:768] = wlo
    pos = pos_ref[...]
    ypos = pos >> 10
    xcol = jnp.transpose(jnp.broadcast_to(pos & (CX - 1), (NB, NB)))
    for q in range(NX):
        hot = (iota((NB, NB), 1) + q * NB == xcol).astype(F32).astype(BF16)
        oht[0:NB, q * NB : (q + 1) * NB] = hot
        oht[NB : 2 * NB, q * NB : (q + 1) * NB] = hot

    pl.semaphore_wait(barrier, ND - 1 + 2)

    def halo_copies():
        up = pltpu.make_async_remote_copy(
            src_ref=hs.at[0], dst_ref=hr.at[1], send_sem=h_send.at[0], recv_sem=h_recv.at[1],
            device_id={"strip": north}, device_id_type=MESH)
        down = pltpu.make_async_remote_copy(
            src_ref=hs.at[1], dst_ref=hr.at[0], send_sem=h_send.at[1], recv_sem=h_recv.at[0],
            device_id={"strip": south}, device_id_type=MESH)
        return up, down

    def lines(z, x, y):
        return pl.ds(z * ZR + x * YR + y, 8, stride=ZR)

    def landed(t):
        load_c(t).wait()
        for x in range(NX):
            load_t(t, x).wait()

    def arrive(t):
        landed(t)

        def planes(i, c):
            for u in range(4):
                z = i * 4 + u
                for x in range(NX):
                    k_v[z, x, prows(t), :] = pick(cat_v[z, rows(t), x * 128 : (x + 1) * 128])
            return c

        lax.fori_loop(0, CZ // 4, planes, 0)

    arrive(NT - 1)
    for x in range(NX):
        for z in range(0, CZ, 8):
            hs[1, 0, x, z : z + 8, :] = t2[lines(z, x, PAD + CY - 1), :]
            hs[1, 1, x, z : z + 8, :] = k2[lines(z, x, PAD + CY - 1), :]
    halo_copies()[1].start()
    arrive(0)
    for x in range(NX):
        for z in range(0, CZ, 8):
            hs[0, 0, x, z : z + 8, :] = t2[lines(z, x, PAD), :]
            hs[0, 1, x, z : z + 8, :] = k2[lines(z, x, PAD), :]
    halo_copies()[0].start()

    who8 = iota((8, NB), 1)
    west, east = who8 == 0, who8 == 127

    def faces(t):
        def clamp(i):
            return jnp.clip(i, 0, CZ // GZ - 1)

        def at_of(i):
            base = pl.multiple_of(i * GZ * ZR + t * YT + PAD, YT)
            return [base + u * ZR + x * YR for u in range(GZ) for x in range(NX)]

        n = GZ * NX

        def step(i, c):
            i0, i1, i2 = clamp(i), clamp(i - 1), clamp(i - 2)
            at = at_of(i1)
            at2 = at_of(i2)
            fe2 = [fe_s[m] for m in range(n)]
            rf = [pltpu.roll(v, 1, 1) for v in fe2]
            tc = [t2[pl.ds(a, YT), :] for a in at]
            kc = [k2[pl.ds(a, YT), :] for a in at]
            rt = [pltpu.roll(v, 127, 1) for v in tc]
            rk = [pltpu.roll(v, 127, 1) for v in kc]
            ta = [t2[pl.ds(a - 1, YT), :] for a in at]
            ka = [k2[pl.ds(a - 1, YT), :] for a in at]
            for m in range(n):
                f2[pl.ds(at[m], YT), :] = (kc[m] + ka[m]) * (ta[m] - tc[m])
            for m in range(n):
                x = m % NX
                told = t2[pl.ds(at2[m], YT), :]
                edge = k2[pl.ds(at2[m], YT), :] * told if x == 0 else rf[m - 1]
                h_o[i2 * GZ + m // NX, rows(t), x * 128 : (x + 1) * 128] = (
                    told + (fe2[m] - jnp.where(west, edge, rf[m])))
            inner = lambda m: (m + 1) % NX != 0
            te = [jnp.where(east, rt[m + 1] if inner(m) else 0.0, rt[m]) for m in range(n)]
            ke = [jnp.where(east, rk[m + 1] if inner(m) else 0.0, rk[m]) for m in range(n)]
            for m in range(n):
                fe_s[m] = (kc[m] + ke[m]) * (te[m] - tc[m])
            for m in range(n):
                z, x = i0 * GZ + m // NX, m % NX
                k_v[z, x, prows(t), :] = pick(cat_v[z, rows(t), x * 128 : (x + 1) * 128])
            return c

        lax.fori_loop(0, CZ // GZ + 2, step, 0)

    def arrive_next(t, c):
        landed(t)
        faces(t)
        return c

    lax.fori_loop(1, NT - 1, arrive_next, 0)
    faces(NT - 1)

    def g_copy(j, source):
        return pltpu.make_async_remote_copy(
            src_ref=gs, dst_ref=ga.at[source], send_sem=g_send.at[j], recv_sem=g_recv.at[source],
            device_id={"depth": j}, device_id_type=MESH)

    def w_copy(j, source):
        return pltpu.make_async_remote_copy(
            src_ref=ws, dst_ref=wa.at[source], send_sem=w_send.at[j], recv_sem=w_recv.at[source],
            device_id={"depth": j}, device_id_type=MESH)

    def halo_in():
        up, down = halo_copies()
        up.wait()
        down.wait()
        has_north = (strip > 0).astype(F32)
        has_south = (strip < NS - 1).astype(F32)
        for x in range(NX):
            for z in range(0, CZ, 8):
                t2[lines(z, x, PAD - 1), :] = hr[0, 0, x, z : z + 8, :] * has_north
                k2[lines(z, x, PAD - 1), :] = hr[0, 1, x, z : z + 8, :] * has_north
                tb = hr[1, 0, x, z : z + 8, :] * has_south
                kb = hr[1, 1, x, z : z + 8, :] * has_south
                tc = t2[lines(z, x, PAD + CY - 1), :]
                kc = k2[lines(z, x, PAD + CY - 1), :]
                f2[lines(z, x, PAD + CY), :] = (kb + kc) * (tc - tb)

    sub8 = iota((8, NB), 0)

    def fetch(b, acc):
        p = pos_s[b]
        col = ((p >> 7) & 7) * YR + (p >> 10) + PAD
        shift = (b - p) & 127
        mine = who8 == b
        for m in range(8):
            ref = t2 if m < 4 else k2
            z0 = (m % 4) * 8
            got = ref[pl.ds(col + z0 * ZR, 8), :]
            for u in range(1, 8):
                got = jnp.where(sub8 == u, ref[pl.ds(col + (z0 + u) * ZR - u, 8), :], got)
            acc[m] = jnp.where(mine, pltpu.roll(got, shift, 1), acc[m])
        return acc

    def wells():
        def some(i, acc):
            acc = list(acc)
            for u in range(PER):
                acc = fetch(i * PER + u, acc)
            return tuple(acc)

        acc = lax.fori_loop(0, NB // PER, some, tuple(jnp.zeros((8, NB), F32) for _ in range(8)))
        for zg in range(4):
            part = slice(zg * 8, zg * 8 + 8)
            cond = 10.0 * acc[4 + zg]
            rate = speed_ref[...] * cond / (1.0 + cond)
            level = iota((8, NB), 0) + (me * CZ + zg * 8)
            rate_v[part, :] = jnp.where(level < reach_ref[...], rate, 0.0)
            rock_v[part, :] = acc[zg]
        prod = jnp.ones((1, NB), F32)
        add_d = jnp.zeros((1, NB), F32)
        add_r = jnp.zeros((1, NB), F32)
        for z in range(CZ):
            r = rate_v[z : z + 1, :]
            prod = prod * (1.0 - r)
            add_d = (1.0 - r) * add_d + r * rock_v[z : z + 1, :]
            y = CZ - 1 - z
            r = rate_v[y : y + 1, :]
            add_r = (1.0 - r) * add_r + r * rock_v[y : y + 1, :]
        gs[0:1, :] = prod
        gs[1:2, :] = add_d
        gs[2:3, :] = add_r
        last = CZ - 1
        gs[3:4, :] = jnp.broadcast_to(g_ref[0:1, 0:1], (1, NB))
        gs[4:5, :] = jnp.broadcast_to(g_ref[0:1, last:CZ], (1, NB))
        gs[5:6, :] = jnp.broadcast_to(g_ref[last:CZ, 0:1], (1, NB))
        gs[6:7, :] = jnp.broadcast_to(g_ref[last:CZ, last:CZ], (1, NB))
        gs[7:8, :] = jnp.full((1, NB), link_s[0], F32)
        ga[me] = gs[...]
        others(lambda j: g_copy(j, me).start())

    def a_copy(o, source):
        return pltpu.make_async_remote_copy(
            src_ref=fl.at[o], dst_ref=rx.at[source], send_sem=a_send.at[o],
            recv_sem=a_recv.at[source], device_id={"depth": o}, device_id_type=MESH)

    def sums(t):
        def planes(i, c):
            base = pl.multiple_of(i * 2 * ZR + t * YT + PAD, YT)
            at = [base + u * ZR + x * YR for u in range(2) for x in range(NX)]
            fu = [f2[pl.ds(a, YT), :] for a in at]
            fd = [f2[pl.ds(a + 1, YT), :] for a in at]
            d = [h_o[i * 2 + u, rows(t), x * 128 : (x + 1) * 128]
                 for u in range(2) for x in range(NX)]
            r = [d[m] + (fu[m] - fd[m]) for m in range(2 * NX)]
            low = pl.multiple_of(i * 16, 16)
            high = pl.multiple_of(256 + i * 16, 16)
            for x in range(NX):
                hi, lo = split(jnp.concatenate([r[x], r[NX + x]], axis=0))
                lanes = slice((x % 2) * 128, (x % 2) * 128 + 128)
                x2[x // 2, pl.ds(low, 16), lanes] = hi
                x2[x // 2, pl.ds(high, 16), lanes] = lo
            return c

        lax.fori_loop(0, CZ // 2, planes, 0)

    def block(t, n):
        xh, xl = x2[n, 0:256, :], x2[n, 256:512, :]
        res = dot(kcat[...], jnp.concatenate([xh, xl, xh], axis=0)).reshape(CZ, YT, 256)
        cols = slice(n * 256, n * 256 + 256)
        h_o[:, rows(t), cols] = res
        part = slice((n % 2) * 256, (n % 2) * 256 + 256)
        fl[2 * t + n // 2, 0, :, part] = res[0]
        fl[2 * t + n // 2, 1, :, part] = res[CZ - 1]

    halo_in()
    faces(0)
    wells()

    def work(i, c):
        t = ring(i)
        sums(t)
        for n in range(4):
            block(t, n)
        for half in range(2):
            o = 2 * t + half

            @pl.when(o == me)
            def _():
                rx[me] = fl[o]

            @pl.when(o != me)
            def _():
                a_copy(o, me).start()
        return c

    lax.fori_loop(0, NT, work, 0)

    others(lambda j: g_copy(j, j).wait())

    flow = inlet_ref[...]
    mine = jnp.zeros((1, NB), F32)
    for j in range(ND):
        mine = mine + flow * (me == j).astype(F32)
        flow = ga[j, 0:1, :] * flow + ga[j, 1:2, :]
    rising = jnp.zeros((1, NB), F32)
    for j in reversed(range(ND)):
        rising = rising + flow * (me == j).astype(F32)
        flow = ga[j, 0:1, :] * flow + ga[j, 2:3, :]
    for z in range(CZ):
        r = rate_v[z : z + 1, :]
        down_v[z : z + 1, :] = mine
        mine = (1.0 - r) * mine + r * rock_v[z : z + 1, :]
        y = CZ - 1 - z
        r = rate_v[y : y + 1, :]
        up_v[y : y + 1, :] = rising
        rising = (1.0 - r) * rising + r * rock_v[y : y + 1, :]
    ext = rate_v[...] * (2.0 * rock_v[...] - down_v[...] - up_v[...])
    wmat = -2.0 * dot(g, ext, HIGHEST)
    ws[0:1, :] = wmat[0:1, :]
    ws[1:2, :] = wmat[CZ - 1 : CZ, :]
    wa[me, 0:2, :] = ws[0:2, :]
    others(lambda j: w_copy(j, me).start())

    one = jnp.ones((1, NB), F32)
    zero = jnp.zeros((1, NB), F32)
    cs = [zero]
    for j in range(1, ND):
        cs.append(ga[j, 7:8, :] * (CZ / (CZ + 1.0)) / jnp.sqrt(ga[j - 1, 6:7, :] * ga[j, 3:4, :]))
    cs.append(zero)
    q = zero
    for j in range(ND):
        vf = cs[j] * ga[j, 3:4, :]
        vl = cs[j] * ga[j, 5:6, :]
        wf = cs[j + 1] * ga[j, 4:5, :]
        wl = cs[j + 1] * ga[j, 6:7, :]
        den = one - vf * q
        inv = one / den
        coef[j, 0:1, :] = vl * q * inv
        coef[j, 1:2, :] = vl * inv
        coef[j, 2:3, :] = inv
        coef[j, 3:4, :] = vf * inv
        coef[j, 4:5, :] = wf * inv
        coef[j, 5:6, :] = cs[j]
        coef[j, 6:7, :] = q
        coef[j, 7:8, :] = cs[j + 1]
        q = wl + vl * q * wf * inv

    def hot_rows(w, t):
        here = ((iota((YT, NB), 0) + t * YT) == ypos).astype(F32)
        hi, lo = split((w[:, None, :] * here[None, :, :]).reshape(w.shape[0] * YT, NB))
        return jnp.concatenate([hi, lo], axis=1)

    others(lambda j: w_copy(j, j).wait())
    lhs = hot_rows(wa[:, 0:2, :].reshape(2 * ND, NB), me >> 1)
    half = pl.ds(pl.multiple_of((me & 1) * HX, HX), HX)
    wells_part = dot(lhs, oht[:, half]).reshape(ND, 2, YT, HX)
    others(lambda j: a_copy(j, j).wait())
    rx[...] += wells_part

    for xs in range(HX // 128):
        cols = slice(xs * 128, (xs + 1) * 128)
        p = jnp.zeros((YT, 128), F32)
        ps = []
        for j in range(ND):
            ps.append(p)
            p = rx[j, 1, :, cols] + coef[j, 0:1, :] * rx[j, 0, :, cols] + coef[j, 1:2, :] * p
        a = jnp.zeros((YT, 128), F32)
        for j in reversed(range(ND)):
            tx[j, 1, :, cols] = coef[j, 7:8, :] * a
            a = coef[j, 2:3, :] * rx[j, 0, :, cols] + coef[j, 3:4, :] * ps[j] + coef[j, 4:5, :] * a
            tx[j, 0, :, cols] = coef[j, 5:6, :] * (ps[j] + coef[j, 6:7, :] * a)

    def block_of(o):
        return (slice(None), rows(o >> 1), pl.ds(pl.multiple_of((o & 1) * HX, HX), HX))

    def b_copy(j, source):
        return pltpu.make_async_remote_copy(
            src_ref=tx.at[j], dst_ref=pq_h.at[block_of(source)], send_sem=b_send.at[j],
            recv_sem=b_recv.at[source], device_id={"depth": j}, device_id_type=MESH)

    others(lambda j: b_copy(j, me).start())
    own = pltpu.make_async_copy(tx.at[me], pq_h.at[block_of(me)], own_sem)
    own.start()

    for b in range(NB // ND):
        leave_s[b] = jnp.sum(jnp.where(who8[0:1] == perm_s[me * (NB // ND) + b], flow, 0.0))

    def add_wells(t, c):
        lhs = hot_rows(wmat, t)
        for n in range(4):
            cols = slice(n * 256, n * 256 + 256)
            h_o[:, rows(t), cols] += dot(lhs, oht[:, cols]).reshape(CZ, YT, 256)
        return c

    lax.fori_loop(0, NT, add_wells, 0)
    own.wait()
    others(lambda j: b_copy(j, j).wait())


def fused(*args):
    dma = pltpu.SemaphoreType.DMA
    vm = lambda *s: pltpu.VMEM(s, F32)
    vb = lambda *s: pltpu.VMEM(s, BF16)
    any_ = pl.BlockSpec(memory_space=pl.ANY)
    smem = pl.BlockSpec(memory_space=pltpu.SMEM)
    vmem = pl.BlockSpec(memory_space=pltpu.VMEM)
    return pl.pallas_call(
        kernel,
        out_shape=(
            pltpu.VMEM((CZ, CY, CX), F32),
            pltpu.VMEM((2, CY, CX), F32),
            jax.ShapeDtypeStruct((NB // ND,), F32),
        ),
        in_specs=[any_, any_, smem, vmem, smem, smem, vmem, smem, vmem, vmem, vmem],
        out_specs=(vmem, vmem, smem),
        scratch_shapes=[
            vm(CZ, NX, YR, 128), vm(CZ, NX, YR, 128), vm(CZ, NX, YR, 128),
            pltpu.VMEM((CZ, CY, CX), jnp.int32), vb(4, 512, 256), vm(GZ * NX, YT, 128), vb(256, 768), vb(2 * NB, CX),
            vm(CZ, NB), vm(CZ, NB), vm(CZ, NB), vm(CZ, NB),
            vm(8, NB), vm(ND, 8, NB), vm(8, NB), vm(ND, 8, NB),
            vm(2, 2, NX, CZ, 128), vm(2, 2, NX, CZ, 128),
            vm(ND, 2, YT, HX), vm(ND, 2, YT, HX), vm(ND, 2, YT, HX),
            vm(ND, 8, NB),
            dma((NT, NX)), dma((NT,)), dma((2,)), dma((2,)),
            dma((ND,)), dma((ND,)), dma((ND,)), dma((ND,)),
            dma((ND,)), dma((ND,)), dma((ND,)), dma((ND,)), dma,
        ],
        compiler_params=pltpu.CompilerParams(
            collective_id=0, has_side_effects=True, vmem_limit_bytes=VMEM_LIMIT
        ),
    )(*args)


def finish_kernel(local, pq, g_s, out_h, ring, sem):
    def copy(i):
        slot = lax.rem(i, OS)
        return pltpu.make_async_copy(
            ring.at[slot], out_h.at[pl.ds(i * OZ, OZ)], sem.at[slot])

    def step(i, c):
        slot = lax.rem(i, OS)

        @pl.when(i >= OS)
        def _():
            copy(i - OS).wait()
        for u in range(OZ):
            z = i * OZ + u
            for y in range(0, CY, YT):
                rows = slice(y, y + YT)
                ring[slot, u, rows, :] = local[z, rows, :] + (
                    g_s[z, 0] * pq[0, rows, :] + g_s[z, CZ - 1] * pq[1, rows, :])
        copy(i).start()
        return c

    lax.fori_loop(0, CZ // OZ, step, 0)

    def drain(i, c):
        copy(i).wait()
        return c

    lax.fori_loop(CZ // OZ - OS, CZ // OZ, drain, 0)


def finish(local, pq, pivot):
    vmem = pl.BlockSpec(memory_space=pltpu.VMEM)
    return pl.pallas_call(
        finish_kernel,
        out_shape=jax.ShapeDtypeStruct((CZ, CY, CX), F32),
        in_specs=[vmem, vmem, pl.BlockSpec(memory_space=pltpu.SMEM)],
        out_specs=pl.BlockSpec(memory_space=pl.ANY),
        scratch_shapes=[pltpu.VMEM((OS, OZ, CY, CX), F32), pltpu.SemaphoreType.DMA((OS,))],
        compiler_params=pltpu.CompilerParams(vmem_limit_bytes=FINISH_LIMIT),
    )(local, pq, pivot)


def body(warmth, category, catalogue, pivot, linkage, position, holder, reach, entering, speed):
    row = lambda v: v.reshape(1, NB)
    local, pq, leaving = fused(
        warmth, category, catalogue, pivot, linkage, position, row(position), holder, row(reach),
        row(entering), row(speed),
    )
    return finish(local, pq, pivot), leaving


def solution(mesh):
    in_specs = (
        P("depth", "strip", None),
        P("depth", "strip", None),
        P(),
        P("depth", None),
        P("depth"),
        P("strip"),
        P("strip"),
        P("strip"),
        P("strip"),
        P("strip"),
    )
    out_specs = (P("depth", "strip", None), P(("strip", "depth")))
    return jax.shard_map(body, mesh=mesh, in_specs=in_specs, out_specs=out_specs, check_vma=False)
```

```python
import jax
import jax.numpy as jnp
from jax import lax
from jax.experimental import pallas as pl
from jax.experimental.pallas import tpu as pltpu
from jax.sharding import PartitionSpec as P

F32 = jnp.float32
BF16 = jnp.bfloat16
MESH = pl.DeviceIdType.MESH
HIGHEST = lax.Precision.HIGHEST

CZ, CY, CX = 32, 64, 1024
NB = 128
ND = 16
NS = 8
YT = 8
NT = CY // YT
HX = CX // 2
PAD = 8
NX = CX // 128
YR = CY + PAD
ZR = (NX + 1) * YR
GZ = 2
PER = 4
EARLY = 2
VMEM_LIMIT = 52 * 1024 * 1024
FINISH_LIMIT = 16 * 1024 * 1024
OZ = 2
OS = 4


def dot(a, b, precision=None):
    return lax.dot_general(
        a, b, (((1,), (0,)), ((), ())), precision=precision, preferred_element_type=F32
    )


def split(v):
    hi = v.astype(BF16)
    lo = (v - hi.astype(F32)).astype(BF16)
    return hi, lo


def iota(shape, dim):
    return lax.broadcasted_iota(jnp.int32, shape, dim)


def kernel(
    t_h, cat_h, table_s, g_ref, g_s, link_s, pos_s, pos_ref, perm_s, reach_ref, inlet_ref, speed_ref,
    h_o, pq_h, leave_s,
    t_v, k_v, f_v, cat_v, x2, fe_s, kcat, oht, rate_v, rock_v, p_v, d_v, q_v, u_v, w3,
    gs, ga, wr, hs, hr, fl, rx, tx, coef,
    in_t, in_c, h_send, h_recv, g_send, g_recv, a_send, a_recv, b_send, b_recv,
    own_sem,
):
    me = lax.axis_index("depth")
    strip = lax.axis_index("strip")
    north = lax.rem(strip + NS - 1, NS)
    south = lax.rem(strip + 1, NS)
    first = me >> 1
    t2 = t_v.reshape(CZ * ZR, 128)
    k2 = k_v.reshape(CZ * ZR, 128)
    f2 = f_v.reshape(CZ * ZR, 128)

    def rows(t):
        return pl.ds(pl.multiple_of(t * YT, YT), YT)

    def prows(t):
        return pl.ds(pl.multiple_of(t * YT + PAD, YT), YT)

    def load_c(t):
        return pltpu.make_async_copy(cat_h.at[:, rows(t), :], cat_v.at[:, rows(t), :], in_c.at[t])

    def load_t(t, x):
        return pltpu.make_async_copy(
            t_h.at[:, rows(t), x * 128 : (x + 1) * 128], t_v.at[:, x, prows(t), :], in_t.at[t, x])

    def load(t):
        load_c(t).start()
        for x in range(NX):
            load_t(t, x).start()

    def ring(i):
        return lax.rem(first + i, NT)

    load(NT - 1)
    load(0)

    def load_rest(t, c):
        load(t)
        return c

    lax.fori_loop(1, NT - 1, load_rest, 0)

    barrier = pltpu.get_barrier_semaphore()
    pl.semaphore_signal(barrier, inc=1, device_id={"strip": north}, device_id_type=MESH)
    pl.semaphore_signal(barrier, inc=1, device_id={"strip": south}, device_id_type=MESH)

    def others(fn):
        def step(i, c):
            fn(lax.rem(me + i, ND))
            return c
        lax.fori_loop(1, ND, step, 0)

    others(lambda j: pl.semaphore_signal(
        barrier, inc=1, device_id={"depth": j}, device_id_type=MESH))

    table = [table_s[i] * 0.1 for i in range(8)]
    level_of = jnp.zeros((8, 128), F32)
    for i in range(8):
        level_of = jnp.where(iota((8, 128), 0) == i, table[i], level_of)

    def pick(cat):
        return jnp.take_along_axis(level_of, cat, axis=0, mode="promise_in_bounds")

    g = g_ref[...]
    spread = ((iota((256, CZ), 0) >> 3) == iota((256, CZ), 1)).astype(F32)
    spread_t = ((iota((CZ, 256), 1) >> 3) == iota((CZ, 256), 0)).astype(F32)
    wide = dot(dot(spread, g, HIGHEST), spread_t, HIGHEST)
    wide = jnp.where((iota((256, 256), 0) & 7) == (iota((256, 256), 1) & 7), wide, 0.0)
    whi, wlo = split(wide)
    kcat[:, 0:256] = whi
    kcat[:, 256:512] = whi
    kcat[:, 512:768] = wlo
    pos = pos_ref[...]
    ypos = pos >> 10
    xcol = jnp.transpose(jnp.broadcast_to(pos & (CX - 1), (NB, NB)))
    for q in range(NX):
        hot = (iota((NB, NB), 1) + q * NB == xcol).astype(F32).astype(BF16)
        oht[0:NB, q * NB : (q + 1) * NB] = hot
        oht[NB : 2 * NB, q * NB : (q + 1) * NB] = hot

    pl.semaphore_wait(barrier, ND - 1 + 2)

    def halo_copies():
        up = pltpu.make_async_remote_copy(
            src_ref=hs.at[0], dst_ref=hr.at[1], send_sem=h_send.at[0], recv_sem=h_recv.at[1],
            device_id={"strip": north}, device_id_type=MESH)
        down = pltpu.make_async_remote_copy(
            src_ref=hs.at[1], dst_ref=hr.at[0], send_sem=h_send.at[1], recv_sem=h_recv.at[0],
            device_id={"strip": south}, device_id_type=MESH)
        return up, down

    def lines(z, x, y):
        return pl.ds(z * ZR + x * YR + y, 8, stride=ZR)

    def landed(t):
        load_c(t).wait()
        for x in range(NX):
            load_t(t, x).wait()

    def arrive(t):
        landed(t)

        def planes(i, c):
            for u in range(4):
                z = i * 4 + u
                for x in range(NX):
                    k_v[z, x, prows(t), :] = pick(cat_v[z, rows(t), x * 128 : (x + 1) * 128])
            return c

        lax.fori_loop(0, CZ // 4, planes, 0)

    arrive(NT - 1)
    for x in range(NX):
        for z in range(0, CZ, 8):
            hs[1, 0, x, z : z + 8, :] = t2[lines(z, x, PAD + CY - 1), :]
            hs[1, 1, x, z : z + 8, :] = k2[lines(z, x, PAD + CY - 1), :]
    halo_copies()[1].start()
    arrive(0)
    for x in range(NX):
        for z in range(0, CZ, 8):
            hs[0, 0, x, z : z + 8, :] = t2[lines(z, x, PAD), :]
            hs[0, 1, x, z : z + 8, :] = k2[lines(z, x, PAD), :]
    halo_copies()[0].start()

    who8 = iota((8, NB), 1)
    west, east = who8 == 0, who8 == 127

    def at_of(t, i):
        base = pl.multiple_of(i * GZ * ZR + t * YT + PAD, YT)
        return [base + u * ZR + x * YR for u in range(GZ) for x in range(NX)]

    n = GZ * NX

    def right_of(t, i):
        at = at_of(t, i)
        fu = [f2[pl.ds(a, YT), :] for a in at]
        fd = [f2[pl.ds(a + 1, YT), :] for a in at]
        d = [h_o[i * GZ + m // NX, rows(t), m % NX * 128 : (m % NX + 1) * 128] for m in range(n)]
        return [d[m] + (fu[m] - fd[m]) for m in range(n)]

    def weigh(t, i, acc):
        right = right_of(t, i)
        for u in range(GZ):
            g0 = g_s[0, i * GZ + u]
            g1 = g_s[CZ - 1, i * GZ + u]
            for x in range(NX):
                acc[x] = acc[x] + g0 * right[u * NX + x]
                acc[NX + x] = acc[NX + x] + g1 * right[u * NX + x]
        return acc

    zeros16 = tuple(jnp.zeros((YT, 128), F32) for _ in range(2 * NX))

    def a_copy(o, source):
        return pltpu.make_async_remote_copy(
            src_ref=fl.at[o], dst_ref=rx.at[source], send_sem=a_send.at[o],
            recv_sem=a_recv.at[source], device_id={"depth": o}, device_id_type=MESH)

    def hand_out(t, acc):
        for half in range(2):
            o = 2 * t + half
            for r in range(2):
                for x in range(4):
                    fl[o, r, :, x * 128 : (x + 1) * 128] = acc[r * NX + half * 4 + x]

            @pl.when(o == me)
            def _():
                rx[me] = fl[o]

            @pl.when(o != me)
            def _():
                a_copy(o, me).start()

    def faces(t, before):
        def clamp(i):
            return jnp.clip(i, 0, CZ // GZ - 1)

        def step(i, acc):
            i0, i1, i2 = clamp(i), clamp(i - 1), clamp(i - 2)
            at = at_of(t, i1)
            at2 = at_of(t, i2)
            fe2 = [fe_s[m] for m in range(n)]
            rf = [pltpu.roll(v, 1, 1) for v in fe2]
            tc = [t2[pl.ds(a, YT), :] for a in at]
            kc = [k2[pl.ds(a, YT), :] for a in at]
            rt = [pltpu.roll(v, 127, 1) for v in tc]
            rk = [pltpu.roll(v, 127, 1) for v in kc]
            start = i == 2
            acc = weigh(before, i2, [jnp.where(start, 0.0, v) for v in acc])
            ta = [t2[pl.ds(a - 1, YT), :] for a in at]
            ka = [k2[pl.ds(a - 1, YT), :] for a in at]
            for m in range(n):
                f2[pl.ds(at[m], YT), :] = (kc[m] + ka[m]) * (ta[m] - tc[m])
            for m in range(n):
                x = m % NX
                told = t2[pl.ds(at2[m], YT), :]
                edge = k2[pl.ds(at2[m], YT), :] * told if x == 0 else rf[m - 1]
                h_o[i2 * GZ + m // NX, rows(t), x * 128 : (x + 1) * 128] = (
                    told + (fe2[m] - jnp.where(west, edge, rf[m])))
            inner = lambda m: (m + 1) % NX != 0
            te = [jnp.where(east, rt[m + 1] if inner(m) else 0.0, rt[m]) for m in range(n)]
            ke = [jnp.where(east, rk[m + 1] if inner(m) else 0.0, rk[m]) for m in range(n)]
            for m in range(n):
                fe_s[m] = (kc[m] + ke[m]) * (te[m] - tc[m])
            for m in range(n):
                z, x = i0 * GZ + m // NX, m % NX
                k_v[z, x, prows(t), :] = pick(cat_v[z, rows(t), x * 128 : (x + 1) * 128])
            return tuple(acc)

        return lax.fori_loop(0, CZ // GZ + 2, step, zeros16)

    def arrive_next(t, c):
        landed(t)
        acc = faces(t, t - 1)

        @pl.when(t >= 2)
        def _():
            hand_out(t - 1, acc)
        return c

    lax.fori_loop(1, NT - 1, arrive_next, 0)

    def g_copy(j, source):
        return pltpu.make_async_remote_copy(
            src_ref=gs, dst_ref=ga.at[source], send_sem=g_send.at[j], recv_sem=g_recv.at[source],
            device_id={"depth": j}, device_id_type=MESH)

    def halo_in():
        up, down = halo_copies()
        up.wait()
        down.wait()
        has_north = (strip > 0).astype(F32)
        has_south = (strip < NS - 1).astype(F32)
        for x in range(NX):
            for z in range(0, CZ, 8):
                t2[lines(z, x, PAD - 1), :] = hr[0, 0, x, z : z + 8, :] * has_north
                k2[lines(z, x, PAD - 1), :] = hr[0, 1, x, z : z + 8, :] * has_north
                tb = hr[1, 0, x, z : z + 8, :] * has_south
                kb = hr[1, 1, x, z : z + 8, :] * has_south
                tc = t2[lines(z, x, PAD + CY - 1), :]
                kc = k2[lines(z, x, PAD + CY - 1), :]
                f2[lines(z, x, PAD + CY), :] = (kb + kc) * (tc - tb)

    sub8 = iota((8, NB), 0)

    def fetch(b, acc):
        p = pos_s[b]
        col = ((p >> 7) & 7) * YR + (p >> 10) + PAD
        shift = (b - p) & 127
        mine = who8 == b
        for m in range(8):
            ref = t2 if m < 4 else k2
            z0 = (m % 4) * 8
            got = ref[pl.ds(col + z0 * ZR, 8), :]
            for u in range(1, 8):
                got = jnp.where(sub8 == u, ref[pl.ds(col + (z0 + u) * ZR - u, 8), :], got)
            acc[m] = jnp.where(mine, pltpu.roll(got, shift, 1), acc[m])
        return acc

    def wells():
        def some(i, acc):
            acc = list(acc)
            for u in range(PER):
                acc = fetch(i * PER + u, acc)
            return tuple(acc)

        acc = lax.fori_loop(0, NB // PER, some, tuple(jnp.zeros((8, NB), F32) for _ in range(8)))
        for zg in range(4):
            part = slice(zg * 8, zg * 8 + 8)
            cond = 10.0 * acc[4 + zg]
            rate = speed_ref[...] * cond / (1.0 + cond)
            level = iota((8, NB), 0) + (me * CZ + zg * 8)
            rate_v[part, :] = jnp.where(level < reach_ref[...], rate, 0.0)
            rock_v[part, :] = acc[zg]
        prod = jnp.ones((1, NB), F32)
        add_d = jnp.zeros((1, NB), F32)
        back = jnp.ones((1, NB), F32)
        add_r = jnp.zeros((1, NB), F32)
        for z in range(CZ):
            p_v[z : z + 1, :] = prod
            d_v[z : z + 1, :] = add_d
            r = rate_v[z : z + 1, :]
            prod = prod * (1.0 - r)
            add_d = (1.0 - r) * add_d + r * rock_v[z : z + 1, :]
            y = CZ - 1 - z
            q_v[y : y + 1, :] = back
            u_v[y : y + 1, :] = add_r
            r = rate_v[y : y + 1, :]
            back = back * (1.0 - r)
            add_r = (1.0 - r) * add_r + r * rock_v[y : y + 1, :]
        rate = rate_v[...]
        w3[:, 0:NB] = 2.0 * rate * (d_v[...] + u_v[...] - 2.0 * rock_v[...])
        w3[:, NB : 2 * NB] = 2.0 * rate * p_v[...]
        w3[:, 2 * NB : 3 * NB] = 2.0 * rate * q_v[...]
        w3[...] = dot(g_ref[...], w3[...], HIGHEST)
        gs[0:1, :] = prod
        gs[1:2, :] = add_d
        gs[2:3, :] = add_r
        for m in range(3):
            gs[8 + m : 9 + m, :] = w3[0:1, m * NB : (m + 1) * NB]
            gs[11 + m : 12 + m, :] = w3[CZ - 1 : CZ, m * NB : (m + 1) * NB]
        gs[14:16, :] = jnp.zeros((2, NB), F32)
        last = CZ - 1
        gs[3:4, :] = jnp.broadcast_to(g_ref[0:1, 0:1], (1, NB))
        gs[4:5, :] = jnp.broadcast_to(g_ref[0:1, last:CZ], (1, NB))
        gs[5:6, :] = jnp.broadcast_to(g_ref[last:CZ, 0:1], (1, NB))
        gs[6:7, :] = jnp.broadcast_to(g_ref[last:CZ, last:CZ], (1, NB))
        gs[7:8, :] = jnp.full((1, NB), link_s[0], F32)
        ga[me] = gs[...]
        others(lambda j: g_copy(j, me).start())

    wells()
    halo_in()

    def last_two(i, c):
        t = jnp.where(i == 0, NT - 1, 0)
        before = jnp.where(i == 0, NT - 2, NT - 1)
        hand_out(before, faces(t, before))
        return c

    lax.fori_loop(0, 2, last_two, 0)
    hand_out(0, lax.fori_loop(
        0, CZ // GZ, lambda i, acc: tuple(weigh(0, i, list(acc))), zeros16))

    others(lambda j: g_copy(j, j).wait())

    flow = inlet_ref[...]
    downs = []
    for j in range(ND):
        downs.append(flow)
        flow = ga[j, 0:1, :] * flow + ga[j, 1:2, :]
    mine = jnp.zeros((1, NB), F32)
    rising = jnp.zeros((1, NB), F32)
    for j in reversed(range(ND)):
        own_block = (me == j).astype(F32)
        mine = mine + downs[j] * own_block
        rising = rising + flow * own_block
        for m in range(2):
            at = 8 + 3 * m
            wr[2 * j + m : 2 * j + m + 1, :] = (
                ga[j, at : at + 1, :] + ga[j, at + 1 : at + 2, :] * downs[j]
                + ga[j, at + 2 : at + 3, :] * flow)
        flow = ga[j, 0:1, :] * flow + ga[j, 2:3, :]
    wmat = w3[:, 0:NB] + w3[:, NB : 2 * NB] * mine + w3[:, 2 * NB : 3 * NB] * rising
    p_v[...] = wmat

    one = jnp.ones((1, NB), F32)
    zero = jnp.zeros((1, NB), F32)
    cs = [zero]
    for j in range(1, ND):
        cs.append(ga[j, 7:8, :] * (CZ / (CZ + 1.0)) / jnp.sqrt(ga[j - 1, 6:7, :] * ga[j, 3:4, :]))
    cs.append(zero)
    q = zero
    for j in range(ND):
        vf = cs[j] * ga[j, 3:4, :]
        vl = cs[j] * ga[j, 5:6, :]
        wf = cs[j + 1] * ga[j, 4:5, :]
        wl = cs[j + 1] * ga[j, 6:7, :]
        den = one - vf * q
        inv = one / den
        coef[j, 0:1, :] = vl * q * inv
        coef[j, 1:2, :] = vl * inv
        coef[j, 2:3, :] = inv
        coef[j, 3:4, :] = vf * inv
        coef[j, 4:5, :] = wf * inv
        coef[j, 5:6, :] = cs[j]
        coef[j, 6:7, :] = q
        coef[j, 7:8, :] = cs[j + 1]
        q = wl + vl * q * wf * inv

    def hot_rows(w, t):
        here = ((iota((YT, NB), 0) + t * YT) == ypos).astype(F32)
        hi, lo = split((w[:, None, :] * here[None, :, :]).reshape(w.shape[0] * YT, NB))
        return jnp.concatenate([hi, lo], axis=1)

    lhs = hot_rows(wr[...], me >> 1)
    half = pl.ds(pl.multiple_of((me & 1) * HX, HX), HX)
    wells_part = dot(lhs, oht[:, half]).reshape(ND, 2, YT, HX)

    def product(t, c):
        def planes(i, c2):
            r = right_of(t, i)
            low = pl.multiple_of(i * 16, 16)
            high = pl.multiple_of(256 + i * 16, 16)
            for x in range(NX):
                hi, lo = split(jnp.concatenate([r[x], r[NX + x]], axis=0))
                lanes = slice((x % 2) * 128, (x % 2) * 128 + 128)
                x2[x // 2, pl.ds(low, 16), lanes] = hi
                x2[x // 2, pl.ds(high, 16), lanes] = lo
            return c2

        lax.fori_loop(0, CZ // GZ, planes, 0)
        left = jnp.concatenate([kcat[...], hot_rows(p_v[...], t)], axis=1)
        for n in range(4):
            xh, xl = x2[n, 0:256, :], x2[n, 256:512, :]
            cols = slice(n * 256, n * 256 + 256)
            res = dot(left, jnp.concatenate([xh, xl, xh, oht[:, cols]], axis=0))
            h_o[:, rows(t), cols] = res.reshape(CZ, YT, 256)
        return c

    lax.fori_loop(0, EARLY, product, 0)
    others(lambda j: a_copy(j, j).wait())
    rx[...] += wells_part

    for xs in range(HX // 128):
        cols = slice(xs * 128, (xs + 1) * 128)
        p = jnp.zeros((YT, 128), F32)
        ps = []
        for j in range(ND):
            ps.append(p)
            p = rx[j, 1, :, cols] + coef[j, 0:1, :] * rx[j, 0, :, cols] + coef[j, 1:2, :] * p
        a = jnp.zeros((YT, 128), F32)
        for j in reversed(range(ND)):
            tx[j, 1, :, cols] = coef[j, 7:8, :] * a
            a = coef[j, 2:3, :] * rx[j, 0, :, cols] + coef[j, 3:4, :] * ps[j] + coef[j, 4:5, :] * a
            tx[j, 0, :, cols] = coef[j, 5:6, :] * (ps[j] + coef[j, 6:7, :] * a)

    def block_of(o):
        return (slice(None), rows(o >> 1), pl.ds(pl.multiple_of((o & 1) * HX, HX), HX))

    def b_copy(j, source):
        return pltpu.make_async_remote_copy(
            src_ref=tx.at[j], dst_ref=pq_h.at[block_of(source)], send_sem=b_send.at[j],
            recv_sem=b_recv.at[source], device_id={"depth": j}, device_id_type=MESH)

    others(lambda j: b_copy(j, me).start())
    own = pltpu.make_async_copy(tx.at[me], pq_h.at[block_of(me)], own_sem)
    own.start()

    for b in range(NB // ND):
        leave_s[b] = jnp.sum(jnp.where(who8[0:1] == perm_s[me * (NB // ND) + b], flow, 0.0))

    lax.fori_loop(EARLY, NT, product, 0)
    own.wait()
    others(lambda j: b_copy(j, j).wait())


def fused(*args):
    dma = pltpu.SemaphoreType.DMA
    vm = lambda *s: pltpu.VMEM(s, F32)
    vb = lambda *s: pltpu.VMEM(s, BF16)
    any_ = pl.BlockSpec(memory_space=pl.ANY)
    smem = pl.BlockSpec(memory_space=pltpu.SMEM)
    vmem = pl.BlockSpec(memory_space=pltpu.VMEM)
    return pl.pallas_call(
        kernel,
        out_shape=(
            pltpu.VMEM((CZ, CY, CX), F32),
            pltpu.VMEM((2, CY, CX), F32),
            jax.ShapeDtypeStruct((NB // ND,), F32),
        ),
        in_specs=[any_, any_, smem, vmem, smem, smem, smem, vmem, smem, vmem, vmem, vmem],
        out_specs=(vmem, vmem, smem),
        scratch_shapes=[
            vm(CZ, NX + 1, YR, 128), vm(CZ, NX + 1, YR, 128), vm(CZ, NX + 1, YR, 128),
            pltpu.VMEM((CZ, CY, CX), jnp.int32), vb(4, 512, 256), vm(GZ * NX, YT, 128), vb(256, 768), vb(2 * NB, CX),
            vm(CZ, NB), vm(CZ, NB), vm(CZ, NB), vm(CZ, NB), vm(CZ, NB), vm(CZ, NB), vm(CZ, 3 * NB),
            vm(16, NB), vm(ND, 16, NB), vm(2 * ND, NB),
            vm(2, 2, NX, CZ, 128), vm(2, 2, NX, CZ, 128),
            vm(ND, 2, YT, HX), vm(ND, 2, YT, HX), vm(ND, 2, YT, HX),
            vm(ND, 8, NB),
            dma((NT, NX)), dma((NT,)), dma((2,)), dma((2,)),
            dma((ND,)), dma((ND,)), dma((ND,)), dma((ND,)), dma((ND,)), dma((ND,)), dma,
        ],
        compiler_params=pltpu.CompilerParams(
            collective_id=0, has_side_effects=True, vmem_limit_bytes=VMEM_LIMIT
        ),
    )(*args)


def finish_kernel(local, pq, g_s, out_h, ring, sem):
    def copy(i):
        slot = lax.rem(i, OS)
        return pltpu.make_async_copy(
            ring.at[slot], out_h.at[pl.ds(i * OZ, OZ)], sem.at[slot])

    def step(i, c):
        slot = lax.rem(i, OS)

        @pl.when(i >= OS)
        def _():
            copy(i - OS).wait()
        for u in range(OZ):
            z = i * OZ + u
            for y in range(0, CY, YT):
                rows = slice(y, y + YT)
                ring[slot, u, rows, :] = local[z, rows, :] + (
                    g_s[z, 0] * pq[0, rows, :] + g_s[z, CZ - 1] * pq[1, rows, :])
        copy(i).start()
        return c

    lax.fori_loop(0, CZ // OZ, step, 0)

    def drain(i, c):
        copy(i).wait()
        return c

    lax.fori_loop(CZ // OZ - OS, CZ // OZ, drain, 0)


def finish(local, pq, pivot):
    vmem = pl.BlockSpec(memory_space=pltpu.VMEM)
    return pl.pallas_call(
        finish_kernel,
        out_shape=jax.ShapeDtypeStruct((CZ, CY, CX), F32),
        in_specs=[vmem, vmem, pl.BlockSpec(memory_space=pltpu.SMEM)],
        out_specs=pl.BlockSpec(memory_space=pl.ANY),
        scratch_shapes=[pltpu.VMEM((OS, OZ, CY, CX), F32), pltpu.SemaphoreType.DMA((OS,))],
        compiler_params=pltpu.CompilerParams(vmem_limit_bytes=FINISH_LIMIT),
    )(local, pq, pivot)


def body(warmth, category, catalogue, pivot, linkage, position, holder, reach, entering, speed):
    row = lambda v: v.reshape(1, NB)
    local, pq, leaving = fused(
        warmth, category, catalogue, pivot, pivot, linkage, position, row(position), holder, row(reach),
        row(entering), row(speed),
    )
    return finish(local, pq, pivot), leaving


def solution(mesh):
    in_specs = (
        P("depth", "strip", None),
        P("depth", "strip", None),
        P(),
        P("depth", None),
        P("depth"),
        P("strip"),
        P("strip"),
        P("strip"),
        P("strip"),
        P("strip"),
    )
    out_specs = (P("depth", "strip", None), P(("strip", "depth")))
    return jax.shard_map(body, mesh=mesh, in_specs=in_specs, out_specs=out_specs, check_vma=False)
```

```python
import jax
import jax.numpy as jnp
from jax import lax
from jax.experimental import pallas as pl
from jax.experimental.pallas import tpu as pltpu
from jax.sharding import PartitionSpec as P

F32 = jnp.float32
BF16 = jnp.bfloat16
MESH = pl.DeviceIdType.MESH
HIGHEST = lax.Precision.HIGHEST

CZ, CY, CX = 32, 64, 1024
NB = 128
ND = 16
NS = 8
YT = 8
NT = CY // YT
HX = CX // 2
PAD = 8
NX = CX // 128
YR = CY + PAD
ZR = (NX + 1) * YR
GZ = 2
PER = 4
EARLY = 2
VMEM_LIMIT = 52 * 1024 * 1024
FINISH_LIMIT = 16 * 1024 * 1024
OZ = 2
OS = 4


def dot(a, b, precision=None):
    return lax.dot_general(
        a, b, (((1,), (0,)), ((), ())), precision=precision, preferred_element_type=F32
    )


def split(v):
    hi = v.astype(BF16)
    lo = (v - hi.astype(F32)).astype(BF16)
    return hi, lo


def iota(shape, dim):
    return lax.broadcasted_iota(jnp.int32, shape, dim)


def kernel(
    t_h, cat_h, table_s, g_ref, g_s, link_s, pos_s, pos_ref, perm_s, reach_ref, inlet_ref, speed_ref,
    h_o, pq_o, leave_s,
    t_v, k_v, f_v, cat_v, x2, fe_s, kcat, oht, rate_v, rock_v, p_v, d_v, q_v, u_v, w3,
    gs, ga, wr, hs, hr, fl, rx, tx, coef,
    in_t, in_c, h_send, h_recv, g_send, g_recv, a_send, a_recv, b_send, b_recv,
):
    me = lax.axis_index("depth")
    strip = lax.axis_index("strip")
    north = lax.rem(strip + NS - 1, NS)
    south = lax.rem(strip + 1, NS)
    first = me >> 1
    t2 = t_v.reshape(CZ * ZR, 128)
    k2 = k_v.reshape(CZ * ZR, 128)
    f2 = f_v.reshape(CZ * ZR, 128)

    def rows(t):
        return pl.ds(pl.multiple_of(t * YT, YT), YT)

    def prows(t):
        return pl.ds(pl.multiple_of(t * YT + PAD, YT), YT)

    def load_c(t):
        return pltpu.make_async_copy(cat_h.at[:, rows(t), :], cat_v.at[:, rows(t), :], in_c.at[t])

    def load_t(t, x):
        return pltpu.make_async_copy(
            t_h.at[:, rows(t), x * 128 : (x + 1) * 128], t_v.at[:, x, prows(t), :], in_t.at[t, x])

    def load(t):
        load_c(t).start()
        for x in range(NX):
            load_t(t, x).start()

    def ring(i):
        return lax.rem(first + i, NT)

    load(NT - 1)
    load(0)

    def load_rest(t, c):
        load(t)
        return c

    lax.fori_loop(1, NT - 1, load_rest, 0)

    barrier = pltpu.get_barrier_semaphore()
    pl.semaphore_signal(barrier, inc=1, device_id={"strip": north}, device_id_type=MESH)
    pl.semaphore_signal(barrier, inc=1, device_id={"strip": south}, device_id_type=MESH)

    def others(fn):
        def step(i, c):
            fn(lax.rem(me + i, ND))
            return c
        lax.fori_loop(1, ND, step, 0)

    others(lambda j: pl.semaphore_signal(
        barrier, inc=1, device_id={"depth": j}, device_id_type=MESH))

    table = [table_s[i] * 0.1 for i in range(8)]
    level_of = jnp.zeros((8, 128), F32)
    for i in range(8):
        level_of = jnp.where(iota((8, 128), 0) == i, table[i], level_of)

    def pick(cat):
        return jnp.take_along_axis(level_of, cat, axis=0, mode="promise_in_bounds")

    g = g_ref[...]
    spread = ((iota((256, CZ), 0) >> 3) == iota((256, CZ), 1)).astype(F32)
    spread_t = ((iota((CZ, 256), 1) >> 3) == iota((CZ, 256), 0)).astype(F32)
    wide = dot(dot(spread, g, HIGHEST), spread_t, HIGHEST)
    wide = jnp.where((iota((256, 256), 0) & 7) == (iota((256, 256), 1) & 7), wide, 0.0)
    whi, wlo = split(wide)
    kcat[:, 0:256] = whi
    kcat[:, 256:512] = whi
    kcat[:, 512:768] = wlo
    pos = pos_ref[...]
    ypos = pos >> 10
    xcol = jnp.transpose(jnp.broadcast_to(pos & (CX - 1), (NB, NB)))
    for q in range(NX):
        hot = (iota((NB, NB), 1) + q * NB == xcol).astype(F32).astype(BF16)
        oht[0:NB, q * NB : (q + 1) * NB] = hot
        oht[NB : 2 * NB, q * NB : (q + 1) * NB] = hot

    pl.semaphore_wait(barrier, ND - 1 + 2)

    def halo_copies():
        up = pltpu.make_async_remote_copy(
            src_ref=hs.at[0], dst_ref=hr.at[1], send_sem=h_send.at[0], recv_sem=h_recv.at[1],
            device_id={"strip": north}, device_id_type=MESH)
        down = pltpu.make_async_remote_copy(
            src_ref=hs.at[1], dst_ref=hr.at[0], send_sem=h_send.at[1], recv_sem=h_recv.at[0],
            device_id={"strip": south}, device_id_type=MESH)
        return up, down

    def lines(z, x, y):
        return pl.ds(z * ZR + x * YR + y, 8, stride=ZR)

    def landed(t):
        load_c(t).wait()
        for x in range(NX):
            load_t(t, x).wait()

    def arrive(t):
        landed(t)

        def planes(i, c):
            for u in range(4):
                z = i * 4 + u
                for x in range(NX):
                    k_v[z, x, prows(t), :] = pick(cat_v[z, rows(t), x * 128 : (x + 1) * 128])
            return c

        lax.fori_loop(0, CZ // 4, planes, 0)

    arrive(NT - 1)
    for x in range(NX):
        for z in range(0, CZ, 8):
            hs[1, 0, x, z : z + 8, :] = t2[lines(z, x, PAD + CY - 1), :]
            hs[1, 1, x, z : z + 8, :] = k2[lines(z, x, PAD + CY - 1), :]
    halo_copies()[1].start()
    arrive(0)
    for x in range(NX):
        for z in range(0, CZ, 8):
            hs[0, 0, x, z : z + 8, :] = t2[lines(z, x, PAD), :]
            hs[0, 1, x, z : z + 8, :] = k2[lines(z, x, PAD), :]
    halo_copies()[0].start()

    who8 = iota((8, NB), 1)
    west, east = who8 == 0, who8 == 127

    def at_of(t, i):
        base = pl.multiple_of(i * GZ * ZR + t * YT + PAD, YT)
        return [base + u * ZR + x * YR for u in range(GZ) for x in range(NX)]

    n = GZ * NX

    def right_of(t, i):
        at = at_of(t, i)
        fu = [f2[pl.ds(a, YT), :] for a in at]
        fd = [f2[pl.ds(a + 1, YT), :] for a in at]
        d = [h_o[i * GZ + m // NX, rows(t), m % NX * 128 : (m % NX + 1) * 128] for m in range(n)]
        return [d[m] + (fu[m] - fd[m]) for m in range(n)]

    def weigh(t, i, acc):
        right = right_of(t, i)
        for u in range(GZ):
            g0 = g_s[0, i * GZ + u]
            g1 = g_s[CZ - 1, i * GZ + u]
            for x in range(NX):
                acc[x] = acc[x] + g0 * right[u * NX + x]
                acc[NX + x] = acc[NX + x] + g1 * right[u * NX + x]
        return acc

    zeros16 = tuple(jnp.zeros((YT, 128), F32) for _ in range(2 * NX))

    def turn_of(t):
        return ((t + NT - 1) & (NT - 1)) >> 1

    def a_copy(o, source, half):
        return pltpu.make_async_remote_copy(
            src_ref=fl.at[o, half], dst_ref=rx.at[source, half], send_sem=a_send.at[o, half],
            recv_sem=a_recv.at[source, half], device_id={"depth": o}, device_id_type=MESH)

    def hand_out(t, acc):
        turn = turn_of(t)
        half, place = turn >> 1, turn & 1
        for x in range(NX):
            for r in range(2):
                fl[2 * x + (t & 1), half, place, r] = acc[r * NX + x]

        @pl.when(place == 1)
        def _():
            def give(x, c):
                o = 2 * x + (t & 1)

                @pl.when(o == me)
                def _():
                    rx[me, half] = fl[o, half]

                @pl.when(o != me)
                def _():
                    a_copy(o, me, half).start()
                return c

            lax.fori_loop(0, NX, give, 0)

    def faces(t, before):
        def clamp(i):
            return jnp.clip(i, 0, CZ // GZ - 1)

        def step(i, acc):
            i0, i1, i2 = clamp(i), clamp(i - 1), clamp(i - 2)
            at = at_of(t, i1)
            at2 = at_of(t, i2)
            fe2 = [fe_s[m] for m in range(n)]
            rf = [pltpu.roll(v, 1, 1) for v in fe2]
            tc = [t2[pl.ds(a, YT), :] for a in at]
            kc = [k2[pl.ds(a, YT), :] for a in at]
            rt = [pltpu.roll(v, 127, 1) for v in tc]
            rk = [pltpu.roll(v, 127, 1) for v in kc]
            start = i == 2
            acc = weigh(before, i2, [jnp.where(start, 0.0, v) for v in acc])
            ta = [t2[pl.ds(a - 1, YT), :] for a in at]
            ka = [k2[pl.ds(a - 1, YT), :] for a in at]
            for m in range(n):
                f2[pl.ds(at[m], YT), :] = (kc[m] + ka[m]) * (ta[m] - tc[m])
            for m in range(n):
                x = m % NX
                told = t2[pl.ds(at2[m], YT), :]
                edge = k2[pl.ds(at2[m], YT), :] * told if x == 0 else rf[m - 1]
                h_o[i2 * GZ + m // NX, rows(t), x * 128 : (x + 1) * 128] = (
                    told + (fe2[m] - jnp.where(west, edge, rf[m])))
            inner = lambda m: (m + 1) % NX != 0
            te = [jnp.where(east, rt[m + 1] if inner(m) else 0.0, rt[m]) for m in range(n)]
            ke = [jnp.where(east, rk[m + 1] if inner(m) else 0.0, rk[m]) for m in range(n)]
            for m in range(n):
                fe_s[m] = (kc[m] + ke[m]) * (te[m] - tc[m])
            for m in range(n):
                z, x = i0 * GZ + m // NX, m % NX
                k_v[z, x, prows(t), :] = pick(cat_v[z, rows(t), x * 128 : (x + 1) * 128])
            return tuple(acc)

        return lax.fori_loop(0, CZ // GZ + 2, step, zeros16)

    def arrive_next(t, c):
        landed(t)
        acc = faces(t, t - 1)

        @pl.when(t >= 2)
        def _():
            hand_out(t - 1, acc)
        return c

    lax.fori_loop(1, NT - 1, arrive_next, 0)

    def g_copy(j, source):
        return pltpu.make_async_remote_copy(
            src_ref=gs, dst_ref=ga.at[source], send_sem=g_send.at[j], recv_sem=g_recv.at[source],
            device_id={"depth": j}, device_id_type=MESH)

    def halo_in():
        up, down = halo_copies()
        up.wait()
        down.wait()
        has_north = (strip > 0).astype(F32)
        has_south = (strip < NS - 1).astype(F32)
        for x in range(NX):
            for z in range(0, CZ, 8):
                t2[lines(z, x, PAD - 1), :] = hr[0, 0, x, z : z + 8, :] * has_north
                k2[lines(z, x, PAD - 1), :] = hr[0, 1, x, z : z + 8, :] * has_north
                tb = hr[1, 0, x, z : z + 8, :] * has_south
                kb = hr[1, 1, x, z : z + 8, :] * has_south
                tc = t2[lines(z, x, PAD + CY - 1), :]
                kc = k2[lines(z, x, PAD + CY - 1), :]
                f2[lines(z, x, PAD + CY), :] = (kb + kc) * (tc - tb)

    sub8 = iota((8, NB), 0)

    def fetch(b, acc):
        p = pos_s[b]
        col = ((p >> 7) & 7) * YR + (p >> 10) + PAD
        shift = (b - p) & 127
        mine = who8 == b
        for m in range(8):
            ref = t2 if m < 4 else k2
            z0 = (m % 4) * 8
            got = ref[pl.ds(col + z0 * ZR, 8), :]
            for u in range(1, 8):
                got = jnp.where(sub8 == u, ref[pl.ds(col + (z0 + u) * ZR - u, 8), :], got)
            acc[m] = jnp.where(mine, pltpu.roll(got, shift, 1), acc[m])
        return acc

    def wells():
        def some(i, acc):
            acc = list(acc)
            for u in range(PER):
                acc = fetch(i * PER + u, acc)
            return tuple(acc)

        acc = lax.fori_loop(0, NB // PER, some, tuple(jnp.zeros((8, NB), F32) for _ in range(8)))
        for zg in range(4):
            part = slice(zg * 8, zg * 8 + 8)
            cond = 10.0 * acc[4 + zg]
            rate = speed_ref[...] * cond / (1.0 + cond)
            level = iota((8, NB), 0) + (me * CZ + zg * 8)
            rate_v[part, :] = jnp.where(level < reach_ref[...], rate, 0.0)
            rock_v[part, :] = acc[zg]
        prod = jnp.ones((1, NB), F32)
        add_d = jnp.zeros((1, NB), F32)
        back = jnp.ones((1, NB), F32)
        add_r = jnp.zeros((1, NB), F32)
        for z in range(CZ):
            p_v[z : z + 1, :] = prod
            d_v[z : z + 1, :] = add_d
            r = rate_v[z : z + 1, :]
            prod = prod * (1.0 - r)
            add_d = (1.0 - r) * add_d + r * rock_v[z : z + 1, :]
            y = CZ - 1 - z
            q_v[y : y + 1, :] = back
            u_v[y : y + 1, :] = add_r
            r = rate_v[y : y + 1, :]
            back = back * (1.0 - r)
            add_r = (1.0 - r) * add_r + r * rock_v[y : y + 1, :]
        rate = rate_v[...]
        w3[:, 0:NB] = 2.0 * rate * (d_v[...] + u_v[...] - 2.0 * rock_v[...])
        w3[:, NB : 2 * NB] = 2.0 * rate * p_v[...]
        w3[:, 2 * NB : 3 * NB] = 2.0 * rate * q_v[...]
        w3[...] = dot(g_ref[...], w3[...], HIGHEST)
        gs[0:1, :] = prod
        gs[1:2, :] = add_d
        gs[2:3, :] = add_r
        for m in range(3):
            gs[8 + m : 9 + m, :] = w3[0:1, m * NB : (m + 1) * NB]
            gs[11 + m : 12 + m, :] = w3[CZ - 1 : CZ, m * NB : (m + 1) * NB]
        gs[14:16, :] = jnp.zeros((2, NB), F32)
        last = CZ - 1
        gs[3:4, :] = jnp.broadcast_to(g_ref[0:1, 0:1], (1, NB))
        gs[4:5, :] = jnp.broadcast_to(g_ref[0:1, last:CZ], (1, NB))
        gs[5:6, :] = jnp.broadcast_to(g_ref[last:CZ, 0:1], (1, NB))
        gs[6:7, :] = jnp.broadcast_to(g_ref[last:CZ, last:CZ], (1, NB))
        gs[7:8, :] = jnp.full((1, NB), link_s[0], F32)
        ga[me] = gs[...]
        others(lambda j: g_copy(j, me).start())

    wells()
    halo_in()

    def last_two(i, c):
        t = jnp.where(i == 0, NT - 1, 0)
        before = jnp.where(i == 0, NT - 2, NT - 1)
        hand_out(before, faces(t, before))
        return c

    lax.fori_loop(0, 2, last_two, 0)
    hand_out(0, lax.fori_loop(
        0, CZ // GZ, lambda i, acc: tuple(weigh(0, i, list(acc))), zeros16))

    others(lambda j: g_copy(j, j).wait())

    flow = inlet_ref[...]
    downs = []
    for j in range(ND):
        downs.append(flow)
        flow = ga[j, 0:1, :] * flow + ga[j, 1:2, :]
    mine = jnp.zeros((1, NB), F32)
    rising = jnp.zeros((1, NB), F32)
    for j in reversed(range(ND)):
        own_block = (me == j).astype(F32)
        mine = mine + downs[j] * own_block
        rising = rising + flow * own_block
        for m in range(2):
            at = 8 + 3 * m
            wr[2 * j + m : 2 * j + m + 1, :] = (
                ga[j, at : at + 1, :] + ga[j, at + 1 : at + 2, :] * downs[j]
                + ga[j, at + 2 : at + 3, :] * flow)
        flow = ga[j, 0:1, :] * flow + ga[j, 2:3, :]
    wmat = w3[:, 0:NB] + w3[:, NB : 2 * NB] * mine + w3[:, 2 * NB : 3 * NB] * rising
    p_v[...] = wmat

    one = jnp.ones((1, NB), F32)
    zero = jnp.zeros((1, NB), F32)
    cs = [zero]
    for j in range(1, ND):
        cs.append(ga[j, 7:8, :] * (CZ / (CZ + 1.0)) / jnp.sqrt(ga[j - 1, 6:7, :] * ga[j, 3:4, :]))
    cs.append(zero)
    q = zero
    for j in range(ND):
        vf = cs[j] * ga[j, 3:4, :]
        vl = cs[j] * ga[j, 5:6, :]
        wf = cs[j + 1] * ga[j, 4:5, :]
        wl = cs[j + 1] * ga[j, 6:7, :]
        den = one - vf * q
        inv = one / den
        coef[j, 0:1, :] = vl * q * inv
        coef[j, 1:2, :] = vl * inv
        coef[j, 2:3, :] = inv
        coef[j, 3:4, :] = vf * inv
        coef[j, 4:5, :] = wf * inv
        coef[j, 5:6, :] = cs[j]
        coef[j, 6:7, :] = q
        coef[j, 7:8, :] = cs[j + 1]
        q = wl + vl * q * wf * inv

    def hot_rows(w, t):
        here = ((iota((YT, NB), 0) + t * YT) == ypos).astype(F32)
        hi, lo = split((w[:, None, :] * here[None, :, :]).reshape(w.shape[0] * YT, NB))
        return jnp.concatenate([hi, lo], axis=1)

    strip_x = pl.ds(pl.multiple_of((me >> 1) * 128, 128), 128)

    def b_copy(j, source, half):
        return pltpu.make_async_remote_copy(
            src_ref=tx.at[j, half], dst_ref=pq_o.at[source, half], send_sem=b_send.at[j, half],
            recv_sem=b_recv.at[source, half], device_id={"depth": j}, device_id_type=MESH)

    def give_back(half):
        parts = []
        for k in range(2):
            t = (2 * (2 * half + k) + 2 - (me & 1)) & (NT - 1)
            parts.append(dot(hot_rows(wr[...], t), oht[:, strip_x]).reshape(ND, 2, YT, 128))
        others(lambda j: a_copy(j, j, half).wait())
        for k in range(2):
            part = parts[k]
            p = jnp.zeros((YT, 128), F32)
            ps, firsts = [], []
            for j in range(ND):
                ps.append(p)
                firsts.append(rx[j, half, k, 0] + part[j, 0])
                last_row = rx[j, half, k, 1] + part[j, 1]
                p = last_row + coef[j, 0:1, :] * firsts[j] + coef[j, 1:2, :] * p
            a = jnp.zeros((YT, 128), F32)
            for j in reversed(range(ND)):
                tx[j, half, k, 1] = coef[j, 7:8, :] * a
                a = coef[j, 2:3, :] * firsts[j] + coef[j, 3:4, :] * ps[j] + coef[j, 4:5, :] * a
                tx[j, half, k, 0] = coef[j, 5:6, :] * (ps[j] + coef[j, 6:7, :] * a)
        others(lambda j: b_copy(j, me, half).start())
        pq_o[me, half] = tx[me, half]

    def product(t, c):
        def planes(i, c2):
            r = right_of(t, i)
            low = pl.multiple_of(i * 16, 16)
            high = pl.multiple_of(256 + i * 16, 16)
            for x in range(NX):
                hi, lo = split(jnp.concatenate([r[x], r[NX + x]], axis=0))
                lanes = slice((x % 2) * 128, (x % 2) * 128 + 128)
                x2[x // 2, pl.ds(low, 16), lanes] = hi
                x2[x // 2, pl.ds(high, 16), lanes] = lo
            return c2

        lax.fori_loop(0, CZ // GZ, planes, 0)
        left = jnp.concatenate([kcat[...], hot_rows(p_v[...], t)], axis=1)
        for n in range(4):
            xh, xl = x2[n, 0:256, :], x2[n, 256:512, :]
            cols = slice(n * 256, n * 256 + 256)
            res = dot(left, jnp.concatenate([xh, xl, xh, oht[:, cols]], axis=0))
            h_o[:, rows(t), cols] = res.reshape(CZ, YT, 256)
        return c

    give_back(0)
    lax.fori_loop(0, EARLY, product, 0)
    give_back(1)

    for b in range(NB // ND):
        leave_s[b] = jnp.sum(jnp.where(who8[0:1] == perm_s[me * (NB // ND) + b], flow, 0.0))

    lax.fori_loop(EARLY, NT, product, 0)
    others(lambda j: b_copy(j, j, 0).wait())
    others(lambda j: b_copy(j, j, 1).wait())


def fused(*args):
    dma = pltpu.SemaphoreType.DMA
    vm = lambda *s: pltpu.VMEM(s, F32)
    vb = lambda *s: pltpu.VMEM(s, BF16)
    any_ = pl.BlockSpec(memory_space=pl.ANY)
    smem = pl.BlockSpec(memory_space=pltpu.SMEM)
    vmem = pl.BlockSpec(memory_space=pltpu.VMEM)
    return pl.pallas_call(
        kernel,
        out_shape=(
            pltpu.VMEM((CZ, CY, CX), F32),
            pltpu.VMEM((ND, 2, 2, 2, YT, 128), F32),
            jax.ShapeDtypeStruct((NB // ND,), F32),
        ),
        in_specs=[any_, any_, smem, vmem, smem, smem, smem, vmem, smem, vmem, vmem, vmem],
        out_specs=(vmem, vmem, smem),
        scratch_shapes=[
            vm(CZ, NX + 1, YR, 128), vm(CZ, NX + 1, YR, 128), vm(CZ, NX + 1, YR, 128),
            pltpu.VMEM((CZ, CY, CX), jnp.int32), vb(4, 512, 256), vm(GZ * NX, YT, 128), vb(256, 768), vb(2 * NB, CX),
            vm(CZ, NB), vm(CZ, NB), vm(CZ, NB), vm(CZ, NB), vm(CZ, NB), vm(CZ, NB), vm(CZ, 3 * NB),
            vm(16, NB), vm(ND, 16, NB), vm(2 * ND, NB),
            vm(2, 2, NX, CZ, 128), vm(2, 2, NX, CZ, 128),
            vm(ND, 2, 2, 2, YT, 128), vm(ND, 2, 2, 2, YT, 128), vm(ND, 2, 2, 2, YT, 128),
            vm(ND, 8, NB),
            dma((NT, NX)), dma((NT,)), dma((2,)), dma((2,)),
            dma((ND,)), dma((ND,)), dma((ND, 2)), dma((ND, 2)), dma((ND, 2)), dma((ND, 2)),
        ],
        compiler_params=pltpu.CompilerParams(
            collective_id=0, has_side_effects=True, vmem_limit_bytes=VMEM_LIMIT
        ),
    )(*args)


def finish_kernel(local, pq, g_s, out_h, ring, sem):
    def copy(i):
        slot = lax.rem(i, OS)
        return pltpu.make_async_copy(
            ring.at[slot], out_h.at[pl.ds(i * OZ, OZ)], sem.at[slot])

    def step(i, c):
        slot = lax.rem(i, OS)

        @pl.when(i >= OS)
        def _():
            copy(i - OS).wait()
        for u in range(OZ):
            z = i * OZ + u
            for y in range(0, CY, YT):
                rows = slice(y, y + YT)
                t = y // YT
                turn = (t + NT - 1) % NT // 2
                for x in range(NX):
                    cols = slice(x * 128, x * 128 + 128)
                    from_o = pq.at[2 * x + t % 2, turn // 2, turn % 2]
                    ring[slot, u, rows, cols] = local[z, rows, cols] + (
                        g_s[z, 0] * from_o[0] + g_s[z, CZ - 1] * from_o[1])
        copy(i).start()
        return c

    lax.fori_loop(0, CZ // OZ, step, 0)

    def drain(i, c):
        copy(i).wait()
        return c

    lax.fori_loop(CZ // OZ - OS, CZ // OZ, drain, 0)


def finish(local, pq, pivot):
    vmem = pl.BlockSpec(memory_space=pltpu.VMEM)
    return pl.pallas_call(
        finish_kernel,
        out_shape=jax.ShapeDtypeStruct((CZ, CY, CX), F32),
        in_specs=[vmem, vmem, pl.BlockSpec(memory_space=pltpu.SMEM)],
        out_specs=pl.BlockSpec(memory_space=pl.ANY),
        scratch_shapes=[pltpu.VMEM((OS, OZ, CY, CX), F32), pltpu.SemaphoreType.DMA((OS,))],
        compiler_params=pltpu.CompilerParams(vmem_limit_bytes=FINISH_LIMIT),
    )(local, pq, pivot)


def body(warmth, category, catalogue, pivot, linkage, position, holder, reach, entering, speed):
    row = lambda v: v.reshape(1, NB)
    local, pq, leaving = fused(
        warmth, category, catalogue, pivot, pivot, linkage, position, row(position), holder, row(reach),
        row(entering), row(speed),
    )
    return finish(local, pq, pivot), leaving


def solution(mesh):
    in_specs = (
        P("depth", "strip", None),
        P("depth", "strip", None),
        P(),
        P("depth", None),
        P("depth"),
        P("strip"),
        P("strip"),
        P("strip"),
        P("strip"),
        P("strip"),
    )
    out_specs = (P("depth", "strip", None), P(("strip", "depth")))
    return jax.shard_map(body, mesh=mesh, in_specs=in_specs, out_specs=out_specs, check_vma=False)
```

```python
import jax
import jax.numpy as jnp
from jax import lax
from jax.experimental import pallas as pl
from jax.experimental.pallas import tpu as pltpu
from jax.sharding import PartitionSpec as P

F32 = jnp.float32
BF16 = jnp.bfloat16
MESH = pl.DeviceIdType.MESH
HIGHEST = lax.Precision.HIGHEST

CZ, CY, CX = 32, 64, 1024
NB = 128
ND = 16
NS = 8
YT = 8
NT = CY // YT
HX = CX // 2
PAD = 8
NX = CX // 128
YR = CY + PAD
ZR = (NX + 1) * YR
GZ = 2
NG = CZ // GZ
PER = 16
EARLY = 5
VMEM_LIMIT = 52 * 1024 * 1024
FINISH_LIMIT = 16 * 1024 * 1024
OZ = 2
OS = 4


def dot(a, b, precision=None):
    return lax.dot_general(
        a, b, (((1,), (0,)), ((), ())), precision=precision, preferred_element_type=F32
    )


def split(v):
    hi = v.astype(BF16)
    lo = (v - hi.astype(F32)).astype(BF16)
    return hi, lo


def iota(shape, dim):
    return lax.broadcasted_iota(jnp.int32, shape, dim)


def kernel(
    t_h, cat_h, table_s, g_ref, g_s, link_s, pos_s, pos_ref, perm_s, reach_ref, inlet_ref, speed_ref,
    h_o, pq_o, leave_s,
    t_v, k_v, f_v, cat_v, fe_s, kcat, oht, rate_v, rock_v, p_v, d_v, q_v, u_v, w3,
    gs, ga, wr, hs, hr, fl, rx, tx, coef,
    in_t, in_c, h_send, h_recv, g_send, g_recv, a_send, a_recv, b_send, b_recv,
):
    me = lax.axis_index("depth")
    strip = lax.axis_index("strip")
    north = lax.rem(strip + NS - 1, NS)
    south = lax.rem(strip + 1, NS)
    first = me >> 1
    t2 = t_v.reshape(CZ * ZR, 128)
    k2 = k_v.reshape(CZ * ZR, 128)
    f2 = f_v.reshape(CZ * ZR, 128)

    def rows(t):
        return pl.ds(pl.multiple_of(t * YT, YT), YT)

    def prows(t):
        return pl.ds(pl.multiple_of(t * YT + PAD, YT), YT)

    def load_c(t):
        return pltpu.make_async_copy(cat_h.at[:, rows(t), :], cat_v.at[:, rows(t), :], in_c.at[t])

    def load_t(t, x):
        return pltpu.make_async_copy(
            t_h.at[:, rows(t), x * 128 : (x + 1) * 128], t_v.at[:, x, prows(t), :], in_t.at[t, x])

    def load(t):
        load_c(t).start()
        for x in range(NX):
            load_t(t, x).start()

    def ring(i):
        return lax.rem(first + i, NT)

    load(NT - 1)
    load(0)

    def load_rest(t, c):
        load(t)
        return c

    lax.fori_loop(1, NT - 1, load_rest, 0)

    barrier = pltpu.get_barrier_semaphore()
    pl.semaphore_signal(barrier, inc=1, device_id={"strip": north}, device_id_type=MESH)
    pl.semaphore_signal(barrier, inc=1, device_id={"strip": south}, device_id_type=MESH)

    def others(fn):
        def step(i, c):
            fn(lax.rem(me + i, ND))
            return c
        lax.fori_loop(1, ND, step, 0)

    others(lambda j: pl.semaphore_signal(
        barrier, inc=1, device_id={"depth": j}, device_id_type=MESH))

    table = [table_s[i] * 0.1 for i in range(8)]
    level_of = jnp.zeros((8, 128), F32)
    for i in range(8):
        level_of = jnp.where(iota((8, 128), 0) == i, table[i], level_of)

    def pick(cat):
        return jnp.take_along_axis(level_of, cat, axis=0, mode="promise_in_bounds")

    g = g_ref[...]
    spread = ((iota((256, CZ), 0) >> 3) == iota((256, CZ), 1)).astype(F32)
    spread_t = ((iota((CZ, 256), 1) >> 3) == iota((CZ, 256), 0)).astype(F32)
    wide = dot(dot(spread, g, HIGHEST), spread_t, HIGHEST)
    wide = jnp.where((iota((256, 256), 0) & 7) == (iota((256, 256), 1) & 7), wide, 0.0)
    whi, wlo = split(wide)
    kcat[:, 0:256] = whi
    kcat[:, 256:512] = whi
    kcat[:, 512:768] = wlo
    pos = pos_ref[...]
    ypos = pos >> 10
    xcol = jnp.transpose(jnp.broadcast_to(pos & (CX - 1), (NB, NB)))
    for q in range(NX):
        hot = (iota((NB, NB), 1) + q * NB == xcol).astype(F32).astype(BF16)
        oht[0:NB, q * NB : (q + 1) * NB] = hot
        oht[NB : 2 * NB, q * NB : (q + 1) * NB] = hot

    pl.semaphore_wait(barrier, ND - 1 + 2)

    def halo_copies():
        up = pltpu.make_async_remote_copy(
            src_ref=hs.at[0], dst_ref=hr.at[1], send_sem=h_send.at[0], recv_sem=h_recv.at[1],
            device_id={"strip": north}, device_id_type=MESH)
        down = pltpu.make_async_remote_copy(
            src_ref=hs.at[1], dst_ref=hr.at[0], send_sem=h_send.at[1], recv_sem=h_recv.at[0],
            device_id={"strip": south}, device_id_type=MESH)
        return up, down

    def lines(z, x, y):
        return pl.ds(z * ZR + x * YR + y, 8, stride=ZR)

    def landed(t):
        load_c(t).wait()
        for x in range(NX):
            load_t(t, x).wait()

    def arrive(t):
        landed(t)

        def planes(i, c):
            for u in range(4):
                z = i * 4 + u
                for x in range(NX):
                    k_v[z, x, prows(t), :] = pick(cat_v[z, rows(t), x * 128 : (x + 1) * 128])
            return c

        lax.fori_loop(0, CZ // 4, planes, 0)

    arrive(NT - 1)
    for x in range(NX):
        for z in range(0, CZ, 8):
            hs[1, 0, x, z : z + 8, :] = t2[lines(z, x, PAD + CY - 1), :]
            hs[1, 1, x, z : z + 8, :] = k2[lines(z, x, PAD + CY - 1), :]
    halo_copies()[1].start()
    arrive(0)
    for x in range(NX):
        for z in range(0, CZ, 8):
            hs[0, 0, x, z : z + 8, :] = t2[lines(z, x, PAD), :]
            hs[0, 1, x, z : z + 8, :] = k2[lines(z, x, PAD), :]
    halo_copies()[0].start()

    who8 = iota((8, NB), 1)
    west, east = who8 == 0, who8 == 127

    def at_of(t, i):
        base = pl.multiple_of(i * GZ * ZR + t * YT + PAD, YT)
        return [base + u * ZR + x * YR for u in range(GZ) for x in range(NX)]

    n = GZ * NX

    def right_of(t, i):
        at = at_of(t, i)
        fu = [f2[pl.ds(a, YT), :] for a in at]
        fd = [f2[pl.ds(a + 1, YT), :] for a in at]
        d = [h_o[i * GZ + m // NX, rows(t), m % NX * 128 : (m % NX + 1) * 128] for m in range(n)]
        return [d[m] + (fu[m] - fd[m]) for m in range(n)]

    def weigh(t, i, acc):
        right = right_of(t, i)
        for u in range(GZ):
            g0 = g_s[0, i * GZ + u]
            g1 = g_s[CZ - 1, i * GZ + u]
            for x in range(NX):
                acc[x] = acc[x] + g0 * right[u * NX + x]
                acc[NX + x] = acc[NX + x] + g1 * right[u * NX + x]
        return acc

    zeros16 = tuple(jnp.zeros((YT, 128), F32) for _ in range(2 * NX))

    def turn_of(t):
        return ((t + NT - 1) & (NT - 1)) >> 1

    def a_copy(o, source, half):
        return pltpu.make_async_remote_copy(
            src_ref=fl.at[o, half], dst_ref=rx.at[source, half], send_sem=a_send.at[o, half],
            recv_sem=a_recv.at[source, half], device_id={"depth": o}, device_id_type=MESH)

    def hand_out(t, acc):
        turn = turn_of(t)
        half, place = turn >> 1, turn & 1
        for x in range(NX):
            for r in range(2):
                fl[2 * x + (t & 1), half, place, r] = acc[r * NX + x]

        @pl.when(place == 1)
        def _():
            def give(x, c):
                o = 2 * x + (t & 1)

                @pl.when(o == me)
                def _():
                    rx[me, half] = fl[o, half]

                @pl.when(o != me)
                def _():
                    a_copy(o, me, half).start()
                return c

            lax.fori_loop(0, NX, give, 0)

    def weigh_tile(t):
        hand_out(t, lax.fori_loop(
            0, NG, lambda i, acc: tuple(weigh(t, i, list(acc))), zeros16))

    def faces(tile_at, count, loads):
        total = count * NG

        def step(i, c):
            where = []
            for lag in range(3):
                g = jnp.clip(i - lag, 0, total - 1)
                where.append((tile_at(g >> 4), g & (NG - 1)))
            (ta0, i0), (ta1, i1), (ta2, i2) = where
            if loads:
                @pl.when(jnp.logical_and(i0 == 0, i < total))
                def _():
                    landed(ta0)
            at = at_of(ta1, i1)
            at2 = at_of(ta2, i2)
            fe2 = [fe_s[m] for m in range(n)]
            rf = [pltpu.roll(v, 1, 1) for v in fe2]
            tc = [t2[pl.ds(a, YT), :] for a in at]
            kc = [k2[pl.ds(a, YT), :] for a in at]
            rt = [pltpu.roll(v, 127, 1) for v in tc]
            rk = [pltpu.roll(v, 127, 1) for v in kc]
            ta = [t2[pl.ds(a - 1, YT), :] for a in at]
            ka = [k2[pl.ds(a - 1, YT), :] for a in at]
            for m in range(n):
                f2[pl.ds(at[m], YT), :] = (kc[m] + ka[m]) * (ta[m] - tc[m])
            for m in range(n):
                x = m % NX
                told = t2[pl.ds(at2[m], YT), :]
                edge = k2[pl.ds(at2[m], YT), :] * told if x == 0 else rf[m - 1]
                h_o[i2 * GZ + m // NX, rows(ta2), x * 128 : (x + 1) * 128] = (
                    told + (fe2[m] - jnp.where(west, edge, rf[m])))
            inner = lambda m: (m + 1) % NX != 0
            te = [jnp.where(east, rt[m + 1] if inner(m) else 0.0, rt[m]) for m in range(n)]
            ke = [jnp.where(east, rk[m + 1] if inner(m) else 0.0, rk[m]) for m in range(n)]
            for m in range(n):
                fe_s[m] = (kc[m] + ke[m]) * (te[m] - tc[m])
            for m in range(n):
                z, x = i0 * GZ + m // NX, m % NX
                k_v[z, x, prows(ta0), :] = pick(cat_v[z, rows(ta0), x * 128 : (x + 1) * 128])

            done = jnp.logical_and(i2 == NG - 1, i >= 2)
            if loads:
                done = jnp.logical_and(done, ta2 >= 2)

            @pl.when(done)
            def _():
                weigh_tile((ta2 + NT - 1) & (NT - 1))
            return c

        lax.fori_loop(0, total + 2, step, 0)

    faces(lambda k: 1 + k, NT - 2, True)

    def g_copy(j, source):
        return pltpu.make_async_remote_copy(
            src_ref=gs, dst_ref=ga.at[source], send_sem=g_send.at[j], recv_sem=g_recv.at[source],
            device_id={"depth": j}, device_id_type=MESH)

    def halo_in():
        up, down = halo_copies()
        up.wait()
        down.wait()
        has_north = (strip > 0).astype(F32)
        has_south = (strip < NS - 1).astype(F32)
        for x in range(NX):
            for z in range(0, CZ, 8):
                t2[lines(z, x, PAD - 1), :] = hr[0, 0, x, z : z + 8, :] * has_north
                k2[lines(z, x, PAD - 1), :] = hr[0, 1, x, z : z + 8, :] * has_north
                tb = hr[1, 0, x, z : z + 8, :] * has_south
                kb = hr[1, 1, x, z : z + 8, :] * has_south
                tc = t2[lines(z, x, PAD + CY - 1), :]
                kc = k2[lines(z, x, PAD + CY - 1), :]
                f2[lines(z, x, PAD + CY), :] = (kb + kc) * (tc - tb)

    sub8 = iota((8, NB), 0)

    def fetch(b, acc):
        p = pos_s[b]
        col = ((p >> 7) & 7) * YR + (p >> 10) + PAD
        shift = (b - p) & 127
        mine = who8 == b
        for m in range(8):
            ref = t2 if m < 4 else k2
            z0 = (m % 4) * 8
            got = ref[pl.ds(col + z0 * ZR, 8), :]
            for u in range(1, 8):
                got = jnp.where(sub8 == u, ref[pl.ds(col + (z0 + u) * ZR - u, 8), :], got)
            acc[m] = jnp.where(mine, pltpu.roll(got, shift, 1), acc[m])
        return acc

    def wells():
        def some(i, acc):
            acc = list(acc)
            for u in range(PER):
                acc = fetch(i * PER + u, acc)
            return tuple(acc)

        acc = lax.fori_loop(0, NB // PER, some, tuple(jnp.zeros((8, NB), F32) for _ in range(8)))
        for zg in range(4):
            part = slice(zg * 8, zg * 8 + 8)
            cond = 10.0 * acc[4 + zg]
            rate = speed_ref[...] * cond / (1.0 + cond)
            level = iota((8, NB), 0) + (me * CZ + zg * 8)
            rate_v[part, :] = jnp.where(level < reach_ref[...], rate, 0.0)
            rock_v[part, :] = acc[zg]
        prod = jnp.ones((1, NB), F32)
        add_d = jnp.zeros((1, NB), F32)
        back = jnp.ones((1, NB), F32)
        add_r = jnp.zeros((1, NB), F32)
        for z in range(CZ):
            p_v[z : z + 1, :] = prod
            d_v[z : z + 1, :] = add_d
            r = rate_v[z : z + 1, :]
            prod = prod * (1.0 - r)
            add_d = (1.0 - r) * add_d + r * rock_v[z : z + 1, :]
            y = CZ - 1 - z
            q_v[y : y + 1, :] = back
            u_v[y : y + 1, :] = add_r
            r = rate_v[y : y + 1, :]
            back = back * (1.0 - r)
            add_r = (1.0 - r) * add_r + r * rock_v[y : y + 1, :]
        rate = rate_v[...]
        w3[:, 0:NB] = 2.0 * rate * (d_v[...] + u_v[...] - 2.0 * rock_v[...])
        w3[:, NB : 2 * NB] = 2.0 * rate * p_v[...]
        w3[:, 2 * NB : 3 * NB] = 2.0 * rate * q_v[...]
        w3[...] = dot(g_ref[...], w3[...], HIGHEST)
        gs[0:1, :] = prod
        gs[1:2, :] = add_d
        gs[2:3, :] = add_r
        for m in range(3):
            gs[8 + m : 9 + m, :] = w3[0:1, m * NB : (m + 1) * NB]
            gs[11 + m : 12 + m, :] = w3[CZ - 1 : CZ, m * NB : (m + 1) * NB]
        gs[14:16, :] = jnp.zeros((2, NB), F32)
        last = CZ - 1
        gs[3:4, :] = jnp.broadcast_to(g_ref[0:1, 0:1], (1, NB))
        gs[4:5, :] = jnp.broadcast_to(g_ref[0:1, last:CZ], (1, NB))
        gs[5:6, :] = jnp.broadcast_to(g_ref[last:CZ, 0:1], (1, NB))
        gs[6:7, :] = jnp.broadcast_to(g_ref[last:CZ, last:CZ], (1, NB))
        gs[7:8, :] = jnp.full((1, NB), link_s[0], F32)
        ga[me] = gs[...]
        others(lambda j: g_copy(j, me).start())

    wells()
    halo_in()

    faces(lambda k: (NT - 1 + k) & (NT - 1), 2, False)
    weigh_tile(0)

    others(lambda j: g_copy(j, j).wait())

    flow = inlet_ref[...]
    downs = []
    for j in range(ND):
        downs.append(flow)
        flow = ga[j, 0:1, :] * flow + ga[j, 1:2, :]
    mine = jnp.zeros((1, NB), F32)
    rising = jnp.zeros((1, NB), F32)
    for j in reversed(range(ND)):
        own_block = (me == j).astype(F32)
        mine = mine + downs[j] * own_block
        rising = rising + flow * own_block
        for m in range(2):
            at = 8 + 3 * m
            wr[2 * j + m : 2 * j + m + 1, :] = (
                ga[j, at : at + 1, :] + ga[j, at + 1 : at + 2, :] * downs[j]
                + ga[j, at + 2 : at + 3, :] * flow)
        flow = ga[j, 0:1, :] * flow + ga[j, 2:3, :]
    wmat = w3[:, 0:NB] + w3[:, NB : 2 * NB] * mine + w3[:, 2 * NB : 3 * NB] * rising
    p_v[...] = wmat

    one = jnp.ones((1, NB), F32)
    zero = jnp.zeros((1, NB), F32)
    cs = [zero]
    for j in range(1, ND):
        cs.append(ga[j, 7:8, :] * (CZ / (CZ + 1.0)) / jnp.sqrt(ga[j - 1, 6:7, :] * ga[j, 3:4, :]))
    cs.append(zero)
    q = zero
    for j in range(ND):
        vf = cs[j] * ga[j, 3:4, :]
        vl = cs[j] * ga[j, 5:6, :]
        wf = cs[j + 1] * ga[j, 4:5, :]
        wl = cs[j + 1] * ga[j, 6:7, :]
        den = one - vf * q
        inv = one / den
        coef[j, 0:1, :] = vl * q * inv
        coef[j, 1:2, :] = vl * inv
        coef[j, 2:3, :] = inv
        coef[j, 3:4, :] = vf * inv
        coef[j, 4:5, :] = wf * inv
        coef[j, 5:6, :] = cs[j]
        coef[j, 6:7, :] = q
        coef[j, 7:8, :] = cs[j + 1]
        q = wl + vl * q * wf * inv

    def hot_rows(w, t):
        here = ((iota((YT, NB), 0) + t * YT) == ypos).astype(F32)
        hi, lo = split((w[:, None, :] * here[None, :, :]).reshape(w.shape[0] * YT, NB))
        return jnp.concatenate([hi, lo], axis=1)

    strip_x = pl.ds(pl.multiple_of((me >> 1) * 128, 128), 128)

    def b_copy(j, source, half):
        return pltpu.make_async_remote_copy(
            src_ref=tx.at[j, half], dst_ref=pq_o.at[source, half], send_sem=b_send.at[j, half],
            recv_sem=b_recv.at[source, half], device_id={"depth": j}, device_id_type=MESH)

    def give_back(half):
        parts = []
        for k in range(2):
            t = (2 * (2 * half + k) + 2 - (me & 1)) & (NT - 1)
            parts.append(dot(hot_rows(wr[...], t), oht[:, strip_x]).reshape(ND, 2, YT, 128))
        others(lambda j: a_copy(j, j, half).wait())
        for k in range(2):
            part = parts[k]
            p = jnp.zeros((YT, 128), F32)
            ps, firsts = [], []
            for j in range(ND):
                ps.append(p)
                firsts.append(rx[j, half, k, 0] + part[j, 0])
                last_row = rx[j, half, k, 1] + part[j, 1]
                p = last_row + coef[j, 0:1, :] * firsts[j] + coef[j, 1:2, :] * p
            a = jnp.zeros((YT, 128), F32)
            for j in reversed(range(ND)):
                tx[j, half, k, 1] = coef[j, 7:8, :] * a
                a = coef[j, 2:3, :] * firsts[j] + coef[j, 3:4, :] * ps[j] + coef[j, 4:5, :] * a
                tx[j, half, k, 0] = coef[j, 5:6, :] * (ps[j] + coef[j, 6:7, :] * a)
        others(lambda j: b_copy(j, me, half).start())
        pq_o[me, half] = tx[me, half]

    def product(t, c):
        left = jnp.concatenate([kcat[...], hot_rows(p_v[...], t)], axis=1)
        top = pl.multiple_of(t * YT + PAD, YT)

        def pair(z, n):
            out = []
            for x in (2 * n, 2 * n + 1):
                at = top + (z * ZR + x * YR)
                out.append(h_o[z, rows(t), x * 128 : (x + 1) * 128]
                           + (f2[pl.ds(at, YT), :] - f2[pl.ds(at + 1, YT), :]))
            return jnp.concatenate(out, axis=1)

        for n in range(4):
            cols = slice(n * 256, n * 256 + 256)
            hi, lo = split(jnp.concatenate([pair(z, n) for z in range(CZ)], axis=0))
            res = dot(left, jnp.concatenate([hi, lo, hi, oht[:, cols]], axis=0))
            h_o[:, rows(t), cols] = res.reshape(CZ, YT, 256)
        return c

    give_back(0)
    lax.fori_loop(0, EARLY, product, 0)
    give_back(1)

    for b in range(NB // ND):
        leave_s[b] = jnp.sum(jnp.where(who8[0:1] == perm_s[me * (NB // ND) + b], flow, 0.0))

    lax.fori_loop(EARLY, NT, product, 0)
    others(lambda j: b_copy(j, j, 0).wait())
    others(lambda j: b_copy(j, j, 1).wait())


def fused(*args):
    dma = pltpu.SemaphoreType.DMA
    vm = lambda *s: pltpu.VMEM(s, F32)
    vb = lambda *s: pltpu.VMEM(s, BF16)
    any_ = pl.BlockSpec(memory_space=pl.ANY)
    smem = pl.BlockSpec(memory_space=pltpu.SMEM)
    vmem = pl.BlockSpec(memory_space=pltpu.VMEM)
    return pl.pallas_call(
        kernel,
        out_shape=(
            pltpu.VMEM((CZ, CY, CX), F32),
            pltpu.VMEM((ND, 2, 2, 2, YT, 128), F32),
            jax.ShapeDtypeStruct((NB // ND,), F32),
        ),
        in_specs=[any_, any_, smem, vmem, smem, smem, smem, vmem, smem, vmem, vmem, vmem],
        out_specs=(vmem, vmem, smem),
        scratch_shapes=[
            vm(CZ, NX + 1, YR, 128), vm(CZ, NX + 1, YR, 128), vm(CZ, NX + 1, YR, 128),
            pltpu.VMEM((CZ, CY, CX), jnp.int32), vm(GZ * NX, YT, 128), vb(256, 768), vb(2 * NB, CX),
            vm(CZ, NB), vm(CZ, NB), vm(CZ, NB), vm(CZ, NB), vm(CZ, NB), vm(CZ, NB), vm(CZ, 3 * NB),
            vm(16, NB), vm(ND, 16, NB), vm(2 * ND, NB),
            vm(2, 2, NX, CZ, 128), vm(2, 2, NX, CZ, 128),
            vm(ND, 2, 2, 2, YT, 128), vm(ND, 2, 2, 2, YT, 128), vm(ND, 2, 2, 2, YT, 128),
            vm(ND, 8, NB),
            dma((NT, NX)), dma((NT,)), dma((2,)), dma((2,)),
            dma((ND,)), dma((ND,)), dma((ND, 2)), dma((ND, 2)), dma((ND, 2)), dma((ND, 2)),
        ],
        compiler_params=pltpu.CompilerParams(
            collective_id=0, has_side_effects=True, vmem_limit_bytes=VMEM_LIMIT
        ),
    )(*args)


def finish_kernel(local, pq, g_s, out_h, ring, sem):
    def copy(i):
        slot = lax.rem(i, OS)
        return pltpu.make_async_copy(
            ring.at[slot], out_h.at[pl.ds(i * OZ, OZ)], sem.at[slot])

    def step(i, c):
        slot = lax.rem(i, OS)

        @pl.when(i >= OS)
        def _():
            copy(i - OS).wait()
        for u in range(OZ):
            z = i * OZ + u
            for y in range(0, CY, YT):
                rows = slice(y, y + YT)
                t = y // YT
                turn = (t + NT - 1) % NT // 2
                for x in range(NX):
                    cols = slice(x * 128, x * 128 + 128)
                    from_o = pq.at[2 * x + t % 2, turn // 2, turn % 2]
                    ring[slot, u, rows, cols] = local[z, rows, cols] + (
                        g_s[z, 0] * from_o[0] + g_s[z, CZ - 1] * from_o[1])
        copy(i).start()
        return c

    lax.fori_loop(0, CZ // OZ, step, 0)

    def drain(i, c):
        copy(i).wait()
        return c

    lax.fori_loop(CZ // OZ - OS, CZ // OZ, drain, 0)


def finish(local, pq, pivot):
    vmem = pl.BlockSpec(memory_space=pltpu.VMEM)
    return pl.pallas_call(
        finish_kernel,
        out_shape=jax.ShapeDtypeStruct((CZ, CY, CX), F32),
        in_specs=[vmem, vmem, pl.BlockSpec(memory_space=pltpu.SMEM)],
        out_specs=pl.BlockSpec(memory_space=pl.ANY),
        scratch_shapes=[pltpu.VMEM((OS, OZ, CY, CX), F32), pltpu.SemaphoreType.DMA((OS,))],
        compiler_params=pltpu.CompilerParams(vmem_limit_bytes=FINISH_LIMIT),
    )(local, pq, pivot)


def body(warmth, category, catalogue, pivot, linkage, position, holder, reach, entering, speed):
    row = lambda v: v.reshape(1, NB)
    local, pq, leaving = fused(
        warmth, category, catalogue, pivot, pivot, linkage, position, row(position), holder, row(reach),
        row(entering), row(speed),
    )
    return finish(local, pq, pivot), leaving


def solution(mesh):
    in_specs = (
        P("depth", "strip", None),
        P("depth", "strip", None),
        P(),
        P("depth", None),
        P("depth"),
        P("strip"),
        P("strip"),
        P("strip"),
        P("strip"),
        P("strip"),
    )
    out_specs = (P("depth", "strip", None), P(("strip", "depth")))
    return jax.shard_map(body, mesh=mesh, in_specs=in_specs, out_specs=out_specs, check_vma=False)
```

```python
import jax
import jax.numpy as jnp
from jax import lax
from jax.experimental import pallas as pl
from jax.experimental.pallas import tpu as pltpu
from jax.sharding import PartitionSpec as P

F32 = jnp.float32
BF16 = jnp.bfloat16
MESH = pl.DeviceIdType.MESH
HIGHEST = lax.Precision.HIGHEST

CZ, CY, CX = 32, 64, 1024
NB = 128
ND = 16
NS = 8
YT = 8
NT = CY // YT
HX = CX // 2
PAD = 8
NX = CX // 128
YR = CY + PAD
ZR = (NX + 1) * YR
GZ = 2
NG = CZ // GZ
PER = 16
EARLY = 3
VMEM_LIMIT = 52 * 1024 * 1024
FINISH_LIMIT = 16 * 1024 * 1024
OZ = 2
OS = 4


def dot(a, b, precision=None):
    return lax.dot_general(
        a, b, (((1,), (0,)), ((), ())), precision=precision, preferred_element_type=F32
    )


def split(v):
    hi = v.astype(BF16)
    lo = (v - hi.astype(F32)).astype(BF16)
    return hi, lo


def iota(shape, dim):
    return lax.broadcasted_iota(jnp.int32, shape, dim)


def kernel(
    t_h, cat_h, table_s, g_ref, g_s, link_s, pos_s, pos_ref, perm_s, reach_ref, inlet_ref, speed_ref,
    h_o, pq_o, leave_s,
    t_v, k_v, f_v, cat_v, fe_s, kcat, oht, rate_v, rock_v, p_v, d_v, q_v, u_v, w3,
    gs, ga, wr, hs, hr, fl, rx, tx, coef,
    in_t, in_c, h_send, h_recv, g_send, g_recv, a_send, a_recv, b_send, b_recv,
):
    me = lax.axis_index("depth")
    strip = lax.axis_index("strip")
    north = lax.rem(strip + NS - 1, NS)
    south = lax.rem(strip + 1, NS)
    first = me >> 1
    t2 = t_v.reshape(CZ * ZR, 128)
    k2 = k_v.reshape(CZ * ZR, 128)
    f2 = f_v.reshape(CZ * ZR, 128)

    def rows(t):
        return pl.ds(pl.multiple_of(t * YT, YT), YT)

    def prows(t):
        return pl.ds(pl.multiple_of(t * YT + PAD, YT), YT)

    def load_c(t):
        return pltpu.make_async_copy(cat_h.at[:, rows(t), :], cat_v.at[:, rows(t), :], in_c.at[t])

    def load_t(t, x):
        return pltpu.make_async_copy(
            t_h.at[:, rows(t), x * 128 : (x + 1) * 128], t_v.at[:, x, prows(t), :], in_t.at[t, x])

    def load(t):
        load_c(t).start()
        for x in range(NX):
            load_t(t, x).start()

    def ring(i):
        return lax.rem(first + i, NT)

    load(NT - 1)
    load(0)

    def load_rest(t, c):
        load(t)
        return c

    lax.fori_loop(1, NT - 1, load_rest, 0)

    barrier = pltpu.get_barrier_semaphore()
    pl.semaphore_signal(barrier, inc=1, device_id={"strip": north}, device_id_type=MESH)
    pl.semaphore_signal(barrier, inc=1, device_id={"strip": south}, device_id_type=MESH)

    def others(fn):
        def step(i, c):
            fn(lax.rem(me + i, ND))
            return c
        lax.fori_loop(1, ND, step, 0)

    others(lambda j: pl.semaphore_signal(
        barrier, inc=1, device_id={"depth": j}, device_id_type=MESH))

    table = [table_s[i] * 0.1 for i in range(8)]
    level_of = jnp.zeros((8, 128), F32)
    for i in range(8):
        level_of = jnp.where(iota((8, 128), 0) == i, table[i], level_of)

    def pick(cat):
        return jnp.take_along_axis(level_of, cat, axis=0, mode="promise_in_bounds")

    g = g_ref[...]
    spread = ((iota((256, CZ), 0) >> 3) == iota((256, CZ), 1)).astype(F32)
    spread_t = ((iota((CZ, 256), 1) >> 3) == iota((CZ, 256), 0)).astype(F32)
    wide = dot(dot(spread, g, HIGHEST), spread_t, HIGHEST)
    wide = jnp.where((iota((256, 256), 0) & 7) == (iota((256, 256), 1) & 7), wide, 0.0)
    whi, wlo = split(wide)
    kcat[:, 0:256] = whi
    kcat[:, 256:512] = whi
    kcat[:, 512:768] = wlo
    pos = pos_ref[...]
    ypos = pos >> 10
    xcol = jnp.transpose(jnp.broadcast_to(pos & (CX - 1), (NB, NB)))
    for q in range(NX):
        hot = (iota((NB, NB), 1) + q * NB == xcol).astype(F32).astype(BF16)
        oht[0:NB, q * NB : (q + 1) * NB] = hot
        oht[NB : 2 * NB, q * NB : (q + 1) * NB] = hot

    pl.semaphore_wait(barrier, ND - 1 + 2)

    def halo_copies():
        up = pltpu.make_async_remote_copy(
            src_ref=hs.at[0], dst_ref=hr.at[1], send_sem=h_send.at[0], recv_sem=h_recv.at[1],
            device_id={"strip": north}, device_id_type=MESH)
        down = pltpu.make_async_remote_copy(
            src_ref=hs.at[1], dst_ref=hr.at[0], send_sem=h_send.at[1], recv_sem=h_recv.at[0],
            device_id={"strip": south}, device_id_type=MESH)
        return up, down

    def lines(z, x, y):
        return pl.ds(z * ZR + x * YR + y, 8, stride=ZR)

    def landed(t):
        load_c(t).wait()
        for x in range(NX):
            load_t(t, x).wait()

    def arrive(t):
        landed(t)

        def planes(i, c):
            for u in range(4):
                z = i * 4 + u
                for x in range(NX):
                    k_v[z, x, prows(t), :] = pick(cat_v[z, rows(t), x * 128 : (x + 1) * 128])
            return c

        lax.fori_loop(0, CZ // 4, planes, 0)

    arrive(NT - 1)
    for x in range(NX):
        for z in range(0, CZ, 8):
            hs[1, 0, x, z : z + 8, :] = t2[lines(z, x, PAD + CY - 1), :]
            hs[1, 1, x, z : z + 8, :] = k2[lines(z, x, PAD + CY - 1), :]
    halo_copies()[1].start()
    arrive(0)
    for x in range(NX):
        for z in range(0, CZ, 8):
            hs[0, 0, x, z : z + 8, :] = t2[lines(z, x, PAD), :]
            hs[0, 1, x, z : z + 8, :] = k2[lines(z, x, PAD), :]
    halo_copies()[0].start()

    who8 = iota((8, NB), 1)
    west, east = who8 == 0, who8 == 127

    def at_of(t, i):
        base = pl.multiple_of(i * GZ * ZR + t * YT + PAD, YT)
        return [base + u * ZR + x * YR for u in range(GZ) for x in range(NX)]

    n = GZ * NX

    def right_of(t, i):
        at = at_of(t, i)
        fu = [f2[pl.ds(a, YT), :] for a in at]
        fd = [f2[pl.ds(a + 1, YT), :] for a in at]
        d = [h_o[i * GZ + m // NX, rows(t), m % NX * 128 : (m % NX + 1) * 128] for m in range(n)]
        return [d[m] + (fu[m] - fd[m]) for m in range(n)]

    def weigh(t, i, acc):
        right = right_of(t, i)
        for u in range(GZ):
            g0 = g_s[0, i * GZ + u]
            g1 = g_s[CZ - 1, i * GZ + u]
            for x in range(NX):
                acc[x] = acc[x] + g0 * right[u * NX + x]
                acc[NX + x] = acc[NX + x] + g1 * right[u * NX + x]
        return acc

    zeros16 = tuple(jnp.zeros((YT, 128), F32) for _ in range(2 * NX))

    def turn_of(t):
        return ((t + NT - 1) & (NT - 1)) >> 1

    def a_copy(o, source, half):
        return pltpu.make_async_remote_copy(
            src_ref=fl.at[o, half], dst_ref=rx.at[source, half], send_sem=a_send.at[o, half],
            recv_sem=a_recv.at[source, half], device_id={"depth": o}, device_id_type=MESH)

    def hand_out(t, acc):
        turn = turn_of(t)
        half, place = turn >> 1, turn & 1
        for x in range(NX):
            for r in range(2):
                fl[2 * x + (t & 1), half, place, r] = acc[r * NX + x]

        @pl.when(place == 1)
        def _():
            def give(i, c):
                o = 2 * ((i + (me >> 1)) & (NX - 1)) + (t & 1)

                @pl.when(o == me)
                def _():
                    rx[me, half] = fl[o, half]

                @pl.when(o != me)
                def _():
                    a_copy(o, me, half).start()
                return c

            lax.fori_loop(0, NX, give, 0)

    def weigh_tile(t):
        hand_out(t, lax.fori_loop(
            0, NG, lambda i, acc: tuple(weigh(t, i, list(acc))), zeros16))

    def faces(tile_at, count, loads):
        total = count * NG

        def step(i, c):
            where = []
            for lag in range(3):
                g = jnp.clip(i - lag, 0, total - 1)
                where.append((tile_at(g >> 4), g & (NG - 1)))
            (ta0, i0), (ta1, i1), (ta2, i2) = where
            if loads:
                @pl.when(jnp.logical_and(i0 == 0, i < total))
                def _():
                    landed(ta0)
            at = at_of(ta1, i1)
            at2 = at_of(ta2, i2)
            fe2 = [fe_s[m] for m in range(n)]
            rf = [pltpu.roll(v, 1, 1) for v in fe2]
            tc = [t2[pl.ds(a, YT), :] for a in at]
            kc = [k2[pl.ds(a, YT), :] for a in at]
            rt = [pltpu.roll(v, 127, 1) for v in tc]
            rk = [pltpu.roll(v, 127, 1) for v in kc]
            ta = [t2[pl.ds(a - 1, YT), :] for a in at]
            ka = [k2[pl.ds(a - 1, YT), :] for a in at]
            for m in range(n):
                f2[pl.ds(at[m], YT), :] = (kc[m] + ka[m]) * (ta[m] - tc[m])
            for m in range(n):
                x = m % NX
                told = t2[pl.ds(at2[m], YT), :]
                edge = k2[pl.ds(at2[m], YT), :] * told if x == 0 else rf[m - 1]
                h_o[i2 * GZ + m // NX, rows(ta2), x * 128 : (x + 1) * 128] = (
                    told + (fe2[m] - jnp.where(west, edge, rf[m])))
            inner = lambda m: (m + 1) % NX != 0
            te = [jnp.where(east, rt[m + 1] if inner(m) else 0.0, rt[m]) for m in range(n)]
            ke = [jnp.where(east, rk[m + 1] if inner(m) else 0.0, rk[m]) for m in range(n)]
            for m in range(n):
                fe_s[m] = (kc[m] + ke[m]) * (te[m] - tc[m])
            for m in range(n):
                z, x = i0 * GZ + m // NX, m % NX
                k_v[z, x, prows(ta0), :] = pick(cat_v[z, rows(ta0), x * 128 : (x + 1) * 128])

            done = jnp.logical_and(i2 == NG - 1, i >= 2)
            if loads:
                done = jnp.logical_and(done, ta2 >= 2)

            @pl.when(done)
            def _():
                weigh_tile((ta2 + NT - 1) & (NT - 1))
            return c

        lax.fori_loop(0, total + 2, step, 0)

    faces(lambda k: 1 + k, NT - 2, True)

    def g_copy(j, source):
        return pltpu.make_async_remote_copy(
            src_ref=gs, dst_ref=ga.at[source], send_sem=g_send.at[j], recv_sem=g_recv.at[source],
            device_id={"depth": j}, device_id_type=MESH)

    def halo_in():
        up, down = halo_copies()
        up.wait()
        down.wait()
        has_north = (strip > 0).astype(F32)
        has_south = (strip < NS - 1).astype(F32)
        for x in range(NX):
            for z in range(0, CZ, 8):
                t2[lines(z, x, PAD - 1), :] = hr[0, 0, x, z : z + 8, :] * has_north
                k2[lines(z, x, PAD - 1), :] = hr[0, 1, x, z : z + 8, :] * has_north
                tb = hr[1, 0, x, z : z + 8, :] * has_south
                kb = hr[1, 1, x, z : z + 8, :] * has_south
                tc = t2[lines(z, x, PAD + CY - 1), :]
                kc = k2[lines(z, x, PAD + CY - 1), :]
                f2[lines(z, x, PAD + CY), :] = (kb + kc) * (tc - tb)

    sub8 = iota((8, NB), 0)

    def fetch(b, acc):
        p = pos_s[b]
        col = ((p >> 7) & 7) * YR + (p >> 10) + PAD
        shift = (b - p) & 127
        mine = who8 == b
        for m in range(8):
            ref = t2 if m < 4 else k2
            z0 = (m % 4) * 8
            got = ref[pl.ds(col + z0 * ZR, 8), :]
            for u in range(1, 8):
                got = jnp.where(sub8 == u, ref[pl.ds(col + (z0 + u) * ZR - u, 8), :], got)
            acc[m] = jnp.where(mine, pltpu.roll(got, shift, 1), acc[m])
        return acc

    def wells():
        def some(i, acc):
            acc = list(acc)
            for u in range(PER):
                acc = fetch(i * PER + u, acc)
            return tuple(acc)

        acc = lax.fori_loop(0, NB // PER, some, tuple(jnp.zeros((8, NB), F32) for _ in range(8)))
        for zg in range(4):
            part = slice(zg * 8, zg * 8 + 8)
            cond = 10.0 * acc[4 + zg]
            rate = speed_ref[...] * cond / (1.0 + cond)
            level = iota((8, NB), 0) + (me * CZ + zg * 8)
            rate_v[part, :] = jnp.where(level < reach_ref[...], rate, 0.0)
            rock_v[part, :] = acc[zg]
        prod = jnp.ones((1, NB), F32)
        add_d = jnp.zeros((1, NB), F32)
        back = jnp.ones((1, NB), F32)
        add_r = jnp.zeros((1, NB), F32)
        for z in range(CZ):
            p_v[z : z + 1, :] = prod
            d_v[z : z + 1, :] = add_d
            r = rate_v[z : z + 1, :]
            prod = prod * (1.0 - r)
            add_d = (1.0 - r) * add_d + r * rock_v[z : z + 1, :]
            y = CZ - 1 - z
            q_v[y : y + 1, :] = back
            u_v[y : y + 1, :] = add_r
            r = rate_v[y : y + 1, :]
            back = back * (1.0 - r)
            add_r = (1.0 - r) * add_r + r * rock_v[y : y + 1, :]
        rate = rate_v[...]
        w3[:, 0:NB] = 2.0 * rate * (d_v[...] + u_v[...] - 2.0 * rock_v[...])
        w3[:, NB : 2 * NB] = 2.0 * rate * p_v[...]
        w3[:, 2 * NB : 3 * NB] = 2.0 * rate * q_v[...]
        w3[...] = dot(g_ref[...], w3[...], HIGHEST)
        gs[0:1, :] = prod
        gs[1:2, :] = add_d
        gs[2:3, :] = add_r
        for m in range(3):
            gs[8 + m : 9 + m, :] = w3[0:1, m * NB : (m + 1) * NB]
            gs[11 + m : 12 + m, :] = w3[CZ - 1 : CZ, m * NB : (m + 1) * NB]
        gs[14:16, :] = jnp.zeros((2, NB), F32)
        last = CZ - 1
        gs[3:4, :] = jnp.broadcast_to(g_ref[0:1, 0:1], (1, NB))
        gs[4:5, :] = jnp.broadcast_to(g_ref[0:1, last:CZ], (1, NB))
        gs[5:6, :] = jnp.broadcast_to(g_ref[last:CZ, 0:1], (1, NB))
        gs[6:7, :] = jnp.broadcast_to(g_ref[last:CZ, last:CZ], (1, NB))
        gs[7:8, :] = jnp.full((1, NB), link_s[0], F32)
        ga[me] = gs[...]
        others(lambda j: g_copy(j, me).start())

    wells()
    halo_in()

    faces(lambda k: (NT - 1 + k) & (NT - 1), 2, False)
    weigh_tile(0)

    others(lambda j: g_copy(j, j).wait())

    flow = inlet_ref[...]
    downs = []
    for j in range(ND):
        downs.append(flow)
        flow = ga[j, 0:1, :] * flow + ga[j, 1:2, :]
    mine = jnp.zeros((1, NB), F32)
    rising = jnp.zeros((1, NB), F32)
    for j in reversed(range(ND)):
        own_block = (me == j).astype(F32)
        mine = mine + downs[j] * own_block
        rising = rising + flow * own_block
        for m in range(2):
            at = 8 + 3 * m
            wr[2 * j + m : 2 * j + m + 1, :] = (
                ga[j, at : at + 1, :] + ga[j, at + 1 : at + 2, :] * downs[j]
                + ga[j, at + 2 : at + 3, :] * flow)
        flow = ga[j, 0:1, :] * flow + ga[j, 2:3, :]
    wmat = w3[:, 0:NB] + w3[:, NB : 2 * NB] * mine + w3[:, 2 * NB : 3 * NB] * rising
    p_v[...] = wmat

    one = jnp.ones((1, NB), F32)
    zero = jnp.zeros((1, NB), F32)
    cs = [zero]
    for j in range(1, ND):
        cs.append(ga[j, 7:8, :] * (CZ / (CZ + 1.0)) / jnp.sqrt(ga[j - 1, 6:7, :] * ga[j, 3:4, :]))
    cs.append(zero)
    q = zero
    for j in range(ND):
        vf = cs[j] * ga[j, 3:4, :]
        vl = cs[j] * ga[j, 5:6, :]
        wf = cs[j + 1] * ga[j, 4:5, :]
        wl = cs[j + 1] * ga[j, 6:7, :]
        den = one - vf * q
        inv = one / den
        coef[j, 0:1, :] = vl * q * inv
        coef[j, 1:2, :] = vl * inv
        coef[j, 2:3, :] = inv
        coef[j, 3:4, :] = vf * inv
        coef[j, 4:5, :] = wf * inv
        coef[j, 5:6, :] = cs[j]
        coef[j, 6:7, :] = q
        coef[j, 7:8, :] = cs[j + 1]
        q = wl + vl * q * wf * inv

    def hot_rows(w, t):
        here = ((iota((YT, NB), 0) + t * YT) == ypos).astype(F32)
        hi, lo = split((w[:, None, :] * here[None, :, :]).reshape(w.shape[0] * YT, NB))
        return jnp.concatenate([hi, lo], axis=1)

    strip_x = pl.ds(pl.multiple_of((me >> 1) * 128, 128), 128)

    def b_copy(j, source, half):
        return pltpu.make_async_remote_copy(
            src_ref=tx.at[j, half], dst_ref=pq_o.at[source, half], send_sem=b_send.at[j, half],
            recv_sem=b_recv.at[source, half], device_id={"depth": j}, device_id_type=MESH)

    def give_back(half):
        parts = []
        for k in range(2):
            t = (2 * (2 * half + k) + 2 - (me & 1)) & (NT - 1)
            parts.append(dot(hot_rows(wr[...], t), oht[:, strip_x]).reshape(ND, 2, YT, 128))
        others(lambda j: a_copy(j, j, half).wait())
        for k in range(2):
            part = parts[k]
            p = jnp.zeros((YT, 128), F32)
            ps, firsts = [], []
            for j in range(ND):
                ps.append(p)
                firsts.append(rx[j, half, k, 0] + part[j, 0])
                last_row = rx[j, half, k, 1] + part[j, 1]
                p = last_row + coef[j, 0:1, :] * firsts[j] + coef[j, 1:2, :] * p
            a = jnp.zeros((YT, 128), F32)
            for j in reversed(range(ND)):
                tx[j, half, k, 1] = coef[j, 7:8, :] * a
                a = coef[j, 2:3, :] * firsts[j] + coef[j, 3:4, :] * ps[j] + coef[j, 4:5, :] * a
                tx[j, half, k, 0] = coef[j, 5:6, :] * (ps[j] + coef[j, 6:7, :] * a)
        others(lambda j: b_copy(j, me, half).start())
        pq_o[me, half] = tx[me, half]

    def product(t, c):
        left = jnp.concatenate([kcat[...], hot_rows(p_v[...], t)], axis=1)
        top = pl.multiple_of(t * YT + PAD, YT)

        def pair(z, n):
            out = []
            for x in (2 * n, 2 * n + 1):
                at = top + (z * ZR + x * YR)
                out.append(h_o[z, rows(t), x * 128 : (x + 1) * 128]
                           + (f2[pl.ds(at, YT), :] - f2[pl.ds(at + 1, YT), :]))
            return jnp.concatenate(out, axis=1)

        for n in range(4):
            cols = slice(n * 256, n * 256 + 256)
            hi, lo = split(jnp.concatenate([pair(z, n) for z in range(CZ)], axis=0))
            res = dot(left, jnp.concatenate([hi, lo, hi, oht[:, cols]], axis=0))
            h_o[:, rows(t), cols] = res.reshape(CZ, YT, 256)
        return c

    give_back(0)
    lax.fori_loop(0, EARLY, product, 0)
    give_back(1)

    for b in range(NB // ND):
        leave_s[b] = jnp.sum(jnp.where(who8[0:1] == perm_s[me * (NB // ND) + b], flow, 0.0))

    lax.fori_loop(EARLY, NT, product, 0)
    others(lambda j: b_copy(j, j, 0).wait())
    others(lambda j: b_copy(j, j, 1).wait())


def fused(*args):
    dma = pltpu.SemaphoreType.DMA
    vm = lambda *s: pltpu.VMEM(s, F32)
    vb = lambda *s: pltpu.VMEM(s, BF16)
    any_ = pl.BlockSpec(memory_space=pl.ANY)
    smem = pl.BlockSpec(memory_space=pltpu.SMEM)
    vmem = pl.BlockSpec(memory_space=pltpu.VMEM)
    return pl.pallas_call(
        kernel,
        out_shape=(
            pltpu.VMEM((CZ, CY, CX), F32),
            pltpu.VMEM((ND, 2, 2, 2, YT, 128), F32),
            jax.ShapeDtypeStruct((NB // ND,), F32),
        ),
        in_specs=[any_, any_, smem, vmem, smem, smem, smem, vmem, smem, vmem, vmem, vmem],
        out_specs=(vmem, vmem, smem),
        scratch_shapes=[
            vm(CZ, NX + 1, YR, 128), vm(CZ, NX + 1, YR, 128), vm(CZ, NX + 1, YR, 128),
            pltpu.VMEM((CZ, CY, CX), jnp.int32), vm(GZ * NX, YT, 128), vb(256, 768), vb(2 * NB, CX),
            vm(CZ, NB), vm(CZ, NB), vm(CZ, NB), vm(CZ, NB), vm(CZ, NB), vm(CZ, NB), vm(CZ, 3 * NB),
            vm(16, NB), vm(ND, 16, NB), vm(2 * ND, NB),
            vm(2, 2, NX, CZ, 128), vm(2, 2, NX, CZ, 128),
            vm(ND, 2, 2, 2, YT, 128), vm(ND, 2, 2, 2, YT, 128), vm(ND, 2, 2, 2, YT, 128),
            vm(ND, 8, NB),
            dma((NT, NX)), dma((NT,)), dma((2,)), dma((2,)),
            dma((ND,)), dma((ND,)), dma((ND, 2)), dma((ND, 2)), dma((ND, 2)), dma((ND, 2)),
        ],
        compiler_params=pltpu.CompilerParams(
            collective_id=0, has_side_effects=True, vmem_limit_bytes=VMEM_LIMIT
        ),
    )(*args)


def finish_kernel(local, pq, g_s, out_h, ring, sem):
    def copy(i):
        slot = lax.rem(i, OS)
        return pltpu.make_async_copy(
            ring.at[slot], out_h.at[pl.ds(i * OZ, OZ)], sem.at[slot])

    def step(i, c):
        slot = lax.rem(i, OS)

        @pl.when(i >= OS)
        def _():
            copy(i - OS).wait()
        for u in range(OZ):
            z = i * OZ + u
            for y in range(0, CY, YT):
                rows = slice(y, y + YT)
                t = y // YT
                turn = (t + NT - 1) % NT // 2
                for x in range(NX):
                    cols = slice(x * 128, x * 128 + 128)
                    from_o = pq.at[2 * x + t % 2, turn // 2, turn % 2]
                    ring[slot, u, rows, cols] = local[z, rows, cols] + (
                        g_s[z, 0] * from_o[0] + g_s[z, CZ - 1] * from_o[1])
        copy(i).start()
        return c

    lax.fori_loop(0, CZ // OZ, step, 0)

    def drain(i, c):
        copy(i).wait()
        return c

    lax.fori_loop(CZ // OZ - OS, CZ // OZ, drain, 0)


def finish(local, pq, pivot):
    vmem = pl.BlockSpec(memory_space=pltpu.VMEM)
    return pl.pallas_call(
        finish_kernel,
        out_shape=jax.ShapeDtypeStruct((CZ, CY, CX), F32),
        in_specs=[vmem, vmem, pl.BlockSpec(memory_space=pltpu.SMEM)],
        out_specs=pl.BlockSpec(memory_space=pl.ANY),
        scratch_shapes=[pltpu.VMEM((OS, OZ, CY, CX), F32), pltpu.SemaphoreType.DMA((OS,))],
        compiler_params=pltpu.CompilerParams(vmem_limit_bytes=FINISH_LIMIT),
    )(local, pq, pivot)


def body(warmth, category, catalogue, pivot, linkage, position, holder, reach, entering, speed):
    row = lambda v: v.reshape(1, NB)
    local, pq, leaving = fused(
        warmth, category, catalogue, pivot, pivot, linkage, position, row(position), holder, row(reach),
        row(entering), row(speed),
    )
    return finish(local, pq, pivot), leaving


def solution(mesh):
    in_specs = (
        P("depth", "strip", None),
        P("depth", "strip", None),
        P(),
        P("depth", None),
        P("depth"),
        P("strip"),
        P("strip"),
        P("strip"),
        P("strip"),
        P("strip"),
    )
    out_specs = (P("depth", "strip", None), P(("strip", "depth")))
    return jax.shard_map(body, mesh=mesh, in_specs=in_specs, out_specs=out_specs, check_vma=False)
```

```python
import jax
import jax.numpy as jnp
from jax import lax
from jax.experimental import pallas as pl
from jax.experimental.pallas import tpu as pltpu
from jax.sharding import PartitionSpec as P

F32 = jnp.float32
BF16 = jnp.bfloat16
MESH = pl.DeviceIdType.MESH
HIGHEST = lax.Precision.HIGHEST

CZ, CY, CX = 32, 64, 1024
NB = 128
ND = 16
NS = 8
YT = 8
NT = CY // YT
HX = CX // 2
PAD = 8
NX = CX // 128
YR = CY + PAD
ZR = (NX + 1) * YR
GZ = 2
NG = CZ // GZ
PER = 16
EARLY = 1
VMEM_LIMIT = 52 * 1024 * 1024
FINISH_LIMIT = 16 * 1024 * 1024
OZ = 2
OS = 4


def dot(a, b, precision=None):
    return lax.dot_general(
        a, b, (((1,), (0,)), ((), ())), precision=precision, preferred_element_type=F32
    )


def split(v):
    hi = v.astype(BF16)
    lo = (v - hi.astype(F32)).astype(BF16)
    return hi, lo


def iota(shape, dim):
    return lax.broadcasted_iota(jnp.int32, shape, dim)


def kernel(
    t_h, cat_h, table_s, g_ref, g_s, link_s, pos_s, pos_ref, perm_s, reach_ref, inlet_ref, speed_ref,
    h_o, pq_o, leave_s,
    t_v, k_v, f_v, cat_v, fe_s, kcat, oht, rate_v, rock_v, p_v, d_v, q_v, u_v, w3,
    gs, ga, wr, hs, hr, fl, rx, tx, coef,
    in_t, in_c, h_send, h_recv, g_send, g_recv, a_send, a_recv, b_send, b_recv,
):
    me = lax.axis_index("depth")
    strip = lax.axis_index("strip")
    north = lax.rem(strip + NS - 1, NS)
    south = lax.rem(strip + 1, NS)
    first = me >> 1
    t2 = t_v.reshape(CZ * ZR, 128)
    k2 = k_v.reshape(CZ * ZR, 128)
    f2 = f_v.reshape(CZ * ZR, 128)

    def rows(t):
        return pl.ds(pl.multiple_of(t * YT, YT), YT)

    def prows(t):
        return pl.ds(pl.multiple_of(t * YT + PAD, YT), YT)

    def load_c(t):
        return pltpu.make_async_copy(cat_h.at[:, rows(t), :], cat_v.at[:, rows(t), :], in_c.at[t])

    def load_t(t, x):
        return pltpu.make_async_copy(
            t_h.at[:, rows(t), x * 128 : (x + 1) * 128], t_v.at[:, x, prows(t), :], in_t.at[t, x])

    def load(t):
        load_c(t).start()
        for x in range(NX):
            load_t(t, x).start()

    def ring(i):
        return lax.rem(first + i, NT)

    load(NT - 1)
    load(0)

    def load_rest(t, c):
        load(t)
        return c

    lax.fori_loop(1, NT - 1, load_rest, 0)

    barrier = pltpu.get_barrier_semaphore()
    pl.semaphore_signal(barrier, inc=1, device_id={"strip": north}, device_id_type=MESH)
    pl.semaphore_signal(barrier, inc=1, device_id={"strip": south}, device_id_type=MESH)

    def others(fn):
        def step(i, c):
            fn(lax.rem(me + i, ND))
            return c
        lax.fori_loop(1, ND, step, 0)

    others(lambda j: pl.semaphore_signal(
        barrier, inc=1, device_id={"depth": j}, device_id_type=MESH))

    table = [table_s[i] * 0.1 for i in range(8)]
    level_of = jnp.zeros((8, 128), F32)
    for i in range(8):
        level_of = jnp.where(iota((8, 128), 0) == i, table[i], level_of)

    def pick(cat):
        return jnp.take_along_axis(level_of, cat, axis=0, mode="promise_in_bounds")

    g = g_ref[...]
    spread = ((iota((256, CZ), 0) >> 3) == iota((256, CZ), 1)).astype(F32)
    spread_t = ((iota((CZ, 256), 1) >> 3) == iota((CZ, 256), 0)).astype(F32)
    wide = dot(dot(spread, g, HIGHEST), spread_t, HIGHEST)
    wide = jnp.where((iota((256, 256), 0) & 7) == (iota((256, 256), 1) & 7), wide, 0.0)
    whi, wlo = split(wide)
    kcat[:, 0:256] = whi
    kcat[:, 256:512] = whi
    kcat[:, 512:768] = wlo
    pos = pos_ref[...]
    ypos = pos >> 10
    xcol = jnp.transpose(jnp.broadcast_to(pos & (CX - 1), (NB, NB)))
    for q in range(NX):
        hot = (iota((NB, NB), 1) + q * NB == xcol).astype(F32).astype(BF16)
        oht[0:NB, q * NB : (q + 1) * NB] = hot
        oht[NB : 2 * NB, q * NB : (q + 1) * NB] = hot

    pl.semaphore_wait(barrier, ND - 1 + 2)

    def halo_copies():
        up = pltpu.make_async_remote_copy(
            src_ref=hs.at[0], dst_ref=hr.at[1], send_sem=h_send.at[0], recv_sem=h_recv.at[1],
            device_id={"strip": north}, device_id_type=MESH)
        down = pltpu.make_async_remote_copy(
            src_ref=hs.at[1], dst_ref=hr.at[0], send_sem=h_send.at[1], recv_sem=h_recv.at[0],
            device_id={"strip": south}, device_id_type=MESH)
        return up, down

    def lines(z, x, y):
        return pl.ds(z * ZR + x * YR + y, 8, stride=ZR)

    def landed(t):
        load_c(t).wait()
        for x in range(NX):
            load_t(t, x).wait()

    def arrive(t):
        landed(t)

        def planes(i, c):
            for u in range(4):
                z = i * 4 + u
                for x in range(NX):
                    k_v[z, x, prows(t), :] = pick(cat_v[z, rows(t), x * 128 : (x + 1) * 128])
            return c

        lax.fori_loop(0, CZ // 4, planes, 0)

    arrive(NT - 1)
    for x in range(NX):
        for z in range(0, CZ, 8):
            hs[1, 0, x, z : z + 8, :] = t2[lines(z, x, PAD + CY - 1), :]
            hs[1, 1, x, z : z + 8, :] = k2[lines(z, x, PAD + CY - 1), :]
    halo_copies()[1].start()
    arrive(0)
    for x in range(NX):
        for z in range(0, CZ, 8):
            hs[0, 0, x, z : z + 8, :] = t2[lines(z, x, PAD), :]
            hs[0, 1, x, z : z + 8, :] = k2[lines(z, x, PAD), :]
    halo_copies()[0].start()

    who8 = iota((8, NB), 1)
    west, east = who8 == 0, who8 == 127

    def at_of(t, i):
        base = pl.multiple_of(i * GZ * ZR + t * YT + PAD, YT)
        return [base + u * ZR + x * YR for u in range(GZ) for x in range(NX)]

    n = GZ * NX

    def right_of(t, i):
        at = at_of(t, i)
        fu = [f2[pl.ds(a, YT), :] for a in at]
        fd = [f2[pl.ds(a + 1, YT), :] for a in at]
        d = [h_o[i * GZ + m // NX, rows(t), m % NX * 128 : (m % NX + 1) * 128] for m in range(n)]
        return [d[m] + (fu[m] - fd[m]) for m in range(n)]

    def weigh(t, i, acc):
        right = right_of(t, i)
        for u in range(GZ):
            g0 = g_s[0, i * GZ + u]
            g1 = g_s[CZ - 1, i * GZ + u]
            for x in range(NX):
                acc[x] = acc[x] + g0 * right[u * NX + x]
                acc[NX + x] = acc[NX + x] + g1 * right[u * NX + x]
        return acc

    zeros16 = tuple(jnp.zeros((YT, 128), F32) for _ in range(2 * NX))

    def turn_of(t):
        return ((t + NT - 1) & (NT - 1)) >> 1

    def a_copy(o, source, half):
        return pltpu.make_async_remote_copy(
            src_ref=fl.at[o, half], dst_ref=rx.at[source, half], send_sem=a_send.at[o, half],
            recv_sem=a_recv.at[source, half], device_id={"depth": o}, device_id_type=MESH)

    def hand_out(t, acc):
        turn = turn_of(t)
        half, place = turn >> 1, turn & 1
        for x in range(NX):
            for r in range(2):
                fl[2 * x + (t & 1), half, place, r] = acc[r * NX + x]

        @pl.when(place == 1)
        def _():
            def give(i, c):
                o = 2 * ((i + (me >> 1)) & (NX - 1)) + (t & 1)

                @pl.when(o == me)
                def _():
                    rx[me, half] = fl[o, half]

                @pl.when(o != me)
                def _():
                    a_copy(o, me, half).start()
                return c

            lax.fori_loop(0, NX, give, 0)

    def weigh_tile(t):
        hand_out(t, lax.fori_loop(
            0, NG, lambda i, acc: tuple(weigh(t, i, list(acc))), zeros16))

    def faces(tile_at, count, loads):
        total = count * NG

        def step(i, c):
            where = []
            for lag in range(3):
                g = jnp.clip(i - lag, 0, total - 1)
                where.append((tile_at(g >> 4), g & (NG - 1)))
            (ta0, i0), (ta1, i1), (ta2, i2) = where
            if loads:
                @pl.when(jnp.logical_and(i0 == 0, i < total))
                def _():
                    landed(ta0)
            at = at_of(ta1, i1)
            at2 = at_of(ta2, i2)
            fe2 = [fe_s[m] for m in range(n)]
            rf = [pltpu.roll(v, 1, 1) for v in fe2]
            tc = [t2[pl.ds(a, YT), :] for a in at]
            kc = [k2[pl.ds(a, YT), :] for a in at]
            rt = [pltpu.roll(v, 127, 1) for v in tc]
            rk = [pltpu.roll(v, 127, 1) for v in kc]
            ta = [t2[pl.ds(a - 1, YT), :] for a in at]
            ka = [k2[pl.ds(a - 1, YT), :] for a in at]
            for m in range(n):
                f2[pl.ds(at[m], YT), :] = (kc[m] + ka[m]) * (ta[m] - tc[m])
            for m in range(n):
                x = m % NX
                told = t2[pl.ds(at2[m], YT), :]
                edge = k2[pl.ds(at2[m], YT), :] * told if x == 0 else rf[m - 1]
                h_o[i2 * GZ + m // NX, rows(ta2), x * 128 : (x + 1) * 128] = (
                    told + (fe2[m] - jnp.where(west, edge, rf[m])))
            inner = lambda m: (m + 1) % NX != 0
            te = [jnp.where(east, rt[m + 1] if inner(m) else 0.0, rt[m]) for m in range(n)]
            ke = [jnp.where(east, rk[m + 1] if inner(m) else 0.0, rk[m]) for m in range(n)]
            for m in range(n):
                fe_s[m] = (kc[m] + ke[m]) * (te[m] - tc[m])
            for m in range(n):
                z, x = i0 * GZ + m // NX, m % NX
                k_v[z, x, prows(ta0), :] = pick(cat_v[z, rows(ta0), x * 128 : (x + 1) * 128])

            done = jnp.logical_and(i2 == NG - 1, i >= 2)
            if loads:
                done = jnp.logical_and(done, ta2 >= 2)

            @pl.when(done)
            def _():
                weigh_tile((ta2 + NT - 1) & (NT - 1))
            return c

        lax.fori_loop(0, total + 2, step, 0)

    faces(lambda k: 1 + k, NT - 2, True)

    def g_copy(j, source):
        return pltpu.make_async_remote_copy(
            src_ref=gs, dst_ref=ga.at[source], send_sem=g_send.at[j], recv_sem=g_recv.at[source],
            device_id={"depth": j}, device_id_type=MESH)

    def halo_in():
        up, down = halo_copies()
        up.wait()
        down.wait()
        has_north = (strip > 0).astype(F32)
        has_south = (strip < NS - 1).astype(F32)
        for x in range(NX):
            for z in range(0, CZ, 8):
                t2[lines(z, x, PAD - 1), :] = hr[0, 0, x, z : z + 8, :] * has_north
                k2[lines(z, x, PAD - 1), :] = hr[0, 1, x, z : z + 8, :] * has_north
                tb = hr[1, 0, x, z : z + 8, :] * has_south
                kb = hr[1, 1, x, z : z + 8, :] * has_south
                tc = t2[lines(z, x, PAD + CY - 1), :]
                kc = k2[lines(z, x, PAD + CY - 1), :]
                f2[lines(z, x, PAD + CY), :] = (kb + kc) * (tc - tb)

    sub8 = iota((8, NB), 0)

    def fetch(b, acc):
        p = pos_s[b]
        col = ((p >> 7) & 7) * YR + (p >> 10) + PAD
        shift = (b - p) & 127
        mine = who8 == b
        for m in range(8):
            ref = t2 if m < 4 else k2
            z0 = (m % 4) * 8
            got = ref[pl.ds(col + z0 * ZR, 8), :]
            for u in range(1, 8):
                got = jnp.where(sub8 == u, ref[pl.ds(col + (z0 + u) * ZR - u, 8), :], got)
            acc[m] = jnp.where(mine, pltpu.roll(got, shift, 1), acc[m])
        return acc

    def wells():
        def some(i, acc):
            acc = list(acc)
            for u in range(PER):
                acc = fetch(i * PER + u, acc)
            return tuple(acc)

        acc = lax.fori_loop(0, NB // PER, some, tuple(jnp.zeros((8, NB), F32) for _ in range(8)))
        for zg in range(4):
            part = slice(zg * 8, zg * 8 + 8)
            cond = 10.0 * acc[4 + zg]
            rate = speed_ref[...] * cond / (1.0 + cond)
            level = iota((8, NB), 0) + (me * CZ + zg * 8)
            rate_v[part, :] = jnp.where(level < reach_ref[...], rate, 0.0)
            rock_v[part, :] = acc[zg]
        prod = jnp.ones((1, NB), F32)
        add_d = jnp.zeros((1, NB), F32)
        back = jnp.ones((1, NB), F32)
        add_r = jnp.zeros((1, NB), F32)
        for z in range(CZ):
            p_v[z : z + 1, :] = prod
            d_v[z : z + 1, :] = add_d
            r = rate_v[z : z + 1, :]
            prod = prod * (1.0 - r)
            add_d = (1.0 - r) * add_d + r * rock_v[z : z + 1, :]
            y = CZ - 1 - z
            q_v[y : y + 1, :] = back
            u_v[y : y + 1, :] = add_r
            r = rate_v[y : y + 1, :]
            back = back * (1.0 - r)
            add_r = (1.0 - r) * add_r + r * rock_v[y : y + 1, :]
        rate = rate_v[...]
        w3[:, 0:NB] = 2.0 * rate * (d_v[...] + u_v[...] - 2.0 * rock_v[...])
        w3[:, NB : 2 * NB] = 2.0 * rate * p_v[...]
        w3[:, 2 * NB : 3 * NB] = 2.0 * rate * q_v[...]
        w3[...] = dot(g_ref[...], w3[...], HIGHEST)
        gs[0:1, :] = prod
        gs[1:2, :] = add_d
        gs[2:3, :] = add_r
        for m in range(3):
            gs[8 + m : 9 + m, :] = w3[0:1, m * NB : (m + 1) * NB]
            gs[11 + m : 12 + m, :] = w3[CZ - 1 : CZ, m * NB : (m + 1) * NB]
        gs[14:16, :] = jnp.zeros((2, NB), F32)
        last = CZ - 1
        gs[3:4, :] = jnp.broadcast_to(g_ref[0:1, 0:1], (1, NB))
        gs[4:5, :] = jnp.broadcast_to(g_ref[0:1, last:CZ], (1, NB))
        gs[5:6, :] = jnp.broadcast_to(g_ref[last:CZ, 0:1], (1, NB))
        gs[6:7, :] = jnp.broadcast_to(g_ref[last:CZ, last:CZ], (1, NB))
        gs[7:8, :] = jnp.full((1, NB), link_s[0], F32)
        ga[me] = gs[...]
        others(lambda j: g_copy(j, me).start())

    wells()
    halo_in()

    faces(lambda k: (NT - 1 + k) & (NT - 1), 2, False)
    weigh_tile(0)

    others(lambda j: g_copy(j, j).wait())

    flow = inlet_ref[...]
    downs = []
    for j in range(ND):
        downs.append(flow)
        flow = ga[j, 0:1, :] * flow + ga[j, 1:2, :]
    mine = jnp.zeros((1, NB), F32)
    rising = jnp.zeros((1, NB), F32)
    for j in reversed(range(ND)):
        own_block = (me == j).astype(F32)
        mine = mine + downs[j] * own_block
        rising = rising + flow * own_block
        for m in range(2):
            at = 8 + 3 * m
            wr[2 * j + m : 2 * j + m + 1, :] = (
                ga[j, at : at + 1, :] + ga[j, at + 1 : at + 2, :] * downs[j]
                + ga[j, at + 2 : at + 3, :] * flow)
        flow = ga[j, 0:1, :] * flow + ga[j, 2:3, :]
    wmat = w3[:, 0:NB] + w3[:, NB : 2 * NB] * mine + w3[:, 2 * NB : 3 * NB] * rising
    p_v[...] = wmat

    one = jnp.ones((1, NB), F32)
    zero = jnp.zeros((1, NB), F32)
    cs = [zero]
    for j in range(1, ND):
        cs.append(ga[j, 7:8, :] * (CZ / (CZ + 1.0)) / jnp.sqrt(ga[j - 1, 6:7, :] * ga[j, 3:4, :]))
    cs.append(zero)
    q = zero
    for j in range(ND):
        vf = cs[j] * ga[j, 3:4, :]
        vl = cs[j] * ga[j, 5:6, :]
        wf = cs[j + 1] * ga[j, 4:5, :]
        wl = cs[j + 1] * ga[j, 6:7, :]
        den = one - vf * q
        inv = one / den
        coef[j, 0:1, :] = vl * q * inv
        coef[j, 1:2, :] = vl * inv
        coef[j, 2:3, :] = inv
        coef[j, 3:4, :] = vf * inv
        coef[j, 4:5, :] = wf * inv
        coef[j, 5:6, :] = cs[j]
        coef[j, 6:7, :] = q
        coef[j, 7:8, :] = cs[j + 1]
        q = wl + vl * q * wf * inv

    def hot_rows(w, t):
        here = ((iota((YT, NB), 0) + t * YT) == ypos).astype(F32)
        hi, lo = split((w[:, None, :] * here[None, :, :]).reshape(w.shape[0] * YT, NB))
        return jnp.concatenate([hi, lo], axis=1)

    strip_x = pl.ds(pl.multiple_of((me >> 1) * 128, 128), 128)

    def b_copy(j, source, half):
        return pltpu.make_async_remote_copy(
            src_ref=tx.at[j, half], dst_ref=pq_o.at[source, half], send_sem=b_send.at[j, half],
            recv_sem=b_recv.at[source, half], device_id={"depth": j}, device_id_type=MESH)

    def give_back(half):
        parts = []
        for k in range(2):
            t = (2 * (2 * half + k) + 2 - (me & 1)) & (NT - 1)
            parts.append(dot(hot_rows(wr[...], t), oht[:, strip_x]).reshape(ND, 2, YT, 128))
        others(lambda j: a_copy(j, j, half).wait())
        for k in range(2):
            part = parts[k]
            p = jnp.zeros((YT, 128), F32)
            ps, firsts = [], []
            for j in range(ND):
                ps.append(p)
                firsts.append(rx[j, half, k, 0] + part[j, 0])
                last_row = rx[j, half, k, 1] + part[j, 1]
                p = last_row + coef[j, 0:1, :] * firsts[j] + coef[j, 1:2, :] * p
            a = jnp.zeros((YT, 128), F32)
            for j in reversed(range(ND)):
                tx[j, half, k, 1] = coef[j, 7:8, :] * a
                a = coef[j, 2:3, :] * firsts[j] + coef[j, 3:4, :] * ps[j] + coef[j, 4:5, :] * a
                tx[j, half, k, 0] = coef[j, 5:6, :] * (ps[j] + coef[j, 6:7, :] * a)
        others(lambda j: b_copy(j, me, half).start())
        pq_o[me, half] = tx[me, half]

    def product(t, c):
        left = jnp.concatenate([kcat[...], hot_rows(p_v[...], t)], axis=1)
        top = pl.multiple_of(t * YT + PAD, YT)

        def pair(z, n):
            out = []
            for x in (2 * n, 2 * n + 1):
                at = top + (z * ZR + x * YR)
                out.append(h_o[z, rows(t), x * 128 : (x + 1) * 128]
                           + (f2[pl.ds(at, YT), :] - f2[pl.ds(at + 1, YT), :]))
            return jnp.concatenate(out, axis=1)

        for n in range(4):
            cols = slice(n * 256, n * 256 + 256)
            hi, lo = split(jnp.concatenate([pair(z, n) for z in range(CZ)], axis=0))
            res = dot(left, jnp.concatenate([hi, lo, hi, oht[:, cols]], axis=0))
            h_o[:, rows(t), cols] = res.reshape(CZ, YT, 256)
        return c

    give_back(0)
    lax.fori_loop(0, EARLY, product, 0)
    give_back(1)

    for b in range(NB // ND):
        leave_s[b] = jnp.sum(jnp.where(who8[0:1] == perm_s[me * (NB // ND) + b], flow, 0.0))

    lax.fori_loop(EARLY, NT, product, 0)
    others(lambda j: b_copy(j, j, 0).wait())
    others(lambda j: b_copy(j, j, 1).wait())


def fused(*args):
    dma = pltpu.SemaphoreType.DMA
    vm = lambda *s: pltpu.VMEM(s, F32)
    vb = lambda *s: pltpu.VMEM(s, BF16)
    any_ = pl.BlockSpec(memory_space=pl.ANY)
    smem = pl.BlockSpec(memory_space=pltpu.SMEM)
    vmem = pl.BlockSpec(memory_space=pltpu.VMEM)
    return pl.pallas_call(
        kernel,
        out_shape=(
            pltpu.VMEM((CZ, CY, CX), F32),
            pltpu.VMEM((ND, 2, 2, 2, YT, 128), F32),
            jax.ShapeDtypeStruct((NB // ND,), F32),
        ),
        in_specs=[any_, any_, smem, vmem, smem, smem, smem, vmem, smem, vmem, vmem, vmem],
        out_specs=(vmem, vmem, smem),
        scratch_shapes=[
            vm(CZ, NX + 1, YR, 128), vm(CZ, NX + 1, YR, 128), vm(CZ, NX + 1, YR, 128),
            pltpu.VMEM((CZ, CY, CX), jnp.int32), vm(GZ * NX, YT, 128), vb(256, 768), vb(2 * NB, CX),
            vm(CZ, NB), vm(CZ, NB), vm(CZ, NB), vm(CZ, NB), vm(CZ, NB), vm(CZ, NB), vm(CZ, 3 * NB),
            vm(16, NB), vm(ND, 16, NB), vm(2 * ND, NB),
            vm(2, 2, NX, CZ, 128), vm(2, 2, NX, CZ, 128),
            vm(ND, 2, 2, 2, YT, 128), vm(ND, 2, 2, 2, YT, 128), vm(ND, 2, 2, 2, YT, 128),
            vm(ND, 8, NB),
            dma((NT, NX)), dma((NT,)), dma((2,)), dma((2,)),
            dma((ND,)), dma((ND,)), dma((ND, 2)), dma((ND, 2)), dma((ND, 2)), dma((ND, 2)),
        ],
        compiler_params=pltpu.CompilerParams(
            collective_id=0, has_side_effects=True, vmem_limit_bytes=VMEM_LIMIT
        ),
    )(*args)


def finish_kernel(local, pq, g_s, out_h, ring, sem):
    def copy(i):
        slot = lax.rem(i, OS)
        return pltpu.make_async_copy(
            ring.at[slot], out_h.at[pl.ds(i * OZ, OZ)], sem.at[slot])

    def step(i, c):
        slot = lax.rem(i, OS)

        @pl.when(i >= OS)
        def _():
            copy(i - OS).wait()
        for u in range(OZ):
            z = i * OZ + u
            for y in range(0, CY, YT):
                rows = slice(y, y + YT)
                t = y // YT
                turn = (t + NT - 1) % NT // 2
                for x in range(NX):
                    cols = slice(x * 128, x * 128 + 128)
                    from_o = pq.at[2 * x + t % 2, turn // 2, turn % 2]
                    ring[slot, u, rows, cols] = local[z, rows, cols] + (
                        g_s[z, 0] * from_o[0] + g_s[z, CZ - 1] * from_o[1])
        copy(i).start()
        return c

    lax.fori_loop(0, CZ // OZ, step, 0)

    def drain(i, c):
        copy(i).wait()
        return c

    lax.fori_loop(CZ // OZ - OS, CZ // OZ, drain, 0)


def finish(local, pq, pivot):
    vmem = pl.BlockSpec(memory_space=pltpu.VMEM)
    return pl.pallas_call(
        finish_kernel,
        out_shape=jax.ShapeDtypeStruct((CZ, CY, CX), F32),
        in_specs=[vmem, vmem, pl.BlockSpec(memory_space=pltpu.SMEM)],
        out_specs=pl.BlockSpec(memory_space=pl.ANY),
        scratch_shapes=[pltpu.VMEM((OS, OZ, CY, CX), F32), pltpu.SemaphoreType.DMA((OS,))],
        compiler_params=pltpu.CompilerParams(vmem_limit_bytes=FINISH_LIMIT),
    )(local, pq, pivot)


def body(warmth, category, catalogue, pivot, linkage, position, holder, reach, entering, speed):
    row = lambda v: v.reshape(1, NB)
    local, pq, leaving = fused(
        warmth, category, catalogue, pivot, pivot, linkage, position, row(position), holder, row(reach),
        row(entering), row(speed),
    )
    return finish(local, pq, pivot), leaving


def solution(mesh):
    in_specs = (
        P("depth", "strip", None),
        P("depth", "strip", None),
        P(),
        P("depth", None),
        P("depth"),
        P("strip"),
        P("strip"),
        P("strip"),
        P("strip"),
        P("strip"),
    )
    out_specs = (P("depth", "strip", None), P(("strip", "depth")))
    return jax.shard_map(body, mesh=mesh, in_specs=in_specs, out_specs=out_specs, check_vma=False)
```
